32 devices in a mesh: gx: 4 (over y, x), gz: 8 (over z, core).
Axes of the slice: x: 2, y: 2, z: 4, core: 2. Of those that a mesh axis runs over, the one named last changes fastest.
Arguments:
- constituent_mass: float32 [5, 4, 64, 512], P(None, None, 'gz', 'gx'), may hold values from 0.05 to 0.5
- flow_speeds: float32 [3, 4, 64, 512], P(None, None, 'gz', 'gx'), may hold values from -3 to 4
- thermal_pair: float32 [2, 4, 64, 512], P(None, None, 'gz', 'gx'), may hold values from 0.005 to 0.05
- blowing_indicator: int32 [64, 512], P('gz', 'gx'), may hold values 0 or 1
Outputs:
- tendency: float32 [10, 4, 64, 512], P(None, None, 'gz', 'gx')
- coefficients: float32 [3, 4, 512], P(None, None, 'gx')
The draws below stay inside these ranges and needn't reach their ends.
All inputs are finite; a program needn't handle non-finite values. No bound on the sum of `blowing_indicator` on one device may be relied on, other than what follows from the above.
Results may differ from the reference program's by a relative error of at most 0.000029.
Values sent between devices are 32-bit elements; how exact they have to be, the bound alone decides.
No kernel may reach another device: no remote copies, remote signals or barrier semaphores. Data moves between devices by JAX's collectives and lax.ppermute only.
A program may use at most 64 MiB of HBM per device.

```python
import math
import jax
import jax.numpy as jnp
from jax import lax

CXD = 128
WALL_DEPTH_COUNT = 4
NSP = 5
DOWNWIND_COUNT = 512
CROSSWISE_COUNT = 64
N_GX = 4


def draw_flow_speeds(key, part):
    noise_key, column_key = jax.random.split(key)
    span_place = jnp.arange(CROSSWISE_COUNT, dtype=jnp.float32) / CROSSWISE_COUNT
    column_scale = 3.2 ** jax.random.uniform(column_key, (DOWNWIND_COUNT,), jnp.float32)
    span_rise = 3.2 ** span_place
    noise = jnp.clip(jax.random.normal(noise_key, (3, WALL_DEPTH_COUNT, CROSSWISE_COUNT, DOWNWIND_COUNT), jnp.float32), -4.0, 4.0)
    amplitude = 0.05 * span_rise[:, None] * column_scale[None, :]
    profile = (jnp.arange(WALL_DEPTH_COUNT, dtype=jnp.float32) + 1.0) / WALL_DEPTH_COUNT
    mean_flow = jnp.stack([profile, 0.0 * profile, 0.0 * profile])[:, :, None, None]
    return (mean_flow + amplitude * noise).astype(jnp.float32)


def plant(values, stream_key, low, high):
    extent = values.shape
    spot = [jax.random.randint(jax.random.fold_in(stream_key, axis), (), 0, extent[axis]) for axis in range(len(extent))]
    values = values.at[tuple(spot)].set(low)
    longest = extent.index(max(extent))
    spot[longest] = (spot[longest] + 1) % extent[longest]
    return values.at[tuple(spot)].set(high)


def level_of(own_key, shape, cuts, smallest, largest):
    loudness = 1.0
    for position, blocks in cuts:
        heights = jax.random.uniform(jax.random.fold_in(jax.random.fold_in(own_key, 6), position), (blocks,), jnp.float32, smallest / len(cuts), largest / len(cuts))
        loudness = loudness * jnp.repeat(jnp.exp(heights), shape[position] // blocks).reshape((-1,) + (1,) * (len(shape) - 1 - position))
    return loudness


def setup_inputs(seed: int = 0) -> dict:
    keys = jax.random.split(jax.random.key(seed), 5)
    return {
        "constituent_mass": jnp.clip(jnp.exp(math.log(0.5) - 2.3025851 * jax.random.uniform(keys[0], (NSP, WALL_DEPTH_COUNT, CROSSWISE_COUNT, DOWNWIND_COUNT), jnp.float32) ** level_of(keys[0], (NSP, WALL_DEPTH_COUNT, CROSSWISE_COUNT, DOWNWIND_COUNT), ((2, 8), (3, 4)), -0.2, 0.2)), 0.05, 0.5),
        "flow_speeds": draw_flow_speeds(jax.random.fold_in(keys[4], 71), 0),
        "thermal_pair": jnp.clip(jnp.exp(math.log(0.05) - 2.3025851 * jax.random.uniform(keys[2], (2, WALL_DEPTH_COUNT, CROSSWISE_COUNT, DOWNWIND_COUNT), jnp.float32) ** level_of(keys[2], (2, WALL_DEPTH_COUNT, CROSSWISE_COUNT, DOWNWIND_COUNT), ((2, 8), (3, 4)), -0.2, 0.2)), 0.005, 0.05),
        "blowing_indicator": plant((jax.random.randint(keys[3], (CROSSWISE_COUNT, DOWNWIND_COUNT), 0, 3) < 1).astype(jnp.int32), jax.random.fold_in(keys[3], 1), 0, 1),
    }


SPECIFIC_HEAT = 2.5
SPECIFIC_HEAT_P = 3.5
HEAT_RATIO = 1.4
STEP_STREAM = 1.0
STEP_NORMAL = 0.5
STEP_SPAN = 1.0
FILTER_SQUARE = 0.5 ** (2.0 / 3.0)
TEST_SQUARE = 2.0 ** (2.0 / 3.0)
FORMATION = (0.0, 0.0, 0.1, 0.5, 0.25)
BLOWING = 0.3
RELAX_TIME = 0.5
SMOOTH_FLOOR = 0.01
RATIO_EPSILON = 1e-06

def shrink(values, margin):
    if margin == 0:
        return values
    return values[..., margin:-margin, margin:-margin]

def shrink_span(values, margin):
    if margin == 0:
        return values
    return values[..., margin:-margin, :]

def window(values, offset, length, dimension):
    return lax.slice_in_dim(values, offset, offset + length, axis=values.ndim + dimension)

def cell_state(flow_variables):
    partial_value = flow_variables[:NSP]
    density = lax.optimization_barrier(jnp.sum(partial_value, axis=0))
    motion = flow_variables[NSP:NSP + 3]
    thermal = flow_variables[NSP + 3]
    vibration = flow_variables[NSP + 4]
    return (partial_value, density, motion, thermal, vibration)

def conserved_fluxes(flow_variables, component):
    partial_value, density, motion, thermal, vibration = cell_state(flow_variables)
    pressure = density * thermal
    formation_energy = sum((FORMATION[s] * partial_value[s] for s in range(NSP)))
    energy = density * (SPECIFIC_HEAT * thermal + vibration + 0.5 * lax.optimization_barrier(jnp.sum(motion * motion, axis=0))) + formation_energy
    momentum = density[None] * motion
    conserved = jnp.concatenate([partial_value, momentum, energy[None], (density * vibration)[None]], axis=0)
    speed_along = motion[component]
    direction = jnp.array([1.0 if k == component else 0.0 for k in range(3)], dtype=flow_variables.dtype)
    direction = direction.reshape((3,) + (1,) * (flow_variables.ndim - 1))
    fluxes = jnp.concatenate([partial_value * speed_along, momentum * speed_along + direction * pressure, ((energy + pressure) * speed_along)[None], (density * vibration * speed_along)[None]], axis=0)
    signal = jnp.abs(speed_along) + jnp.sqrt(HEAT_RATIO * thermal)
    return (conserved, fluxes, signal)

def upwind_blend(stencil):
    guesses = ((2.0 * stencil[0] - 7.0 * stencil[1] + 11.0 * stencil[2]) / 6.0, (-stencil[1] + 5.0 * stencil[2] + 2.0 * stencil[3]) / 6.0, (2.0 * stencil[2] + 5.0 * stencil[3] - stencil[4]) / 6.0)
    roughness = (13.0 / 12.0 * (stencil[0] - 2.0 * stencil[1] + stencil[2]) ** 2 + 0.25 * (stencil[0] - 4.0 * stencil[1] + 3.0 * stencil[2]) ** 2, 13.0 / 12.0 * (stencil[1] - 2.0 * stencil[2] + stencil[3]) ** 2 + 0.25 * (stencil[1] - stencil[3]) ** 2, 13.0 / 12.0 * (stencil[2] - 2.0 * stencil[3] + stencil[4]) ** 2 + 0.25 * (3.0 * stencil[2] - 4.0 * stencil[3] + stencil[4]) ** 2)
    weights = [linear_weight / (SMOOTH_FLOOR + smooth) ** 2 for linear_weight, smooth in zip((0.1, 0.6, 0.3), roughness)]
    return (weights[0] * guesses[0] + weights[1] * guesses[1] + weights[2] * guesses[2]) / (weights[0] + weights[1] + weights[2])

def upwind_faces(flow_variables, component, dimension):
    conserved, fluxes, signal = conserved_fluxes(flow_variables, component)
    face_count = flow_variables.shape[dimension] - 5
    face_signal = jnp.maximum(window(signal, 2, face_count, dimension), window(signal, 3, face_count, dimension))
    plus_side = [0.5 * (window(fluxes, o, face_count, dimension) + face_signal * window(conserved, o, face_count, dimension)) for o in range(5)]
    minus_side = [0.5 * (window(fluxes, o, face_count, dimension) - face_signal * window(conserved, o, face_count, dimension)) for o in range(1, 6)]
    return upwind_blend(plus_side) + upwind_blend(minus_side[::-1])

def normal_slope(values):
    bottom_slope = (values[..., 1:2, :, :] - values[..., 0:1, :, :]) / STEP_NORMAL
    middle = (values[..., 2:, :, :] - values[..., :-2, :, :]) / (2.0 * STEP_NORMAL)
    top_slope = (values[..., -1:, :, :] - values[..., -2:-1, :, :]) / STEP_NORMAL
    return jnp.concatenate([bottom_slope, middle, top_slope], axis=-3)

def gradient(values):
    stream_slope = (values[..., 1:-1, 2:] - values[..., 1:-1, :-2]) / (2.0 * STEP_STREAM)
    span_slope = (values[..., 2:, 1:-1] - values[..., :-2, 1:-1]) / (2.0 * STEP_SPAN)
    normal_part = normal_slope(values[..., 1:-1, 1:-1])
    return jnp.stack([stream_slope, normal_part, span_slope])

def strain_parts(gradients):
    strain = 0.5 * (gradients + jnp.swapaxes(gradients, 0, 1))
    third_trace = (strain[0, 0] + strain[1, 1] + strain[2, 2]) / 3.0
    identity = jnp.eye(3, dtype=gradients.dtype).reshape((3, 3) + (1,) * (gradients.ndim - 2))
    deviator = strain - identity * third_trace
    magnitude = jnp.sqrt(2.0 * lax.optimization_barrier(jnp.sum(deviator * deviator, axis=(0, 1))) + 1e-06)
    return (deviator, magnitude)

def test_filter(values):
    stream_pass = 0.25 * values[..., :-2] + 0.5 * values[..., 1:-1] + 0.25 * values[..., 2:]
    return 0.25 * stream_pass[..., :-2, :] + 0.5 * stream_pass[..., 1:-1, :] + 0.25 * stream_pass[..., 2:, :]

def germano_sums(padded_block, margin):
    partial_value, density, motion, thermal, vibration = cell_state(padded_block)
    fraction = partial_value / density
    deviator, magnitude = strain_parts(gradient(motion))
    density_in = shrink(density, 1)
    motion_in = shrink(motion, 1)
    thermal_in = shrink(thermal, 1)
    eddy_scale = FILTER_SQUARE * density_in * magnitude
    thermal_grad = gradient(thermal)
    fraction_grad = gradient(fraction)
    momentum_in = density_in * motion_in
    hat_density = test_filter(density_in)
    hat_momentum = test_filter(momentum_in)
    hat_product = test_filter(momentum_in[:, None] * motion_in[None])
    hat_stress = test_filter(eddy_scale * deviator)
    hat_thermal = test_filter(density_in * thermal_in)
    hat_thermal_flux = test_filter(momentum_in * thermal_in)
    hat_thermal_grad = test_filter(eddy_scale * thermal_grad)
    hat_partial = test_filter(shrink(partial_value, 1))
    hat_partial_flux = test_filter(momentum_in[:, None] * shrink(fraction, 1)[None])
    hat_partial_grad = test_filter(eddy_scale * fraction_grad)
    favre_motion = hat_momentum / hat_density
    favre_thermal = hat_thermal / hat_density
    favre_fraction = hat_partial / hat_density
    test_deviator, test_magnitude = strain_parts(gradient(favre_motion))
    test_density = shrink(hat_density, 1)
    test_eddy = TEST_SQUARE * test_density * test_magnitude
    outer_momentum = shrink(hat_momentum, 1)
    leonard = shrink(hat_product, 1) - outer_momentum[:, None] * outer_momentum[None] / test_density
    modelled_terms = 2.0 * (shrink(hat_stress, 1) - test_eddy * test_deviator)
    leonard_thermal = shrink(hat_thermal_flux, 1) - outer_momentum * shrink(hat_thermal, 1) / test_density
    modelled_thermal = shrink(hat_thermal_grad, 1) - test_eddy * gradient(favre_thermal)
    leonard_partial = shrink(hat_partial_flux, 1) - outer_momentum[:, None] * shrink(hat_partial, 1)[None] / test_density
    modelled_partial = shrink(hat_partial_grad, 1) - test_eddy * gradient(favre_fraction)
    contract = [lax.optimization_barrier(jnp.sum(leonard * modelled_terms, axis=(0, 1))), lax.optimization_barrier(jnp.sum(modelled_terms * modelled_terms, axis=(0, 1))), lax.optimization_barrier(jnp.sum(leonard_thermal * modelled_thermal, axis=0)), lax.optimization_barrier(jnp.sum(modelled_thermal * modelled_thermal, axis=0)), lax.optimization_barrier(jnp.sum(leonard_partial * modelled_partial, axis=(0, 1))), lax.optimization_barrier(jnp.sum(modelled_partial * modelled_partial, axis=(0, 1)))]
    span_rim = margin - 3
    totals = jnp.stack([lax.optimization_barrier(jnp.sum(shrink_span(contracted, span_rim), axis=-2)) for contracted in contract])
    grid_rim = margin - 2
    grid_fields = (shrink(motion_in, grid_rim), shrink(deviator, grid_rim), shrink(eddy_scale, grid_rim), shrink(thermal_grad, grid_rim), shrink(gradient(vibration), grid_rim), shrink(fraction_grad, grid_rim))
    return (totals, grid_fields)

def dynamic_ratio(totals, span_count):
    averages = totals / span_count
    return averages[0::2] / (averages[1::2] + RATIO_EPSILON)

def subgrid_flux(grid_fields, coefficient):
    motion, deviator, eddy_scale, thermal_grad, vibration_grad, fraction_grad = grid_fields
    viscous = coefficient[0][:, None, :] * eddy_scale
    conduct = coefficient[1][:, None, :] * eddy_scale
    diffuse = coefficient[2][:, None, :] * eddy_scale
    stress = -2.0 * viscous * deviator
    heat_flux = -SPECIFIC_HEAT_P * conduct * thermal_grad
    vibration_flux = -conduct * vibration_grad
    species_flux = -diffuse * fraction_grad
    stress_work = lax.optimization_barrier(jnp.sum(motion[:, None] * stress, axis=0))
    formation_energy = sum((FORMATION[s] * species_flux[:, s] for s in range(NSP)))
    energy_flux = stress_work + heat_flux + vibration_flux + formation_energy
    return jnp.concatenate([jnp.swapaxes(species_flux, 0, 1), stress, energy_flux[None], vibration_flux[None]], axis=0)

def normal_faces(flow_variables, subgrid, wall_mask):
    conserved, fluxes, signal = conserved_fluxes(flow_variables, 1)
    face_signal = jnp.maximum(signal[:-1], signal[1:])
    inside = 0.5 * (fluxes[:, :-1] + fluxes[:, 1:]) - 0.5 * face_signal * (conserved[:, 1:] - conserved[:, :-1]) + 0.5 * (subgrid[:, :-1] + subgrid[:, 1:])
    top_flux = fluxes[:, -1:] + subgrid[:, -1:]
    partial_value, density, motion, thermal, vibration = cell_state(flow_variables[:, 0])
    fraction = partial_value / density
    inflow = BLOWING * wall_mask.astype(density.dtype)
    lift_speed = inflow / density
    nothing = jnp.zeros_like(inflow)
    enthalpy = SPECIFIC_HEAT_P * thermal + vibration + 0.5 * lift_speed * lift_speed + sum((FORMATION[s] * fraction[s] for s in range(NSP)))
    wall_flux = jnp.concatenate([inflow * fraction, jnp.stack([nothing, inflow * lift_speed + density * thermal, nothing, inflow * enthalpy, inflow * vibration])], axis=0)
    return jnp.concatenate([wall_flux[:, None], inside, top_flux], axis=1)

def tendency_of(padded_block, grid_fields, coefficient, wall_mask):
    subgrid = subgrid_flux(grid_fields, coefficient)
    stream_sub = subgrid[:, 0, :, 1:-1, :]
    span_sub = subgrid[:, 2, :, :, 1:-1]
    normal_sub = subgrid[:, 1, :, 1:-1, 1:-1]
    stream_faces = upwind_faces(padded_block[..., 3:-3, :], 0, -1) + 0.5 * (stream_sub[..., :-1] + stream_sub[..., 1:])
    span_faces = upwind_faces(padded_block[..., 3:-3], 2, -2) + 0.5 * (span_sub[..., :-1, :] + span_sub[..., 1:, :])
    interior = shrink(padded_block, 3)
    normal_flux = normal_faces(interior, normal_sub, wall_mask)
    change = -(stream_faces[..., 1:] - stream_faces[..., :-1]) / STEP_STREAM - (span_faces[..., 1:, :] - span_faces[..., :-1, :]) / STEP_SPAN - (normal_flux[:, 1:] - normal_flux[:, :-1]) / STEP_NORMAL
    partial_value, density, motion, thermal, vibration = cell_state(interior)
    relaxation = density * (thermal - vibration) / RELAX_TIME
    return change + jnp.concatenate([jnp.zeros_like(change[:-1]), relaxation[None]], axis=0)

def reference(constituent_mass, flow_speeds, thermal_pair, blowing_indicator):
    flow_variables = jnp.concatenate([constituent_mass, flow_speeds, thermal_pair], axis=0)
    padded = jnp.pad(flow_variables, ((0, 0), (0, 0), (3, 3), (0, 0)), mode='wrap')
    padded = jnp.pad(padded, ((0, 0), (0, 0), (0, 0), (3, 3)), mode='edge')
    offsets = jnp.arange(N_GX, dtype=jnp.int32) * CXD

    def block_totals(offset):
        column_block = lax.dynamic_slice_in_dim(padded, offset, CXD + 6, axis=3)
        return germano_sums(column_block, 3)[0]
    totals = lax.map(block_totals, offsets)
    totals = jnp.moveaxis(totals, 0, 2).reshape(6, WALL_DEPTH_COUNT, DOWNWIND_COUNT)
    coefficients = dynamic_ratio(totals, CROSSWISE_COUNT)
    extended = jnp.pad(coefficients, ((0, 0), (0, 0), (1, 1)), mode='edge')

    def block_tendency(offset):
        column_block = lax.dynamic_slice_in_dim(padded, offset, CXD + 6, axis=3)
        grid_fields = germano_sums(column_block, 3)[1]
        columns = lax.dynamic_slice_in_dim(extended, offset, CXD + 2, axis=2)
        wall_mask = lax.dynamic_slice_in_dim(blowing_indicator, offset, CXD, axis=1)
        return tendency_of(column_block, grid_fields, columns, wall_mask)
    tendency = lax.map(block_tendency, offsets)
    tendency = jnp.moveaxis(tendency, 0, 3).reshape(NSP + 5, WALL_DEPTH_COUNT, CROSSWISE_COUNT, DOWNWIND_COUNT)
    return (tendency, coefficients)
```

```python
import jax
import jax.numpy as jnp
from jax import lax
from jax.experimental import pallas as pl
from jax.experimental.pallas import tpu as pltpu
from jax.sharding import PartitionSpec as P


NSP = 5
NF = 10
ROWS = 4
TILE = 8
LANES = 128
HALO = 3
GROUPS = NF * ROWS
PAIRS = NF // 2
MAIN_ROWS = PAIRS * HALO * TILE
MESSAGE_ROWS = MAIN_ROWS + 2 * TILE

HEAT_RATIO = 1.4
FILTER_SQUARE = 0.5 ** (2.0 / 3.0)
TEST_SQUARE = 2.0 ** (2.0 / 3.0)
FORMATION = (0.0, 0.0, 0.1, 0.5, 0.25)
BLOWING = 0.3
SMOOTH_FLOOR = 0.01
RATIO_EPSILON = 1e-06

VMEM = pl.BlockSpec(memory_space=pltpu.VMEM)
F32 = jnp.float32


def lanes():
    return lax.broadcasted_iota(jnp.int32, (TILE, LANES), 1)


def sublanes():
    return lax.broadcasted_iota(jnp.int32, (TILE, LANES), 0)


def shift_x(tile, step):
    if isinstance(step, int):
        step = step % LANES
        if step == 0:
            return tile
    return pltpu.roll(tile, step, 1)


def shift_s(tile, step):
    return pltpu.roll(tile, step % TILE, 0)


def is_even():
    return (sublanes() & 1) == 0


def level_edges():
    level = sublanes() >> 1
    return level == 0, level == 3


def tile_of(ref, index):
    return ref[pl.ds(index * TILE, TILE), :]


def pack_kernel(mass_ref, speed_ref, heat_ref, own_ref, left_ref, right_ref, up_ref, down_ref):
    lane = lanes()
    even = is_even()
    to_left = jnp.zeros((TILE, LANES), F32)
    to_right = jnp.zeros((TILE, LANES), F32)
    tiles = {}
    for field in range(NF):
        if field < NSP:
            ref, base = mass_ref, field
        elif field < NSP + 3:
            ref, base = speed_ref, field - NSP
        else:
            ref, base = heat_ref, field - NSP - 3
        for zz in range(ROWS):
            group = field * ROWS + zz
            tile = ref[pl.ds(base * 32 + zz, TILE, stride=4), :]
            tiles[field, zz] = tile
            own_ref[pl.ds(group * TILE, TILE), :] = tile
            reached = lane >= 3 * group
            to_left = jnp.where(reached, shift_x(tile, 3 * group), to_left)
            to_right = jnp.where(reached, shift_x(tile, 3 * group + 3), to_right)
        if field % 2:
            pair = field // 2
            for k in range(HALO):
                slot = pl.ds((pair * HALO + k) * TILE, TILE)
                up_ref[slot, :] = jnp.where(
                    even, shift_s(tiles[field - 1, k + 1], -1), tiles[field, k + 1]
                )
                down_ref[slot, :] = jnp.where(
                    even, tiles[field, k], shift_s(tiles[field - 1, k], 1)
                )
    left_ref[...] = to_left
    right_ref[...] = to_right


def edge_kernel(
    position_ref, got_left_ref, got_right_ref, to_left_ref, to_right_ref, up_in, down_in,
    up_ref, down_ref, edge_ref
):
    up_ref[pl.ds(0, MAIN_ROWS), :] = up_in[...]
    down_ref[pl.ds(0, MAIN_ROWS), :] = down_in[...]
    lane = lanes()
    third = lane - 3 * ((lane * 171) >> 9)
    own_left = to_left_ref[...]
    own_right = to_right_ref[...]
    clamp_left = jnp.where(
        third == 0, own_left,
        jnp.where(third == 1, shift_x(own_left, 1), shift_x(own_left, 2)),
    )
    clamp_right = jnp.where(
        third == 2, own_right,
        jnp.where(third == 1, shift_x(own_right, -1), shift_x(own_right, -2)),
    )
    left = jnp.where(position_ref[0] == 1, clamp_left, got_left_ref[...])
    right = jnp.where(position_ref[1] == 1, clamp_right, got_right_ref[...])
    for ref, start in ((up_ref, MAIN_ROWS), (down_ref, MAIN_ROWS), (edge_ref, 0)):
        ref[pl.ds(start, TILE), :] = left
        ref[pl.ds(start + TILE, TILE), :] = right


def row_tile(own_ref, below_ref, above_ref, field, zz):
    if 0 <= zz < ROWS:
        return tile_of(own_ref, field * ROWS + zz)
    pair, second = divmod(field, 2)
    if zz < 0:
        k = zz + ROWS
        halo = tile_of(below_ref, pair * HALO + k - 1)
        if second:
            halo = shift_s(halo, -1)
        return jnp.where(is_even(), halo, shift_s(tile_of(own_ref, field * ROWS + k), 1))
    k = zz - ROWS
    halo = tile_of(above_ref, pair * HALO + k)
    if second:
        halo = shift_s(halo, 1)
    return jnp.where(is_even(), shift_s(tile_of(own_ref, field * ROWS + k), -1), halo)


def halo_packs(edge_ref, below_ref, above_ref):
    even = is_even()
    packs = []
    for side in range(2):
        own = tile_of(edge_ref, side)
        low = below_ref[pl.ds(MAIN_ROWS + side * TILE, TILE), :]
        high = above_ref[pl.ds(MAIN_ROWS + side * TILE, TILE), :]
        packs.append(
            (
                jnp.where(even, shift_s(low, -1), shift_s(own, 1)),
                own,
                jnp.where(even, shift_s(own, -1), shift_s(high, 1)),
            )
        )
    return packs


def spread(left_pack, right_pack, group):
    return jnp.where(
        lanes() < 64,
        shift_x(right_pack, (LANES - 3 * group)),
        shift_x(left_pack, LANES - HALO - 3 * group),
    )


def state_of(fields):
    mass, motion = fields[:NSP], fields[NSP : NSP + 3]
    thermal, vibration = fields[NSP + 3], fields[NSP + 4]
    density = (mass[0] + mass[1]) + (mass[2] + mass[3]) + mass[4]
    formed = FORMATION[2] * mass[2] + FORMATION[3] * mass[3] + FORMATION[4] * mass[4]
    motion_square = motion[0] * motion[0] + motion[1] * motion[1] + motion[2] * motion[2]
    energy = density * (2.5 * thermal + vibration + 0.5 * motion_square) + formed
    conserved = (
        list(mass) + [density * speed for speed in motion] + [energy, density * vibration]
    )
    return density, density * thermal, jnp.sqrt(HEAT_RATIO * thermal), conserved


def flux_of(conserved, pressure, speed, component):
    flux = [value * speed for value in conserved]
    flux[NSP + component] = flux[NSP + component] + pressure
    flux[NSP + 3] = flux[NSP + 3] + pressure * speed
    return flux


def correction(d0, d1, d2, d3):
    floor = 4.0 * SMOOTH_FLOOR * 12.0 / 13.0
    share = 3.0 / 13.0
    e0, e1, e2 = d1 - d0, d2 - d1, d3 - d2
    g0, g1, g2 = e0 + (d1 + d1), d1 + d2, e2 - (d2 + d2)
    b0 = (e0 * e0 + floor) + share * (g0 * g0)
    b1 = (e1 * e1 + floor) + share * (g1 * g1)
    b2 = (e2 * e2 + floor) + share * (g2 * g2)
    p0, p1, p2 = b1 * b2, b0 * b2, b0 * b1
    w0 = p0 * p0
    w1 = 6.0 * (p1 * p1)
    w2 = 3.0 * (p2 * p2)
    r0 = 5.0 * d1 - (d0 + d0)
    r1 = d1 + (d2 + d2)
    r2 = 4.0 * d2 - d3
    return (w0 * r0 + w1 * r1 + w2 * r2) / (w0 + w1 + w2)


def face_flux(here, slopes, jumps, signal):
    waves = [signal * jump for jump in jumps]
    plus = [slopes[k] + waves[k] for k in range(4)]
    minus = [waves[k] - slopes[k] for k in range(1, 5)]
    gain = correction(*plus)
    loss = correction(minus[3], minus[2], minus[1], minus[0])
    return here + 0.5 * (slopes[2] - waves[2]) + (gain + loss) * (1.0 / 12.0)


def stream_kernel(own_ref, edge_ref, blow_ref, out_ref, first_ref, blow_rows):
    lane = lanes()
    bottom, top = level_edges()
    for level in range(4):
        blow_rows[pl.ds(level * TILE, TILE), :] = blow_ref[...].astype(F32)
    left_pack = tile_of(edge_ref, 0)
    right_pack = tile_of(edge_ref, 1)

    fields = []
    for field in range(NF):
        gathered = jnp.zeros((TILE, LANES), F32)
        for zz in range(ROWS):
            group = field * ROWS + zz
            halo = shift_x(left_pack, LANES - 3 - 3 * group)
            tile = jnp.where(lane >= LANES - HALO, halo, tile_of(own_ref, group))
            gathered = jnp.where(lane >= 8 * zz, shift_x(tile, 8 * zz + 3), gathered)
        fields.append(gathered)
    density, pressure, sound, conserved = state_of(fields)
    speed = fields[NSP]
    flux = flux_of(conserved, pressure, speed, 0)
    signal = jnp.abs(speed) + sound
    signal = jnp.maximum(signal, shift_x(signal, -1))
    for field in range(NF):
        slope = shift_x(flux[field], -1) - flux[field]
        jump = shift_x(conserved[field], -1) - conserved[field]
        slopes = [shift_x(slope, -k) for k in range(-2, 3)]
        jumps = [shift_x(jump, -k) for k in range(-2, 3)]
        first_ref[pl.ds(field * TILE, TILE), :] = face_flux(
            flux[field], slopes, jumps, signal
        )

    low = lane < HALO
    high = lane >= LANES - HALO

    def row(zz, carry):
        fields, halos = [], []
        for field in range(NF):
            group = field * ROWS + zz
            start = pl.multiple_of(group * TILE, TILE)
            fields.append(own_ref[pl.ds(start, TILE), :])
            halos.append(
                jnp.where(
                    lane < 64,
                    pltpu.roll(right_pack, (LANES - 3 * group) & (LANES - 1), 1),
                    pltpu.roll(left_pack, LANES - HALO - 3 * group, 1),
                )
            )
        density, pressure, sound, conserved = state_of(fields)
        halo_density, halo_pressure, halo_sound, halo_conserved = state_of(
            [jnp.where(low | high, h, f) for h, f in zip(halos, fields)]
        )
        speed, halo_speed = fields[NSP], jnp.where(low | high, halos[NSP], fields[NSP])
        flux = flux_of(conserved, pressure, speed, 0)
        halo_flux = flux_of(halo_conserved, halo_pressure, halo_speed, 0)
        signal = jnp.abs(speed) + sound
        halo_signal = jnp.abs(halo_speed) + halo_sound
        signal = jnp.maximum(signal, shift_x(jnp.where(lane == 0, halo_signal, signal), -1))

        normal_speed = fields[NSP + 1]
        normal_flux = flux_of(conserved, pressure, normal_speed, 1)
        normal_signal = jnp.abs(normal_speed) + sound
        normal_signal = 0.5 * jnp.maximum(normal_signal, shift_s(normal_signal, -2))
        blown = BLOWING * blow_rows[pl.ds(zz, TILE, stride=4), :]
        lift = blown / density
        enthalpy = 3.5 * fields[NSP + 3] + fields[NSP + 4] + 0.5 * lift * lift
        wall = [lift * fields[s] for s in range(NSP)]
        formed = FORMATION[2] * wall[2] + FORMATION[3] * wall[3] + FORMATION[4] * wall[4]
        zero = jnp.zeros((TILE, LANES), F32)
        wall = wall + [
            zero, blown * lift + pressure, zero, blown * enthalpy + formed, blown * fields[NSP + 4]
        ]

        for field in range(NF):
            def differences(value, halo):
                left, right = jnp.where(high, halo, value), jnp.where(low, halo, value)
                near = shift_x(left, -1) - left
                far = shift_x(right, -1) - right
                here = jnp.where(low, near, far)
                return [
                    shift_x(jnp.where(lane >= LANES - 2, near, here), 2),
                    shift_x(jnp.where(lane >= LANES - 1, near, here), 1),
                    here,
                    shift_x(jnp.where(lane < 1, far, here), -1),
                    shift_x(jnp.where(lane < 2, far, here), -2),
                ]

            slopes = differences(flux[field], halo_flux[field])
            jumps = differences(conserved[field], halo_conserved[field])
            face = face_flux(flux[field], slopes, jumps, signal)
            first = pltpu.roll(
                first_ref[pl.ds(field * TILE, TILE), :], LANES - 2 - 8 * zz, 1
            )
            change = jnp.where(lane == 0, first, shift_x(face, 1)) - face

            value, above = conserved[field], shift_s(conserved[field], -2)
            level_face = 0.5 * (normal_flux[field] + shift_s(normal_flux[field], -2)) - normal_signal * (
                above - value
            )
            level_face = jnp.where(top, normal_flux[field], level_face)
            under = jnp.where(bottom, wall[field], shift_s(level_face, 2))
            change = change + 2.0 * (under - level_face)
            if field == NF - 1:
                change = change + 2.0 * density * (fields[NSP + 3] - fields[NSP + 4])
            start = pl.multiple_of((field * ROWS + zz) * TILE, TILE)
            out_ref[pl.ds(start, TILE), :] = change
        return carry

    lax.fori_loop(0, ROWS, row, 0)


SPAN_TILES = ROWS + 2 * HALO


def span_kernel(own_ref, below_ref, above_ref, part_ref, out_ref, value_ref, flux_ref, signal_ref):
    for zz in range(-HALO, ROWS + HALO):
        fields = [row_tile(own_ref, below_ref, above_ref, field, zz) for field in range(NF)]
        _, pressure, sound, conserved = state_of(fields)
        speed = fields[NSP + 2]
        flux = flux_of(conserved, pressure, speed, 2)
        signal_ref[zz + HALO] = jnp.abs(speed) + sound
        for field in range(NF):
            value_ref[zz + HALO, field] = conserved[field]
            flux_ref[zz + HALO, field] = flux[field]

    def faces_of(place):
        signal = jnp.maximum(signal_ref[place], signal_ref[place + 1])
        faces = []
        for field in range(NF):
            flux = [flux_ref[place + k, field] for k in range(-2, 4)]
            value = [value_ref[place + k, field] for k in range(-2, 4)]
            slopes = [flux[k + 1] - flux[k] for k in range(5)]
            jumps = [value[k + 1] - value[k] for k in range(5)]
            faces.append(face_flux(flux[2], slopes, jumps, signal))
        return tuple(faces)

    def row(zz, before):
        faces = faces_of(zz + HALO)
        for field in range(NF):
            start = pl.multiple_of((field * ROWS + zz) * TILE, TILE)
            out_ref[pl.ds(start, TILE), :] = (
                part_ref[pl.ds(start, TILE), :] + before[field] - faces[field]
            )
        return faces

    lax.fori_loop(0, ROWS, row, faces_of(HALO - 1))


MASS, MOMENTUM, HEAT = 0, 5, 8
SPEED, THERMAL, VIBRATION, FRACTION, DENSITY = 9, 12, 13, 14, 19
STATE_COUNT = 20
SLOPED = 10
STATE_ROWS = 8
GRID_ROWS = 6
PAIR_INDEX = ((0, 0), (1, 1), (0, 1), (0, 2), (1, 2), (2, 2))

PRODUCT, STRESS, HEAT_FLUX, HEAT_SLOPE, MASS_FLUX, MASS_SLOPE = 0, 6, 11, 14, 17, 29
FILTERED = 41

TERMS = 12
TERM_FIELD = (0, 1, 2, 3, 4, 5, 6, 7, 8, 8, 8, 9)
TERM_MODEL = (2, 2, 2, 2, 2, 0, 0, 0, 0, 1, 2, 1)


def model_state(fields):
    mass, motion = fields[:NSP], fields[NSP : NSP + 3]
    thermal, vibration = fields[NSP + 3], fields[NSP + 4]
    density = (mass[0] + mass[1]) + (mass[2] + mass[3]) + mass[4]
    inverse = 1.0 / density
    fraction = [m * inverse for m in mass]
    return (
        list(mass)
        + [density * speed for speed in motion]
        + [density * thermal]
        + list(motion)
        + [thermal, vibration]
        + fraction
        + [density]
    )


def level_slope(value, scale):
    bottom, top = level_edges()
    above = jnp.where(top, value, shift_s(value, -2))
    below = jnp.where(bottom, value, shift_s(value, 2))
    return scale * (above - below)


def strain(slopes):
    diagonal = [2.0 * slopes[k][k] for k in range(3)]
    third = (diagonal[0] + diagonal[1] + diagonal[2]) * (1.0 / 3.0)
    first, second = diagonal[0] - third, diagonal[1] - third
    mixed = [slopes[0][1] + slopes[1][0], slopes[0][2] + slopes[2][0], slopes[1][2] + slopes[2][1]]
    last = diagonal[2] - third
    square = (
        first * first + second * second + last * last
        + 2.0 * (mixed[0] * mixed[0] + mixed[1] * mixed[1] + mixed[2] * mixed[2])
    )
    magnitude = jnp.sqrt(0.125 * square + 1e-06)
    return [first, second] + mixed + [last], magnitude


def grid_terms(here, slopes):
    deviator, magnitude = strain(slopes[:3])
    eddy = FILTER_SQUARE * here(DENSITY) * magnitude
    speed = [here(SPEED + k) for k in range(3)]
    momentum = [here(MOMENTUM + k) for k in range(3)]
    thermal = here(THERMAL)
    stress = [eddy * part for part in deviator]
    tiles = [momentum[i] * speed[j] for i, j in PAIR_INDEX]
    tiles += stress[:5]
    tiles += [m * thermal for m in momentum]
    tiles += [eddy * slopes[3][d] for d in range(3)]
    tiles += [here(MASS + s) * speed[d] for s in range(4) for d in range(3)]
    tiles += [eddy * slopes[5 + s][d] for s in range(4) for d in range(3)]
    vibration = [eddy * slopes[4][d] for d in range(3)]
    return tiles, vibration, stress[5]


def subgrid_terms(tiles, vibration, last_stress, speed, d):
    stress = tiles[STRESS : STRESS + 5] + [last_stress]
    full = ((0, 2, 3), (2, 1, 4), (3, 4, 5))
    tau = [stress[full[i][d]] for i in range(3)]
    species = [tiles[MASS_SLOPE + 3 * s + d] for s in range(4)]
    species.append(-((species[0] + species[1]) + (species[2] + species[3])))
    work = speed[0] * tau[0] + speed[1] * tau[1] + speed[2] * tau[2]
    heat = 3.5 * tiles[HEAT_SLOPE + d] + vibration[d]
    formed = FORMATION[2] * species[2] + FORMATION[3] * species[3] + FORMATION[4] * species[4]
    return species + tau + [work, heat, formed, vibration[d]]


def favre(hat):
    density = (hat[0] + hat[1]) + (hat[2] + hat[3]) + hat[4]
    inverse = 1.0 / density
    return density, [hat[5 + k] * inverse for k in range(3)], hat[8] * inverse, [
        hat[s] * inverse for s in range(4)
    ]


def contractions(hat, density, momentum, favre_here, slopes):
    speed, thermal, fraction = favre_here
    deviator, magnitude = strain(slopes[:3])
    eddy = TEST_SQUARE * density * magnitude
    stress = list(hat[STRESS : STRESS + 5])
    stress.append(-(stress[0] + stress[1]))
    sums = []
    top = bottom = None

    def add(total, value):
        return value if total is None else total + value

    off_top = off_bottom = None
    for n, (i, j) in enumerate(PAIR_INDEX):
        resolved = hat[PRODUCT + n] - momentum[i] * speed[j]
        model = stress[n] - eddy * deviator[n]
        if i == j:
            top, bottom = add(top, resolved * model), add(bottom, model * model)
        else:
            off_top, off_bottom = add(off_top, resolved * model), add(off_bottom, model * model)
    sums += [top + (off_top + off_top), bottom + (off_bottom + off_bottom)]
    top = bottom = None
    for d in range(3):
        resolved = hat[HEAT_FLUX + d] - momentum[d] * thermal
        model = hat[HEAT_SLOPE + d] - eddy * slopes[3][d]
        top, bottom = add(top, resolved * model), add(bottom, model * model)
    sums += [top, bottom]
    top = bottom = None
    for d in range(3):
        last_resolved = last_model = None
        for s in range(4):
            resolved = hat[MASS_FLUX + 3 * s + d] - momentum[d] * fraction[s]
            model = hat[MASS_SLOPE + 3 * s + d] - eddy * slopes[4 + s][d]
            last_resolved, last_model = add(last_resolved, resolved), add(last_model, model)
            top, bottom = add(top, resolved * model), add(bottom, model * model)
        top, bottom = top + last_resolved * last_model, bottom + last_model * last_model
    return sums + [top, bottom]


def filter_x(tile):
    pair = tile + shift_x(tile, -1)
    return pair + shift_x(pair, 1)


def model_kernel(
    own_ref, edge_ref, below_ref, above_ref,
    totals_ref, terms_ref,
    state_ref, halo_ref, corner_ref, tile_ref, extra_ref, wide_ref, favre_ref, sum_ref,
):
    lane = lanes()
    even = is_even()
    bottom, top = level_edges()
    low = lane < HALO
    high = lane >= LANES - HALO
    scale = jnp.where(bottom | top, 4.0, 2.0)
    packs = halo_packs(edge_ref, below_ref, above_ref)

    for field in range(NF):
        corner_ref[field] = jnp.zeros((TILE, LANES), F32)
    for zz in range(-2, 6):
        block, place = (zz + ROWS) // ROWS, zz % ROWS
        rows, halos = [], []
        start = 8 * (zz + 2)
        for field in range(NF):
            group = field * ROWS + place
            row = row_tile(own_ref, below_ref, above_ref, field, zz)
            halo = spread(packs[0][block], packs[1][block], group)
            rows.append(row)
            halos.append(jnp.where(low | high, halo, row))
            left = shift_x(jnp.where(high, halo, row), start + 3)
            right = shift_x(jnp.where(low, halo, row), 64 + start - 123)
            kept = corner_ref[field]
            kept = jnp.where((lane >= start) & (lane < start + 8), left, kept)
            corner_ref[field] = jnp.where(
                (lane >= 64 + start) & (lane < 72 + start), right, kept
            )
        states = model_state(rows)
        for k in range(STATE_COUNT):
            state_ref[zz + 2, k] = states[k]
        if -1 <= zz <= 4:
            halo_states = model_state(halos)
            for k in range(SLOPED):
                halo_ref[zz + 1, k] = halo_states[SPEED + k]

    def grid_row(row, carry):
        def here(k):
            return state_ref[row + 1, k]

        slopes = []
        for k in range(SLOPED - 1):
            value, halo = here(SPEED + k), halo_ref[row, k]
            along_x = shift_x(jnp.where(lane == 0, halo, value), -1) - shift_x(
                jnp.where(lane == LANES - 1, halo, value), 1
            )
            along_z = state_ref[row + 2, SPEED + k] - state_ref[row, SPEED + k]
            slopes.append((along_x, level_slope(value, scale), along_z))
        tiles, vibration, last = grid_terms(here, slopes)
        for k in range(FILTERED):
            tile_ref[row, k] = tiles[k]
        for d in range(3):
            extra_ref[row, d] = vibration[d]
        extra_ref[row, 3] = last
        hat = []
        for k in range(SPEED):
            total = (state_ref[row, k] + state_ref[row + 2, k]) + 2.0 * here(k)
            hat.append(filter_x(total))
        density, speed, thermal, fraction = favre(hat)
        for k, value in enumerate(speed + [thermal] + fraction):
            favre_ref[row, k] = value
        for k in range(3):
            wide_ref[row, k] = hat[MOMENTUM + k]
        wide_ref[row, 3] = density
        return carry

    lax.fori_loop(0, GRID_ROWS, grid_row, 0)

    corner = model_state([corner_ref[field] for field in range(NF)])

    def corner_slopes(value):
        along_x = shift_x(value, -1) - shift_x(value, 1)
        along_z = shift_x(value, -8) - shift_x(value, 8)
        return along_x, level_slope(value, scale), along_z

    def corner_filter(value):
        pair = value + shift_x(value, -8)
        return filter_x(pair + shift_x(pair, 8))

    slopes = [corner_slopes(corner[SPEED + k]) for k in range(SLOPED - 1)]
    corner_tiles, corner_vibration, corner_last = grid_terms(lambda k: corner[k], slopes)
    hat = [corner_filter(corner[k]) for k in range(SPEED)]
    density, speed, thermal, fraction = favre(hat)
    slopes = [corner_slopes(value) for value in speed + [thermal] + fraction]
    corner_sums = contractions(
        [corner_filter(tile) for tile in corner_tiles],
        density, hat[5:8], (speed, thermal, fraction), slopes,
    )
    corner_totals = []
    for value in corner_sums:
        value = value + shift_x(value, -8)
        corner_totals.append(value + shift_x(value, -16))
    corner_x = subgrid_terms(
        corner_tiles, corner_vibration, corner_last, [corner[SPEED + k] for k in range(3)], 0
    )

    for k in range(6):
        sum_ref[k] = jnp.zeros((TILE, LANES), F32)

    def test_row(zz, carry):
        row = zz + 1
        hat = []
        for k in range(FILTERED):
            total = (tile_ref[row - 1, k] + tile_ref[row + 1, k]) + 2.0 * tile_ref[row, k]
            hat.append(filter_x(total))
        slopes = []
        for k in range(8):
            value = favre_ref[row, k]
            along_x = shift_x(value, -1) - shift_x(value, 1)
            along_z = favre_ref[row + 1, k] - favre_ref[row - 1, k]
            slopes.append((along_x, level_slope(value, scale), along_z))
        values = [favre_ref[row, k] for k in range(8)]
        sums = contractions(
            hat, wide_ref[row, 3], [wide_ref[row, k] for k in range(3)],
            (values[:3], values[3], values[4:]), slopes,
        )
        for k in range(6):
            sum_ref[k] = sum_ref[k] + sums[k]
        return carry

    lax.fori_loop(0, ROWS, test_row, 0)

    edges = jnp.zeros((TILE, LANES), F32)
    for k in range(3):
        packed = []
        for main, side in ((sum_ref[2 * k], corner_totals[2 * k]), (sum_ref[2 * k + 1], corner_totals[2 * k + 1])):
            main = jnp.where(lane < 2, shift_x(side, -19), main)
            main = jnp.where(lane >= LANES - 2, shift_x(side, 126 - 83), main)
            packed.append((main + shift_s(main, 1), side + shift_s(side, 1), main, side))
        top_main = shift_s(packed[0][0], -1) * (1.0 / 512.0)
        top_side = shift_s(packed[0][1], -1) * (1.0 / 512.0)
        totals_ref[pl.ds(k * TILE, TILE), :] = jnp.where(even, top_main, packed[1][0] * (1.0 / 1024.0))
        side = jnp.where(even, top_side, packed[1][1] * (1.0 / 1024.0))
        edges = jnp.where(lane == 2 * k, shift_x(side, 2 * k - 18), edges)
        edges = jnp.where(lane == 2 * k + 1, shift_x(side, 2 * k + 1 - 85), edges)
    totals_ref[pl.ds(3 * TILE, TILE), :] = edges

    for n in range(TERMS):
        corner_ref[n] = corner_x[n]

    def term_row(zz, carry):
        row = zz + 1

        def terms(place, d):
            tiles = {k: tile_ref[place, k] for k in range(STRESS, STRESS + 5)}
            tiles.update({HEAT_SLOPE + d: tile_ref[place, HEAT_SLOPE + d]})
            tiles.update(
                {MASS_SLOPE + 3 * s + d: tile_ref[place, MASS_SLOPE + 3 * s + d] for s in range(4)}
            )
            listed = [tiles.get(k) for k in range(FILTERED)]
            speed = [state_ref[place + 1, SPEED + k] for k in range(3)]
            return subgrid_terms(
                listed, [extra_ref[place, k] for k in range(3)], extra_ref[place, 3], speed, d
            )

        along_x, along_y = terms(row, 0), terms(row, 1)
        before, after = terms(row - 1, 2), terms(row + 1, 2)
        for n in range(TERMS):
            side = corner_ref[n]
            right = pltpu.roll(side, 42 - 8 * zz, 1)
            left = pltpu.roll(side, LANES - 18 - 8 * zz, 1)
            terms_ref[zz, n, 0] = jnp.where(lane == LANES - 1, right, shift_x(along_x[n], -1))
            terms_ref[zz, n, 1] = jnp.where(lane == 0, left, shift_x(along_x[n], 1))
            terms_ref[zz, n, 2] = after[n] - before[n]
            terms_ref[zz, n, 3] = jnp.where(top, along_y[n], shift_s(along_y[n], -2))
            terms_ref[zz, n, 4] = jnp.where(bottom, -along_y[n], shift_s(along_y[n], 2))
        return carry

    lax.fori_loop(0, ROWS, term_row, 0)


def final_kernel(position_ref, *refs, span_count, parts):
    part_refs = refs[:parts]
    base_ref, terms_ref, out_ref, coefficient_ref, scratch = refs[parts:]
    lane = lanes()
    even = is_even()
    bottom, top = level_edges()
    totals = [
        (tile_of(part_refs[0], k) + tile_of(part_refs[1], k))
        + (tile_of(part_refs[2], k) + tile_of(part_refs[3], k))
        for k in range(4)
    ]
    ratios = []
    for total in totals:
        total = total * (1.0 / span_count)
        numerator = jnp.where(even, total, shift_s(total, 1))
        denominator = jnp.where(even, shift_s(total, -1), total)
        ratios.append(numerator / (denominator + RATIO_EPSILON))
    first, last = position_ref[0] == 1, position_ref[1] == 1
    here, ahead, behind, above, below = [], [], [], [], []
    for k in range(3):
        ratio = ratios[k]
        scratch[...] = ratio
        coefficient_ref[k] = scratch[pl.ds(0, 4, stride=2), :]
        before = jnp.where(first, ratio, shift_x(ratios[3], -2 * k))
        after = jnp.where(last, ratio, shift_x(ratios[3], 127 - (2 * k + 1)))
        ratio = 0.25 * ratio
        here.append(ratio)
        ahead.append(jnp.where(lane == LANES - 1, 0.25 * after, shift_x(ratio, -1)))
        behind.append(jnp.where(lane == 0, 0.25 * before, shift_x(ratio, 1)))
        above.append(2.0 * jnp.where(top, ratio, shift_s(ratio, -2)))
        below.append(2.0 * jnp.where(bottom, ratio, shift_s(ratio, 2)))

    for zz in range(ROWS):
        sums = [base_ref[pl.ds((field * ROWS + zz) * TILE, TILE), :] for field in range(NF)]
        for n in range(TERMS):
            k = TERM_MODEL[n]
            change = (
                (ahead[k] * terms_ref[zz, n, 0] - behind[k] * terms_ref[zz, n, 1])
                + here[k] * terms_ref[zz, n, 2]
                + (above[k] * terms_ref[zz, n, 3] - below[k] * terms_ref[zz, n, 4])
            )
            sums[TERM_FIELD[n]] = sums[TERM_FIELD[n]] + change
        for field in range(NF):
            out_ref[pl.ds(field * 32 + zz, TILE, stride=4), :] = sums[field]


def call(kernel, out_shapes, scratch=(), scalars=0, inputs=0, **options):
    smem = pl.BlockSpec(memory_space=pltpu.SMEM)
    shapes = [jax.ShapeDtypeStruct(shape, F32) for shape in out_shapes]
    return pl.pallas_call(
        kernel,
        out_shape=shapes,
        in_specs=[smem] * scalars + [VMEM] * inputs,
        out_specs=[VMEM] * len(shapes),
        scratch_shapes=[pltpu.VMEM(shape, F32) for shape in scratch],
        **options,
    )


def body(constituent_mass, flow_speeds, thermal_pair, blowing_indicator):
    count_x = lax.axis_size("gx")
    count_z = lax.axis_size("gz")
    column = lax.axis_index("gx")
    position = jnp.stack([column == 0, column == count_x - 1]).astype(jnp.int32)

    def ring(axis, count, step):
        return lambda value: lax.ppermute(
            value, axis, [(i, (i + step) % count) for i in range(count)]
        )

    own, to_left, to_right, up, down = call(
        pack_kernel,
        [
            (GROUPS * TILE, LANES), (TILE, LANES), (TILE, LANES),
            (MAIN_ROWS, LANES), (MAIN_ROWS, LANES),
        ],
        inputs=3,
    )(
        constituent_mass.reshape(-1, LANES),
        flow_speeds.reshape(-1, LANES),
        thermal_pair.reshape(-1, LANES),
    )
    got_left = ring("gx", count_x, 1)(to_right)
    got_right = ring("gx", count_x, -1)(to_left)
    up, down, edge = call(
        edge_kernel,
        [(MESSAGE_ROWS, LANES), (MESSAGE_ROWS, LANES), (2 * TILE, LANES)],
        scalars=1,
        inputs=6,
    )(position, got_left, got_right, to_left, to_right, up, down)
    below = ring("gz", count_z, 1)(up)
    above = ring("gz", count_z, -1)(down)

    (part,) = call(
        stream_kernel,
        [(GROUPS * TILE, LANES)],
        scratch=[(NF * TILE, LANES), (4 * TILE, LANES)],
        inputs=3,
    )(own, edge, blowing_indicator)

    totals, terms = call(
        model_kernel,
        [(4 * TILE, LANES), (ROWS, TERMS, 5, TILE, LANES)],
        scratch=[
            (STATE_ROWS, STATE_COUNT, TILE, LANES),
            (GRID_ROWS, SLOPED, TILE, LANES),
            (TERMS, TILE, LANES),
            (GRID_ROWS, FILTERED, TILE, LANES),
            (GRID_ROWS, 4, TILE, LANES),
            (GRID_ROWS, 4, TILE, LANES),
            (GRID_ROWS, 8, TILE, LANES),
            (6, TILE, LANES),
        ],
        inputs=4,
    )(own, edge, below, above)

    (base,) = call(
        span_kernel,
        [(GROUPS * TILE, LANES)],
        scratch=[
            (SPAN_TILES, NF, TILE, LANES), (SPAN_TILES, NF, TILE, LANES), (SPAN_TILES, TILE, LANES)
        ],
        inputs=4,
    )(own, below, above, part)

    def crossed(value, mask):
        return lax.ppermute(value, "gz", [(i, i ^ mask) for i in range(count_z)])

    totals = totals + crossed(totals, 1)
    reach = 2
    while count_z > 4 * reach:
        a, b, c = (crossed(totals, k * reach) for k in (1, 2, 3))
        totals = (totals + a) + (b + c)
        reach *= 4
    parts = [totals] + [
        crossed(totals, k * reach) if k * reach < count_z else jnp.zeros_like(totals)
        for k in (1, 2, 3)
    ]

    def final(position_ref, *refs):
        final_kernel(position_ref, *refs, span_count=TILE * count_z, parts=4)

    tendency, coefficients = call(
        final,
        [(NF * 32, LANES), (3, 4, LANES)],
        scratch=[(TILE, LANES)],
        scalars=1,
        inputs=6,
    )(position, *parts, base, terms)
    return tendency.reshape(NF, 4, TILE, LANES), coefficients


def solution(mesh):
    placed = (
        P(None, None, "gz", "gx"),
        P(None, None, "gz", "gx"),
        P(None, None, "gz", "gx"),
        P("gz", "gx"),
    )
    return jax.shard_map(
        body,
        mesh=mesh,
        in_specs=placed,
        out_specs=(P(None, None, "gz", "gx"), P(None, None, "gx")),
        check_vma=False,
    )
```

```python
import jax
import jax.numpy as jnp
from jax import lax
from jax.experimental import pallas as pl
from jax.experimental.pallas import tpu as pltpu
from jax.sharding import PartitionSpec as P


NSP = 5
NF = 10
ROWS = 4
TILE = 8
LANES = 128
HALO = 3
SPAN = 8
LAST = LANES - 5
GROUPS = NF * ROWS
PAIRS = NF // 2
PACKS = 3
PACK_ROWS = PACKS * TILE
MAIN_ROWS = PAIRS * HALO * TILE
MESSAGE_ROWS = MAIN_ROWS + PACK_ROWS

HEAT_RATIO = 1.4
FILTER_SQUARE = 0.5 ** (2.0 / 3.0)
TEST_SQUARE = 2.0 ** (2.0 / 3.0)
FORMATION = (0.0, 0.0, 0.1, 0.5, 0.25)
BLOWING = 0.3
SMOOTH_FLOOR = 0.01
RATIO_EPSILON = 1e-06

VMEM = pl.BlockSpec(memory_space=pltpu.VMEM)
F32 = jnp.float32
SMALL = pltpu.CompilerParams(vmem_limit_bytes=8 << 20)


def lanes():
    return lax.broadcasted_iota(jnp.int32, (TILE, LANES), 1)


def sublanes():
    return lax.broadcasted_iota(jnp.int32, (TILE, LANES), 0)


def shift_x(tile, step):
    if isinstance(step, int):
        step = step % LANES
        if step == 0:
            return tile
    return pltpu.roll(tile, step, 1)


def shift_s(tile, step):
    return pltpu.roll(tile, step % TILE, 0)


def is_even():
    return (sublanes() & 1) == 0


def level_edges():
    level = sublanes() >> 1
    return level == 0, level == 3


def tile_of(ref, index):
    return ref[pl.ds(index * TILE, TILE), :]


def pack_kernel(
    mass_hbm, speed_hbm, heat_hbm, own_ref, left_ref, right_ref, to_left_ref, to_right_ref,
    up_ref, down_ref, mass_ref, speed_ref, heat_ref, arrived
):
    copies = [
        pltpu.make_async_copy(source, target, arrived.at[k])
        for k, (source, target) in enumerate(
            ((mass_hbm, mass_ref), (speed_hbm, speed_ref), (heat_hbm, heat_ref))
        )
    ]
    for copy in copies:
        copy.start()
    for copy in copies:
        copy.wait()
    lane = lanes()
    even = is_even()
    tiles = {}
    left = right = jnp.zeros((TILE, LANES), F32)
    for field in range(NF):
        if field < NSP:
            ref, base = mass_ref, field
        elif field < NSP + 3:
            ref, base = speed_ref, field - NSP
        else:
            ref, base = heat_ref, field - NSP - 3
        for zz in range(ROWS):
            tile = ref[pl.ds(base * 32 + zz, TILE, stride=4), :]
            tiles[field, zz] = tile
            own_ref[pl.ds((field * ROWS + zz) * TILE, TILE), :] = tile
            start = 32 * (field % 4) + SPAN * zz
            reached = lane >= start
            left = jnp.where(reached, shift_x(tile, start + HALO), left)
            right = jnp.where(reached, shift_x(tile, start - LAST), right)
        if field % 4 == 3 or field == NF - 1:
            slot = pl.ds(field // 4 * TILE, TILE)
            left_ref[slot, :] = left
            right_ref[slot, :] = right
            to_left_ref[slot, :] = shift_x(left, 2)
            to_right_ref[slot, :] = shift_x(right, -2)
        if field % 2:
            pair = field // 2
            for k in range(HALO):
                slot = pl.ds((pair * HALO + k) * TILE, TILE)
                up_ref[slot, :] = jnp.where(
                    even, shift_s(tiles[field - 1, k + 1], -1), tiles[field, k + 1]
                )
                down_ref[slot, :] = jnp.where(
                    even, tiles[field, k], shift_s(tiles[field - 1, k], 1)
                )


def edge_kernel(
    got_left_ref, got_right_ref, left_ref, right_ref, up_in, down_in,
    up_ref, down_ref, edge_ref
):
    up_ref[pl.ds(0, MAIN_ROWS), :] = up_in[...]
    down_ref[pl.ds(0, MAIN_ROWS), :] = down_in[...]
    even = is_even()
    place = lanes() & (SPAN - 1)
    column = lax.axis_index("gx")
    first, last = column == 0, column == lax.axis_size("gx") - 1
    for k in range(PACKS):
        left, right = tile_of(left_ref, k), tile_of(right_ref, k)
        clamped = jnp.where(
            place == 2, shift_x(left, -1),
            jnp.where(place == 1, shift_x(left, -2), shift_x(left, -3)),
        )
        left = jnp.where(place < 3, jnp.where(first, clamped, tile_of(got_left_ref, k)), left)
        clamped = jnp.where(
            place == 5, shift_x(right, 1),
            jnp.where(place == 6, shift_x(right, 2), shift_x(right, 3)),
        )
        right = jnp.where(place > 4, jnp.where(last, clamped, tile_of(got_right_ref, k)), right)
        edge_ref[pl.ds(k * TILE, TILE), :] = left
        edge_ref[pl.ds((PACKS + k) * TILE, TILE), :] = right
        slot = pl.ds(MAIN_ROWS + k * TILE, TILE)
        up_ref[slot, :] = jnp.where(even, shift_s(left, -1), right)
        down_ref[slot, :] = jnp.where(even, left, shift_s(right, 1))


def row_tile(own_ref, below_ref, above_ref, field, zz):
    if 0 <= zz < ROWS:
        return tile_of(own_ref, field * ROWS + zz)
    pair, second = divmod(field, 2)
    if zz < 0:
        k = zz + ROWS
        halo = tile_of(below_ref, pair * HALO + k - 1)
        if second:
            halo = shift_s(halo, -1)
        return jnp.where(is_even(), halo, shift_s(tile_of(own_ref, field * ROWS + k), 1))
    k = zz - ROWS
    halo = tile_of(above_ref, pair * HALO + k)
    if second:
        halo = shift_s(halo, 1)
    return jnp.where(is_even(), shift_s(tile_of(own_ref, field * ROWS + k), -1), halo)


def edge_packs(edge_ref, below_ref, above_ref, k):
    even = is_even()
    left, right = tile_of(edge_ref, k), tile_of(edge_ref, PACKS + k)
    low, high = tile_of(below_ref, MAIN_ROWS // TILE + k), tile_of(above_ref, MAIN_ROWS // TILE + k)
    return (
        (
            jnp.where(even, low, shift_s(left, 1)),
            left,
            jnp.where(even, shift_s(left, -1), shift_s(high, 1)),
        ),
        (
            jnp.where(even, shift_s(low, -1), shift_s(right, 1)),
            right,
            jnp.where(even, shift_s(right, -1), high),
        ),
    )


def state_of(fields):
    mass, motion = fields[:NSP], fields[NSP : NSP + 3]
    thermal, vibration = fields[NSP + 3], fields[NSP + 4]
    density = (mass[0] + mass[1]) + (mass[2] + mass[3]) + mass[4]
    formed = FORMATION[2] * mass[2] + FORMATION[3] * mass[3] + FORMATION[4] * mass[4]
    motion_square = motion[0] * motion[0] + motion[1] * motion[1] + motion[2] * motion[2]
    energy = density * (2.5 * thermal + vibration + 0.5 * motion_square) + formed
    conserved = (
        list(mass) + [density * speed for speed in motion] + [energy, density * vibration]
    )
    return density, density * thermal, jnp.sqrt(HEAT_RATIO * thermal), conserved


def flux_of(conserved, pressure, speed, component):
    flux = [value * speed for value in conserved]
    flux[NSP + component] = flux[NSP + component] + pressure
    flux[NSP + 3] = flux[NSP + 3] + pressure * speed
    return flux


def correction(d0, d1, d2, d3):
    floor = 4.0 * SMOOTH_FLOOR * 12.0 / 13.0
    share = 3.0 / 13.0
    e0, e1, e2 = d1 - d0, d2 - d1, d3 - d2
    g0, g1, g2 = e0 + (d1 + d1), d1 + d2, e2 - (d2 + d2)
    b0 = (e0 * e0 + floor) + share * (g0 * g0)
    b1 = (e1 * e1 + floor) + share * (g1 * g1)
    b2 = (e2 * e2 + floor) + share * (g2 * g2)
    p0, p1, p2 = b1 * b2, b0 * b2, b0 * b1
    w0 = p0 * p0
    w1 = 6.0 * (p1 * p1)
    w2 = 3.0 * (p2 * p2)
    r0 = 5.0 * d1 - (d0 + d0)
    r1 = d1 + (d2 + d2)
    r2 = 4.0 * d2 - d3
    return (w0 * r0 + w1 * r1 + w2 * r2) / (w0 + w1 + w2)


def face_flux(here, slopes, jumps, signal):
    waves = [signal * jump for jump in jumps]
    plus = [slopes[k] + waves[k] for k in range(4)]
    minus = [waves[k] - slopes[k] for k in range(1, 5)]
    gain = correction(*plus)
    loss = correction(minus[3], minus[2], minus[1], minus[0])
    return here + 0.5 * (slopes[2] - waves[2]) + (gain + loss) * (1.0 / 12.0)


def stream_kernel(own_ref, edge_ref, blow_ref, out_ref, edge_face_ref, blow_rows):
    lane = lanes()
    bottom, top = level_edges()
    for level in range(4):
        blow_rows[pl.ds(level * TILE, TILE), :] = blow_ref[...].astype(F32)

    def faces_along_x(flux, conserved, signal):
        slope = shift_x(flux, -1) - flux
        jump = shift_x(conserved, -1) - conserved
        slopes = [shift_x(slope, -k) for k in range(-2, 3)]
        jumps = [shift_x(jump, -k) for k in range(-2, 3)]
        return face_flux(flux, slopes, jumps, signal)

    fields = []
    for field in range(NF):
        pack, start = field // 4, 32 * (field % 4)
        fields.append(
            jnp.where(
                lane < 32,
                shift_x(tile_of(edge_ref, pack), -start),
                shift_x(tile_of(edge_ref, PACKS + pack), 32 - start),
            )
        )
    fields = [jnp.where(lane < 64, value, shift_x(value, 64)) for value in fields]
    density, pressure, sound, conserved = state_of(fields)
    flux = flux_of(conserved, pressure, fields[NSP], 0)
    signal = jnp.abs(fields[NSP]) + sound
    signal = jnp.maximum(signal, shift_x(signal, -1))
    for field in range(NF):
        edge_face_ref[pl.ds(field * TILE, TILE), :] = faces_along_x(
            flux[field], conserved[field], signal
        )

    def row(zz, carry):
        fields = []
        for field in range(NF):
            start = pl.multiple_of((field * ROWS + zz) * TILE, TILE)
            fields.append(own_ref[pl.ds(start, TILE), :])
        density, pressure, sound, conserved = state_of(fields)
        speed = fields[NSP]
        flux = flux_of(conserved, pressure, speed, 0)
        signal = jnp.abs(speed) + sound
        signal = jnp.maximum(signal, shift_x(signal, -1))

        normal_speed = fields[NSP + 1]
        normal_flux = flux_of(conserved, pressure, normal_speed, 1)
        normal_signal = jnp.abs(normal_speed) + sound
        normal_signal = 0.5 * jnp.maximum(normal_signal, shift_s(normal_signal, -2))
        blown = BLOWING * blow_rows[pl.ds(zz, TILE, stride=4), :]
        lift = blown / density
        enthalpy = 3.5 * fields[NSP + 3] + fields[NSP + 4] + 0.5 * lift * lift
        wall = [lift * fields[s] for s in range(NSP)]
        formed = FORMATION[2] * wall[2] + FORMATION[3] * wall[3] + FORMATION[4] * wall[4]
        zero = jnp.zeros((TILE, LANES), F32)
        wall = wall + [
            zero, blown * lift + pressure, zero, blown * enthalpy + formed, blown * fields[NSP + 4]
        ]

        for field in range(NF):
            face = faces_along_x(flux[field], conserved[field], signal)
            edge_face = edge_face_ref[pl.ds(field * TILE, TILE), :]
            left = pltpu.roll(edge_face, LANES - 3 - SPAN * zz, 1)
            right = pltpu.roll(edge_face, LANES - 37 - SPAN * zz, 1)
            face = jnp.where(lane < 2, left, jnp.where(lane >= LANES - 3, right, face))
            change = shift_x(jnp.where(lane == LANES - 1, left, face), 1) - face

            value, above = conserved[field], shift_s(conserved[field], -2)
            level_face = 0.5 * (normal_flux[field] + shift_s(normal_flux[field], -2)) - normal_signal * (
                above - value
            )
            level_face = jnp.where(top, normal_flux[field], level_face)
            under = jnp.where(bottom, wall[field], shift_s(level_face, 2))
            change = change + 2.0 * (under - level_face)
            if field == NF - 1:
                change = change + 2.0 * density * (fields[NSP + 3] - fields[NSP + 4])
            start = pl.multiple_of((field * ROWS + zz) * TILE, TILE)
            out_ref[pl.ds(start, TILE), :] = change
        return carry

    lax.fori_loop(0, ROWS, row, 0)


SPAN_TILES = ROWS + 2 * HALO


def span_kernel(own_ref, below_ref, above_ref, part_ref, out_ref, value_ref, flux_ref, signal_ref):
    for zz in range(-HALO, ROWS + HALO):
        fields = [row_tile(own_ref, below_ref, above_ref, field, zz) for field in range(NF)]
        _, pressure, sound, conserved = state_of(fields)
        speed = fields[NSP + 2]
        flux = flux_of(conserved, pressure, speed, 2)
        signal_ref[zz + HALO] = jnp.abs(speed) + sound
        for field in range(NF):
            value_ref[zz + HALO, field] = conserved[field]
            flux_ref[zz + HALO, field] = flux[field]

    def faces_of(place):
        signal = jnp.maximum(signal_ref[place], signal_ref[place + 1])
        faces = []
        for field in range(NF):
            flux = [flux_ref[place + k, field] for k in range(-2, 4)]
            value = [value_ref[place + k, field] for k in range(-2, 4)]
            slopes = [flux[k + 1] - flux[k] for k in range(5)]
            jumps = [value[k + 1] - value[k] for k in range(5)]
            faces.append(face_flux(flux[2], slopes, jumps, signal))
        return tuple(faces)

    def row(zz, before):
        faces = faces_of(zz + HALO)
        for field in range(NF):
            start = pl.multiple_of((field * ROWS + zz) * TILE, TILE)
            out_ref[pl.ds(start, TILE), :] = (
                part_ref[pl.ds(start, TILE), :] + before[field] - faces[field]
            )
        return faces

    lax.fori_loop(0, ROWS, row, faces_of(HALO - 1))


MASS, MOMENTUM, HEAT = 0, 5, 8
SPEED, THERMAL, VIBRATION, FRACTION, DENSITY = 9, 12, 13, 14, 19
STATE_COUNT = 20
SLOPED = 10
STATE_ROWS = 8
GRID_ROWS = 6
PAIR_INDEX = ((0, 0), (1, 1), (0, 1), (0, 2), (1, 2), (2, 2))

PRODUCT, STRESS, HEAT_FLUX, HEAT_SLOPE, MASS_FLUX, MASS_SLOPE = 0, 6, 11, 14, 17, 29
FILTERED = 41

TERMS = 12
TERM_FIELD = (0, 1, 2, 3, 4, 5, 6, 7, 8, 8, 8, 9)
TERM_MODEL = (2, 2, 2, 2, 2, 0, 0, 0, 0, 1, 2, 1)


def model_state(fields):
    mass, motion = fields[:NSP], fields[NSP : NSP + 3]
    thermal, vibration = fields[NSP + 3], fields[NSP + 4]
    density = (mass[0] + mass[1]) + (mass[2] + mass[3]) + mass[4]
    inverse = 1.0 / density
    fraction = [m * inverse for m in mass]
    return (
        list(mass)
        + [density * speed for speed in motion]
        + [density * thermal]
        + list(motion)
        + [thermal, vibration]
        + fraction
        + [density]
    )


def level_slope(value, scale):
    bottom, top = level_edges()
    above = jnp.where(top, value, shift_s(value, -2))
    below = jnp.where(bottom, value, shift_s(value, 2))
    return scale * (above - below)


def strain(slopes):
    diagonal = [2.0 * slopes[k][k] for k in range(3)]
    third = (diagonal[0] + diagonal[1] + diagonal[2]) * (1.0 / 3.0)
    first, second = diagonal[0] - third, diagonal[1] - third
    mixed = [slopes[0][1] + slopes[1][0], slopes[0][2] + slopes[2][0], slopes[1][2] + slopes[2][1]]
    last = diagonal[2] - third
    square = (
        first * first + second * second + last * last
        + 2.0 * (mixed[0] * mixed[0] + mixed[1] * mixed[1] + mixed[2] * mixed[2])
    )
    magnitude = jnp.sqrt(0.125 * square + 1e-06)
    return [first, second] + mixed + [last], magnitude


def grid_terms(here, slopes):
    deviator, magnitude = strain(slopes[:3])
    eddy = FILTER_SQUARE * here(DENSITY) * magnitude
    speed = [here(SPEED + k) for k in range(3)]
    momentum = [here(MOMENTUM + k) for k in range(3)]
    thermal = here(THERMAL)
    stress = [eddy * part for part in deviator]
    tiles = [momentum[i] * speed[j] for i, j in PAIR_INDEX]
    tiles += stress[:5]
    tiles += [m * thermal for m in momentum]
    tiles += [eddy * slopes[3][d] for d in range(3)]
    tiles += [here(MASS + s) * speed[d] for s in range(4) for d in range(3)]
    tiles += [eddy * slopes[5 + s][d] for s in range(4) for d in range(3)]
    vibration = [eddy * slopes[4][d] for d in range(3)]
    return tiles, vibration, stress[5]


def subgrid_terms(tiles, vibration, last_stress, speed, d):
    stress = tiles[STRESS : STRESS + 5] + [last_stress]
    full = ((0, 2, 3), (2, 1, 4), (3, 4, 5))
    tau = [stress[full[i][d]] for i in range(3)]
    species = [tiles[MASS_SLOPE + 3 * s + d] for s in range(4)]
    species.append(-((species[0] + species[1]) + (species[2] + species[3])))
    work = speed[0] * tau[0] + speed[1] * tau[1] + speed[2] * tau[2]
    heat = 3.5 * tiles[HEAT_SLOPE + d] + vibration[d]
    formed = FORMATION[2] * species[2] + FORMATION[3] * species[3] + FORMATION[4] * species[4]
    return species + tau + [work, heat, formed, vibration[d]]


def favre(hat):
    density = (hat[0] + hat[1]) + (hat[2] + hat[3]) + hat[4]
    inverse = 1.0 / density
    return density, [hat[5 + k] * inverse for k in range(3)], hat[8] * inverse, [
        hat[s] * inverse for s in range(4)
    ]


def contractions(hat, density, momentum, favre_here, slopes):
    speed, thermal, fraction = favre_here
    deviator, magnitude = strain(slopes[:3])
    eddy = TEST_SQUARE * density * magnitude
    stress = list(hat[STRESS : STRESS + 5])
    stress.append(-(stress[0] + stress[1]))
    sums = []
    top = bottom = None

    def add(total, value):
        return value if total is None else total + value

    off_top = off_bottom = None
    for n, (i, j) in enumerate(PAIR_INDEX):
        resolved = hat[PRODUCT + n] - momentum[i] * speed[j]
        model = stress[n] - eddy * deviator[n]
        if i == j:
            top, bottom = add(top, resolved * model), add(bottom, model * model)
        else:
            off_top, off_bottom = add(off_top, resolved * model), add(off_bottom, model * model)
    sums += [top + (off_top + off_top), bottom + (off_bottom + off_bottom)]
    top = bottom = None
    for d in range(3):
        resolved = hat[HEAT_FLUX + d] - momentum[d] * thermal
        model = hat[HEAT_SLOPE + d] - eddy * slopes[3][d]
        top, bottom = add(top, resolved * model), add(bottom, model * model)
    sums += [top, bottom]
    top = bottom = None
    for d in range(3):
        last_resolved = last_model = None
        for s in range(4):
            resolved = hat[MASS_FLUX + 3 * s + d] - momentum[d] * fraction[s]
            model = hat[MASS_SLOPE + 3 * s + d] - eddy * slopes[4 + s][d]
            last_resolved, last_model = add(last_resolved, resolved), add(last_model, model)
            top, bottom = add(top, resolved * model), add(bottom, model * model)
        top, bottom = top + last_resolved * last_model, bottom + last_model * last_model
    return sums + [top, bottom]


def filter_x(tile):
    pair = tile + shift_x(tile, -1)
    return pair + shift_x(pair, 1)


def model_kernel(
    own_ref, edge_ref, below_ref, above_ref,
    totals_ref, tile_ref, extra_ref, corner_x_ref, state_ref,
    corner_ref, wide_ref, favre_ref, sum_ref,
):
    lane = lanes()
    even = is_even()
    bottom, top = level_edges()
    scale = jnp.where(bottom | top, 4.0, 2.0)

    corner = []
    for field in range(NF):
        if field % 4 == 0:
            packs = edge_packs(edge_ref, below_ref, above_ref, field // 4)
        start = 32 * (field % 4)
        tile = None
        for side in range(2):
            for block, (bound, move) in enumerate(((0, -16), (16, 16), (48, 48))):
                moved = shift_x(packs[side][block], 64 * side + move - start)
                tile = moved if tile is None else jnp.where(lane >= 64 * side + bound, moved, tile)
        corner.append(tile)
    corner = model_state(corner)
    for k in range(SLOPED - 1):
        corner_ref[k] = corner[SPEED + k]

    for zz in range(-2, 6):
        states = model_state(
            [row_tile(own_ref, below_ref, above_ref, field, zz) for field in range(NF)]
        )
        for k in range(STATE_COUNT):
            state_ref[zz + 2, k] = states[k]

    def grid_row(row, carry):
        def here(k):
            return state_ref[row + 1, k]

        slopes = []
        for k in range(SLOPED - 1):
            value, side = here(SPEED + k), corner_ref[k]
            ahead = jnp.where(lane == 0, pltpu.roll(side, 51 - SPAN * row, 1), value)
            behind = jnp.where(lane == LANES - 1, pltpu.roll(side, 117 - SPAN * row, 1), value)
            along_x = shift_x(ahead, -1) - shift_x(behind, 1)
            along_z = state_ref[row + 2, SPEED + k] - state_ref[row, SPEED + k]
            slopes.append((along_x, level_slope(value, scale), along_z))
        tiles, vibration, last = grid_terms(here, slopes)
        for k in range(FILTERED):
            tile_ref[row, k] = tiles[k]
        for d in range(3):
            extra_ref[row, d] = vibration[d]
        extra_ref[row, 3] = last
        hat = []
        for k in range(SPEED):
            total = (state_ref[row, k] + state_ref[row + 2, k]) + 2.0 * here(k)
            hat.append(filter_x(total))
        density, speed, thermal, fraction = favre(hat)
        for k, value in enumerate(speed + [thermal] + fraction):
            favre_ref[row, k] = value
        for k in range(3):
            wide_ref[row, k] = hat[MOMENTUM + k]
        wide_ref[row, 3] = density
        return carry

    lax.fori_loop(0, GRID_ROWS, grid_row, 0)

    def corner_slopes(value):
        along_x = shift_x(value, -1) - shift_x(value, 1)
        along_z = shift_x(value, -SPAN) - shift_x(value, SPAN)
        return along_x, level_slope(value, scale), along_z

    def corner_filter(value):
        pair = value + shift_x(value, -SPAN)
        return filter_x(pair + shift_x(pair, SPAN))

    slopes = [corner_slopes(corner[SPEED + k]) for k in range(SLOPED - 1)]
    corner_tiles, corner_vibration, corner_last = grid_terms(lambda k: corner[k], slopes)
    hat = [corner_filter(corner[k]) for k in range(SPEED)]
    density, speed, thermal, fraction = favre(hat)
    slopes = [corner_slopes(value) for value in speed + [thermal] + fraction]
    corner_sums = contractions(
        [corner_filter(tile) for tile in corner_tiles],
        density, hat[5:8], (speed, thermal, fraction), slopes,
    )
    corner_totals = []
    for value in corner_sums:
        value = value + shift_x(value, -SPAN)
        corner_totals.append(value + shift_x(value, -2 * SPAN))
    corner_x = subgrid_terms(
        corner_tiles, corner_vibration, corner_last, [corner[SPEED + k] for k in range(3)], 0
    )
    for n in range(TERMS):
        corner_x_ref[n] = corner_x[n]

    for k in range(6):
        sum_ref[k] = jnp.zeros((TILE, LANES), F32)

    def test_row(zz, carry):
        row = zz + 1
        hat = []
        for k in range(FILTERED):
            total = (tile_ref[row - 1, k] + tile_ref[row + 1, k]) + 2.0 * tile_ref[row, k]
            hat.append(filter_x(total))
        slopes = []
        for k in range(8):
            value = favre_ref[row, k]
            along_x = shift_x(value, -1) - shift_x(value, 1)
            along_z = favre_ref[row + 1, k] - favre_ref[row - 1, k]
            slopes.append((along_x, level_slope(value, scale), along_z))
        values = [favre_ref[row, k] for k in range(8)]
        sums = contractions(
            hat, wide_ref[row, 3], [wide_ref[row, k] for k in range(3)],
            (values[:3], values[3], values[4:]), slopes,
        )
        for k in range(6):
            sum_ref[k] = sum_ref[k] + sums[k]
        return carry

    lax.fori_loop(0, ROWS, test_row, 0)

    edges = jnp.zeros((TILE, LANES), F32)
    for k in range(3):
        packed = []
        for main, side in ((sum_ref[2 * k], corner_totals[2 * k]), (sum_ref[2 * k + 1], corner_totals[2 * k + 1])):
            main = jnp.where(lane < 2, shift_x(side, -19), main)
            main = jnp.where(lane >= LANES - 2, shift_x(side, 126 - 83), main)
            packed.append((main + shift_s(main, 1), side + shift_s(side, 1), main, side))
        top_main = shift_s(packed[0][0], -1) * (1.0 / 512.0)
        top_side = shift_s(packed[0][1], -1) * (1.0 / 512.0)
        totals_ref[pl.ds(k * TILE, TILE), :] = jnp.where(even, top_main, packed[1][0] * (1.0 / 1024.0))
        side = jnp.where(even, top_side, packed[1][1] * (1.0 / 1024.0))
        edges = jnp.where(lane == 2 * k, shift_x(side, 2 * k - 18), edges)
        edges = jnp.where(lane == 2 * k + 1, shift_x(side, 2 * k + 1 - 85), edges)
    totals_ref[pl.ds(3 * TILE, TILE), :] = edges


def term_kernel(tile_ref, extra_ref, corner_ref, state_ref, terms_ref):
    lane = lanes()
    bottom, top = level_edges()

    def term_row(zz, carry):
        row = zz + 1

        def terms(place, d):
            needed = list(range(STRESS, STRESS + 5)) + [HEAT_SLOPE + d]
            needed += [MASS_SLOPE + 3 * s + d for s in range(4)]
            tiles = [tile_ref[place, k] if k in needed else None for k in range(FILTERED)]
            vibration = [extra_ref[place, k] if k == d else None for k in range(3)]
            speed = [state_ref[place + 1, SPEED + k] for k in range(3)]
            return subgrid_terms(tiles, vibration, extra_ref[place, 3], speed, d)

        along_x, along_y = terms(row, 0), terms(row, 1)
        before, after = terms(row - 1, 2), terms(row + 1, 2)
        for n in range(TERMS):
            side = corner_ref[n]
            right = pltpu.roll(side, 42 - SPAN * zz, 1)
            left = pltpu.roll(side, LANES - 18 - SPAN * zz, 1)
            terms_ref[zz, n, 0] = jnp.where(lane == LANES - 1, right, shift_x(along_x[n], -1))
            terms_ref[zz, n, 1] = jnp.where(lane == 0, left, shift_x(along_x[n], 1))
            terms_ref[zz, n, 2] = after[n] - before[n]
            terms_ref[zz, n, 3] = jnp.where(top, along_y[n], shift_s(along_y[n], -2))
            terms_ref[zz, n, 4] = jnp.where(bottom, -along_y[n], shift_s(along_y[n], 2))
        return carry

    lax.fori_loop(0, ROWS, term_row, 0)


def final_kernel(*refs, parts):
    part_refs = refs[:parts]
    base_ref, terms_ref, out_ref, coefficient_ref, scratch = refs[parts:]
    lane = lanes()
    even = is_even()
    bottom, top = level_edges()
    totals = [
        (tile_of(part_refs[0], k) + tile_of(part_refs[1], k))
        + (tile_of(part_refs[2], k) + tile_of(part_refs[3], k))
        for k in range(4)
    ]
    ratios = []
    for total in totals:
        total = total * (1.0 / (TILE * lax.axis_size("gz")))
        numerator = jnp.where(even, total, shift_s(total, 1))
        denominator = jnp.where(even, shift_s(total, -1), total)
        ratios.append(numerator / (denominator + RATIO_EPSILON))
    column = lax.axis_index("gx")
    first, last = column == 0, column == lax.axis_size("gx") - 1
    here, ahead, behind, above, below = [], [], [], [], []
    for k in range(3):
        ratio = ratios[k]
        scratch[...] = ratio
        coefficient_ref[k] = scratch[pl.ds(0, 4, stride=2), :]
        before = jnp.where(first, ratio, shift_x(ratios[3], -2 * k))
        after = jnp.where(last, ratio, shift_x(ratios[3], 127 - (2 * k + 1)))
        ratio = 0.25 * ratio
        here.append(ratio)
        ahead.append(jnp.where(lane == LANES - 1, 0.25 * after, shift_x(ratio, -1)))
        behind.append(jnp.where(lane == 0, 0.25 * before, shift_x(ratio, 1)))
        above.append(2.0 * jnp.where(top, ratio, shift_s(ratio, -2)))
        below.append(2.0 * jnp.where(bottom, ratio, shift_s(ratio, 2)))

    for zz in range(ROWS):
        sums = [base_ref[pl.ds((field * ROWS + zz) * TILE, TILE), :] for field in range(NF)]
        for n in range(TERMS):
            k = TERM_MODEL[n]
            change = (
                (ahead[k] * terms_ref[zz, n, 0] - behind[k] * terms_ref[zz, n, 1])
                + here[k] * terms_ref[zz, n, 2]
                + (above[k] * terms_ref[zz, n, 3] - below[k] * terms_ref[zz, n, 4])
            )
            sums[TERM_FIELD[n]] = sums[TERM_FIELD[n]] + change
        for field in range(NF):
            out_ref[pl.ds(field * 32 + zz, TILE, stride=4), :] = sums[field]


def call(kernel, out_shapes, scratch=(), inputs=0, final=False):
    shape_of = jax.ShapeDtypeStruct if final else pltpu.VMEM
    run = pl.pallas_call(
        kernel,
        out_shape=[shape_of(shape, F32) for shape in out_shapes],
        in_specs=[VMEM] * inputs,
        out_specs=[VMEM] * len(out_shapes),
        scratch_shapes=[pltpu.VMEM(shape, F32) for shape in scratch],
        compiler_params=SMALL,
    )

    def placed(*args):
        return run(*[pltpu.with_memory_space_constraint(arg, pltpu.VMEM) for arg in args])

    return placed


def body(constituent_mass, flow_speeds, thermal_pair, blowing_indicator):
    count_x = lax.axis_size("gx")
    count_z = lax.axis_size("gz")

    def ring(axis, count, step):
        return lambda value: lax.ppermute(
            value, axis, [(i, (i + step) % count) for i in range(count)]
        )

    arrays = [
        value.reshape(-1, LANES) for value in (constituent_mass, flow_speeds, thermal_pair)
    ]
    packed = (PACK_ROWS, LANES)
    own, left, right, to_left, to_right, up, down = pl.pallas_call(
        pack_kernel,
        out_shape=[
            pltpu.VMEM(shape, F32)
            for shape in (
                (GROUPS * TILE, LANES), packed, packed, packed, packed,
                (MAIN_ROWS, LANES), (MAIN_ROWS, LANES),
            )
        ],
        in_specs=[pl.BlockSpec(memory_space=pltpu.HBM)] * 3,
        out_specs=[VMEM] * 7,
        scratch_shapes=[pltpu.VMEM(value.shape, F32) for value in arrays]
        + [pltpu.SemaphoreType.DMA((3,))],
        compiler_params=SMALL,
    )(*[pltpu.with_memory_space_constraint(value, pltpu.HBM) for value in arrays])
    got_left = ring("gx", count_x, 1)(to_right)
    got_right = ring("gx", count_x, -1)(to_left)
    up, down, edge = call(
        edge_kernel,
        [(MESSAGE_ROWS, LANES), (MESSAGE_ROWS, LANES), (2 * PACK_ROWS, LANES)],
        inputs=6,
    )(got_left, got_right, left, right, up, down)
    below = ring("gz", count_z, 1)(up)
    above = ring("gz", count_z, -1)(down)

    (part,) = call(
        stream_kernel,
        [(GROUPS * TILE, LANES)],
        scratch=[(NF * TILE, LANES), (4 * TILE, LANES)],
        inputs=3,
    )(own, edge, blowing_indicator)
    below, above, part = lax.optimization_barrier((below, above, part))

    totals, *kept = call(
        model_kernel,
        [
            (4 * TILE, LANES),
            (GRID_ROWS, FILTERED, TILE, LANES),
            (GRID_ROWS, 4, TILE, LANES),
            (TERMS, TILE, LANES),
            (STATE_ROWS, STATE_COUNT, TILE, LANES),
        ],
        scratch=[
            (SLOPED, TILE, LANES),
            (GRID_ROWS, 4, TILE, LANES),
            (GRID_ROWS, 8, TILE, LANES),
            (6, TILE, LANES),
        ],
        inputs=4,
    )(own, edge, below, above)

    (terms,) = call(term_kernel, [(ROWS, TERMS, 5, TILE, LANES)], inputs=4)(*kept)
    (base,) = call(
        span_kernel,
        [(GROUPS * TILE, LANES)],
        scratch=[
            (SPAN_TILES, NF, TILE, LANES), (SPAN_TILES, NF, TILE, LANES), (SPAN_TILES, TILE, LANES)
        ],
        inputs=4,
    )(own, below, above, part)

    def crossed(value, mask):
        return lax.ppermute(value, "gz", [(i, i ^ mask) for i in range(count_z)])

    totals = totals + crossed(totals, 1)
    reach = 2
    while count_z > 4 * reach:
        a, b, c = (crossed(totals, k * reach) for k in (1, 2, 3))
        totals = (totals + a) + (b + c)
        reach *= 4
    parts = [totals] + [
        crossed(totals, k * reach) if k * reach < count_z else jnp.zeros_like(totals)
        for k in (1, 2, 3)
    ]

    def final(*refs):
        final_kernel(*refs, parts=4)

    tendency, coefficients = call(
        final,
        [(NF * 32, LANES), (3, 4, LANES)],
        scratch=[(TILE, LANES)],
        inputs=6,
        final=True,
    )(*parts, base, terms)
    return tendency.reshape(NF, 4, TILE, LANES), coefficients


def solution(mesh):
    placed = (
        P(None, None, "gz", "gx"),
        P(None, None, "gz", "gx"),
        P(None, None, "gz", "gx"),
        P("gz", "gx"),
    )
    return jax.shard_map(
        body,
        mesh=mesh,
        in_specs=placed,
        out_specs=(P(None, None, "gz", "gx"), P(None, None, "gx")),
        check_vma=False,
    )
```

```python
import jax
import jax.numpy as jnp
from jax import lax
from jax.experimental import pallas as pl
from jax.experimental.pallas import tpu as pltpu
from jax.sharding import PartitionSpec as P


NSP = 5
NF = 10
ROWS = 4
TILE = 8
LANES = 128
HALO = 3
SPAN = 8
LAST = LANES - 5
GROUPS = NF * ROWS
PAIRS = NF // 2
PACKS = 3
PACK_ROWS = PACKS * TILE
MAIN_ROWS = PAIRS * HALO * TILE
MESSAGE_ROWS = MAIN_ROWS + PACK_ROWS

HEAT_RATIO = 1.4
FILTER_SQUARE = 0.5 ** (2.0 / 3.0)
TEST_SQUARE = 2.0 ** (2.0 / 3.0)
FORMATION = (0.0, 0.0, 0.1, 0.5, 0.25)
BLOWING = 0.3
SMOOTH_FLOOR = 0.01
RATIO_EPSILON = 1e-06

VMEM = pl.BlockSpec(memory_space=pltpu.VMEM)
F32 = jnp.float32
SMALL = pltpu.CompilerParams(vmem_limit_bytes=8 << 20)


def lanes():
    return lax.broadcasted_iota(jnp.int32, (TILE, LANES), 1)


def sublanes():
    return lax.broadcasted_iota(jnp.int32, (TILE, LANES), 0)


def shift_x(tile, step):
    if isinstance(step, int):
        step = step % LANES
        if step == 0:
            return tile
    return pltpu.roll(tile, step, 1)


def shift_s(tile, step):
    return pltpu.roll(tile, step % TILE, 0)


def is_even():
    return (sublanes() & 1) == 0


def level_edges():
    level = sublanes() >> 1
    return level == 0, level == 3


def slot_of(index):
    start = index * TILE
    return pl.ds(start if isinstance(index, int) else pl.multiple_of(start, TILE), TILE)


def tile_of(ref, index):
    return ref[slot_of(index), :]


def is_first_of_pair(axis):
    return (lax.axis_index(axis) & 1) == 0


def halo_tile(far_ref, near_ref, below, index):
    first, second = (far_ref, near_ref) if below else (near_ref, far_ref)
    return jnp.where(is_first_of_pair("gz"), tile_of(first, index), tile_of(second, index))


def pack_kernel(
    mass_hbm, speed_hbm, heat_hbm, blow_hbm, own_ref, left_ref, right_ref, far_ref, near_ref,
    blow_rows, given_ref, blow_ref, arrived
):
    start, copies = 0, []
    for k, source in enumerate((mass_hbm, speed_hbm, heat_hbm)):
        target = given_ref.at[pl.ds(start, source.shape[0])]
        copies.append(pltpu.make_async_copy(source, target, arrived.at[k]))
        start += source.shape[0]
    copies.append(pltpu.make_async_copy(blow_hbm, blow_ref, arrived.at[3]))
    for copy in copies:
        copy.start()
    for copy in copies:
        copy.wait()
    lane = lanes()
    even = is_even()
    first_core = is_first_of_pair("gz")

    def post(index, up, down):
        far_ref[slot_of(index), :] = jnp.where(first_core, down, up)
        near_ref[slot_of(index), :] = jnp.where(first_core, up, down)

    tiles = {}
    left = right = jnp.zeros((TILE, LANES), F32)
    for field in range(NF):
        for zz in range(ROWS):
            tile = given_ref[pl.ds(field * 32 + zz, TILE, stride=4), :]
            tiles[field, zz] = tile
            own_ref[slot_of(field * ROWS + zz), :] = tile
            start = 32 * (field % 4) + SPAN * zz
            reached = lane >= start
            left = jnp.where(reached, shift_x(tile, start + HALO), left)
            right = jnp.where(reached, shift_x(tile, start - LAST), right)
        if field % 4 == 3 or field == NF - 1:
            k = field // 4
            left_ref[slot_of(k), :] = left
            right_ref[slot_of(k), :] = right
            post(
                MAIN_ROWS // TILE + k,
                jnp.where(even, shift_s(left, -1), right),
                jnp.where(even, left, shift_s(right, 1)),
            )
        if field % 2:
            for k in range(HALO):
                post(
                    field // 2 * HALO + k,
                    jnp.where(even, shift_s(tiles[field - 1, k + 1], -1), tiles[field, k + 1]),
                    jnp.where(even, tiles[field, k], shift_s(tiles[field - 1, k], 1)),
                )
    for level in range(4):
        blow_rows[pl.ds(level * TILE, TILE), :] = blow_ref[...].astype(F32)


def gather_rows(own_ref, far_ref, near_ref, raw_ref):
    even = is_even()
    for field in range(NF):
        pair, second = divmod(field, 2)
        own = [tile_of(own_ref, field * ROWS + zz) for zz in range(ROWS)]
        for zz in range(ROWS):
            raw_ref[zz + HALO, field] = own[zz]
        for k in range(HALO):
            low = halo_tile(far_ref, near_ref, True, pair * HALO + k)
            high = halo_tile(far_ref, near_ref, False, pair * HALO + k)
            if second:
                low, high = shift_s(low, -1), shift_s(high, 1)
            raw_ref[k, field] = jnp.where(even, low, shift_s(own[k + 1], 1))
            raw_ref[k + HALO + ROWS, field] = jnp.where(even, shift_s(own[k], -1), high)


def edge_packs(left_ref, right_ref, far_ref, near_ref, k):
    even = is_even()
    left, right = tile_of(left_ref, k), tile_of(right_ref, k)
    low, high = (halo_tile(far_ref, near_ref, below, MAIN_ROWS // TILE + k) for below in (True, False))
    return (
        (
            jnp.where(even, low, shift_s(left, 1)),
            left,
            jnp.where(even, shift_s(left, -1), shift_s(high, 1)),
        ),
        (
            jnp.where(even, shift_s(low, -1), shift_s(right, 1)),
            right,
            jnp.where(even, shift_s(right, -1), high),
        ),
    )


def corner_pack_kernel(left_ref, right_ref, far_ref, near_ref, corner_ref, one_ref, other_ref):
    lane = lanes()
    even_column = is_first_of_pair("gx")
    corners = []
    for k in range(PACKS):
        packs = edge_packs(left_ref, right_ref, far_ref, near_ref, k)
        for j in range(min(4, NF - 4 * k)):
            start = 32 * j
            tile = None
            for side in range(2):
                for block, (bound, move) in enumerate(((0, -16), (16, 16), (48, 48))):
                    moved = shift_x(packs[side][block], 64 * side + move - start)
                    tile = (
                        moved if tile is None
                        else jnp.where(lane >= 64 * side + bound, moved, tile)
                    )
            corner_ref[4 * k + j] = tile
            corners.append(tile)
    for pair in range(PAIRS):
        first, second = corners[2 * pair], corners[2 * pair + 1]
        to_left = jnp.where(lane >= 64, shift_x(first, 66), shift_x(second, 2))
        to_right = jnp.where(lane < 64, shift_x(first, -66), shift_x(second, -2))
        one_ref[slot_of(pair), :] = jnp.where(even_column, to_right, to_left)
        other_ref[slot_of(pair), :] = jnp.where(even_column, to_left, to_right)


def state_of(fields):
    mass, motion = fields[:NSP], fields[NSP : NSP + 3]
    thermal, vibration = fields[NSP + 3], fields[NSP + 4]
    density = (mass[0] + mass[1]) + (mass[2] + mass[3]) + mass[4]
    formed = FORMATION[2] * mass[2] + FORMATION[3] * mass[3] + FORMATION[4] * mass[4]
    motion_square = motion[0] * motion[0] + motion[1] * motion[1] + motion[2] * motion[2]
    energy = density * (2.5 * thermal + vibration + 0.5 * motion_square) + formed
    conserved = (
        list(mass) + [density * speed for speed in motion] + [energy, density * vibration]
    )
    return density, density * thermal, jnp.sqrt(HEAT_RATIO * thermal), conserved


def flux_of(conserved, pressure, speed, component):
    flux = [value * speed for value in conserved]
    flux[NSP + component] = flux[NSP + component] + pressure
    flux[NSP + 3] = flux[NSP + 3] + pressure * speed
    return flux


def correction(d0, d1, d2, d3):
    floor = 4.0 * SMOOTH_FLOOR * 12.0 / 13.0
    share = 3.0 / 13.0
    e0, e1, e2 = d1 - d0, d2 - d1, d3 - d2
    g0, g1, g2 = e0 + (d1 + d1), d1 + d2, e2 - (d2 + d2)
    b0 = (e0 * e0 + floor) + share * (g0 * g0)
    b1 = (e1 * e1 + floor) + share * (g1 * g1)
    b2 = (e2 * e2 + floor) + share * (g2 * g2)
    p0, p1, p2 = b1 * b2, b0 * b2, b0 * b1
    w0 = p0 * p0
    w1 = 6.0 * (p1 * p1)
    w2 = 3.0 * (p2 * p2)
    r0 = 5.0 * d1 - (d0 + d0)
    r1 = d1 + (d2 + d2)
    r2 = 4.0 * d2 - d3
    return (w0 * r0 + w1 * r1 + w2 * r2) / (w0 + w1 + w2)


def face_flux(here, slopes, jumps, signal):
    waves = [signal * jump for jump in jumps]
    plus = [slopes[k] + waves[k] for k in range(4)]
    minus = [waves[k] - slopes[k] for k in range(1, 5)]
    gain = correction(*plus)
    loss = correction(minus[3], minus[2], minus[1], minus[0])
    return here + 0.5 * (slopes[2] - waves[2]) + (gain + loss) * (1.0 / 12.0)


def faces_along_x(flux, conserved, signal):
    slope = shift_x(flux, -1) - flux
    jump = shift_x(conserved, -1) - conserved
    slopes = [shift_x(slope, -k) for k in range(-2, 3)]
    jumps = [shift_x(jump, -k) for k in range(-2, 3)]
    return face_flux(flux, slopes, jumps, signal)


def stream_kernel(own_ref, blow_rows, face_ref, part_ref):
    bottom, top = level_edges()

    def row(zz, carry):
        fields = [tile_of(own_ref, field * ROWS + zz) for field in range(NF)]
        density, pressure, sound, conserved = state_of(fields)
        speed = fields[NSP]
        flux = flux_of(conserved, pressure, speed, 0)
        signal = jnp.abs(speed) + sound
        signal = jnp.maximum(signal, shift_x(signal, -1))

        normal_speed = fields[NSP + 1]
        normal_flux = flux_of(conserved, pressure, normal_speed, 1)
        normal_signal = jnp.abs(normal_speed) + sound
        normal_signal = 0.5 * jnp.maximum(normal_signal, shift_s(normal_signal, -2))
        blown = BLOWING * blow_rows[pl.ds(zz, TILE, stride=4), :]
        lift = blown / density
        enthalpy = 3.5 * fields[NSP + 3] + fields[NSP + 4] + 0.5 * lift * lift
        wall = [lift * fields[s] for s in range(NSP)]
        formed = FORMATION[2] * wall[2] + FORMATION[3] * wall[3] + FORMATION[4] * wall[4]
        zero = jnp.zeros((TILE, LANES), F32)
        wall = wall + [
            zero, blown * lift + pressure, zero, blown * enthalpy + formed, blown * fields[NSP + 4]
        ]
        relaxation = 2.0 * density * (fields[NSP + 3] - fields[NSP + 4])
        for field in range(NF):
            value, normal = conserved[field], normal_flux[field]
            slot = slot_of(field * ROWS + zz)
            face_ref[slot, :] = faces_along_x(flux[field], value, signal)
            above = shift_s(value, -2)
            level_face = 0.5 * (normal + shift_s(normal, -2)) - normal_signal * (above - value)
            level_face = jnp.where(top, normal, level_face)
            change = 2.0 * (jnp.where(bottom, wall[field], shift_s(level_face, 2)) - level_face)
            part_ref[slot, :] = change + relaxation if field == NF - 1 else change
        return carry

    lax.fori_loop(0, ROWS, row, 0)


def ends_kernel(corner_ref, face_ref, part_ref, out_ref):
    lane = lanes()
    fields = [corner_ref[field] for field in range(NF)]
    density, pressure, sound, conserved = state_of(fields)
    flux = flux_of(conserved, pressure, fields[NSP], 0)
    signal = jnp.abs(fields[NSP]) + sound
    signal = jnp.maximum(signal, shift_x(signal, -1))
    for field in range(NF):
        end_face = faces_along_x(flux[field], conserved[field], signal)
        for zz in range(ROWS):
            left = shift_x(end_face, 109 - SPAN * zz)
            right = shift_x(end_face, 43 - SPAN * zz)
            slot = slot_of(field * ROWS + zz)
            face = jnp.where(
                lane < 2, left, jnp.where(lane >= LANES - 3, right, face_ref[slot, :])
            )
            before = shift_x(jnp.where(lane == LANES - 1, left, face), 1)
            out_ref[slot, :] = part_ref[slot, :] + (before - face)


SPAN_TILES = ROWS + 2 * HALO


def span_kernel(raw_ref, part_ref, out_ref, value_ref, flux_ref, signal_ref):
    for place in range(SPAN_TILES):
        fields = [raw_ref[place, field] for field in range(NF)]
        _, pressure, sound, conserved = state_of(fields)
        speed = fields[NSP + 2]
        flux = flux_of(conserved, pressure, speed, 2)
        signal_ref[place] = jnp.abs(speed) + sound
        for field in range(NF):
            value_ref[place, field] = conserved[field]
            flux_ref[place, field] = flux[field]

    def faces_of(place):
        signal = jnp.maximum(signal_ref[place], signal_ref[place + 1])
        faces = []
        for field in range(NF):
            flux = [flux_ref[place + k, field] for k in range(-2, 4)]
            value = [value_ref[place + k, field] for k in range(-2, 4)]
            slopes = [flux[k + 1] - flux[k] for k in range(5)]
            jumps = [value[k + 1] - value[k] for k in range(5)]
            faces.append(face_flux(flux[2], slopes, jumps, signal))
        return tuple(faces)

    def row(zz, before):
        faces = faces_of(zz + HALO)
        for field in range(NF):
            slot = slot_of(field * ROWS + zz)
            out_ref[slot, :] = part_ref[slot, :] + (before[field] - faces[field])
        return faces

    lax.fori_loop(0, ROWS, row, faces_of(HALO - 1))


MASS, MOMENTUM, HEAT = 0, 5, 8
SPEED, THERMAL, VIBRATION, FRACTION, DENSITY = 9, 12, 13, 14, 19
STATE_COUNT = 20
SLOPED = 10
STATE_ROWS = 8
GRID_ROWS = 6
PAIR_INDEX = ((0, 0), (1, 1), (0, 1), (0, 2), (1, 2), (2, 2))

PRODUCT, STRESS, HEAT_FLUX, HEAT_SLOPE, MASS_FLUX, MASS_SLOPE = 0, 6, 11, 14, 17, 29
LAST_STRESS = 41
FILTERED = 42
SIDE_SLOPE = FILTERED
TILES = FILTERED + 3

TERMS = 12
TERM_FIELD = (0, 1, 2, 3, 4, 5, 6, 7, 8, 8, 8, 9)
TERM_MODEL = (2, 2, 2, 2, 2, 0, 0, 0, 0, 1, 2, 1)


def model_state(fields):
    mass, motion = fields[:NSP], fields[NSP : NSP + 3]
    thermal, vibration = fields[NSP + 3], fields[NSP + 4]
    density = (mass[0] + mass[1]) + (mass[2] + mass[3]) + mass[4]
    inverse = 1.0 / density
    fraction = [m * inverse for m in mass]
    return (
        list(mass)
        + [density * speed for speed in motion]
        + [density * thermal]
        + list(motion)
        + [thermal, vibration]
        + fraction
        + [density]
    )


def level_slope(value, scale):
    bottom, top = level_edges()
    above = jnp.where(top, value, shift_s(value, -2))
    below = jnp.where(bottom, value, shift_s(value, 2))
    return scale * (above - below)


def strain(slopes):
    diagonal = [2.0 * slopes[k][k] for k in range(3)]
    third = (diagonal[0] + diagonal[1] + diagonal[2]) * (1.0 / 3.0)
    first, second = diagonal[0] - third, diagonal[1] - third
    mixed = [slopes[0][1] + slopes[1][0], slopes[0][2] + slopes[2][0], slopes[1][2] + slopes[2][1]]
    last = diagonal[2] - third
    square = (
        first * first + second * second + last * last
        + 2.0 * (mixed[0] * mixed[0] + mixed[1] * mixed[1] + mixed[2] * mixed[2])
    )
    magnitude = jnp.sqrt(0.125 * square + 1e-06)
    return [first, second] + mixed + [last], magnitude


def grid_terms(here, slopes):
    deviator, magnitude = strain(slopes[:3])
    eddy = FILTER_SQUARE * here(DENSITY) * magnitude
    speed = [here(SPEED + k) for k in range(3)]
    momentum = [here(MOMENTUM + k) for k in range(3)]
    thermal = here(THERMAL)
    stress = [eddy * part for part in deviator]
    tiles = [momentum[i] * speed[j] for i, j in PAIR_INDEX]
    tiles += stress[:5]
    tiles += [m * thermal for m in momentum]
    tiles += [eddy * slopes[3][d] for d in range(3)]
    tiles += [here(MASS + s) * speed[d] for s in range(4) for d in range(3)]
    tiles += [eddy * slopes[5 + s][d] for s in range(4) for d in range(3)]
    tiles.append(stress[5])
    return tiles + [eddy * slopes[4][d] for d in range(3)]


def subgrid_terms(tile, speed, d):
    places = (STRESS, STRESS + 1, STRESS + 2, STRESS + 3, STRESS + 4, LAST_STRESS)
    full = ((0, 2, 3), (2, 1, 4), (3, 4, 5))
    tau = [tile(places[full[i][d]]) for i in range(3)]
    species = [tile(MASS_SLOPE + 3 * s + d) for s in range(4)]
    species.append(-((species[0] + species[1]) + (species[2] + species[3])))
    work = speed[0] * tau[0] + speed[1] * tau[1] + speed[2] * tau[2]
    vibration = tile(SIDE_SLOPE + d)
    heat = 3.5 * tile(HEAT_SLOPE + d) + vibration
    formed = FORMATION[2] * species[2] + FORMATION[3] * species[3] + FORMATION[4] * species[4]
    return species + tau + [work, heat, formed, vibration]


def favre(hat):
    density = (hat[0] + hat[1]) + (hat[2] + hat[3]) + hat[4]
    inverse = 1.0 / density
    return density, [hat[5 + k] * inverse for k in range(3)], hat[8] * inverse, [
        hat[s] * inverse for s in range(4)
    ]


def contractions(hat, density, momentum, favre_here, slopes):
    speed, thermal, fraction = favre_here
    deviator, magnitude = strain(slopes[:3])
    eddy = TEST_SQUARE * density * magnitude
    stress = [hat(STRESS + n) for n in range(5)] + [hat(LAST_STRESS)]
    sums = []
    top = bottom = None

    def add(total, value):
        return value if total is None else total + value

    off_top = off_bottom = None
    for n, (i, j) in enumerate(PAIR_INDEX):
        resolved = hat(PRODUCT + n) - momentum[i] * speed[j]
        model = stress[n] - eddy * deviator[n]
        if i == j:
            top, bottom = add(top, resolved * model), add(bottom, model * model)
        else:
            off_top, off_bottom = add(off_top, resolved * model), add(off_bottom, model * model)
    sums += [top + (off_top + off_top), bottom + (off_bottom + off_bottom)]
    top = bottom = None
    for d in range(3):
        resolved = hat(HEAT_FLUX + d) - momentum[d] * thermal
        model = hat(HEAT_SLOPE + d) - eddy * slopes[3][d]
        top, bottom = add(top, resolved * model), add(bottom, model * model)
    sums += [top, bottom]
    top = bottom = None
    for d in range(3):
        last_resolved = last_model = None
        for s in range(4):
            resolved = hat(MASS_FLUX + 3 * s + d) - momentum[d] * fraction[s]
            model = hat(MASS_SLOPE + 3 * s + d) - eddy * slopes[4 + s][d]
            last_resolved, last_model = add(last_resolved, resolved), add(last_model, model)
            top, bottom = add(top, resolved * model), add(bottom, model * model)
        top, bottom = top + last_resolved * last_model, bottom + last_model * last_model
    return sums + [top, bottom]


def filter_x(tile):
    pair = tile + shift_x(tile, -1)
    return pair + shift_x(pair, 1)


def slope_scale():
    bottom, top = level_edges()
    return jnp.where(bottom | top, 4.0, 2.0)


def model_kernel(
    own_ref, far_ref, near_ref, corner_own_ref,
    sum_ref, clamped_ref, tile_ref, state_ref, raw_ref,
    wide_ref, favre_ref,
):
    scale = slope_scale()
    gather_rows(own_ref, far_ref, near_ref, raw_ref)
    for row in range(STATE_ROWS):
        states = model_state([raw_ref[row + 1, field] for field in range(NF)])
        for k in range(STATE_COUNT):
            state_ref[row, k] = states[k]

    def grid_row(row, carry):
        def here(k):
            return state_ref[row + 1, k]

        slopes = []
        for k in range(SLOPED - 1):
            value = here(SPEED + k)
            along_x = shift_x(value, -1) - shift_x(value, 1)
            along_z = state_ref[row + 2, SPEED + k] - state_ref[row, SPEED + k]
            slopes.append((along_x, level_slope(value, scale), along_z))
        for k, tile in enumerate(grid_terms(here, slopes)):
            tile_ref[row, k] = tile
        hat = []
        for k in range(SPEED):
            total = (state_ref[row, k] + state_ref[row + 2, k]) + 2.0 * here(k)
            hat.append(filter_x(total))
        density, speed, thermal, fraction = favre(hat)
        for k, value in enumerate(speed + [thermal] + fraction):
            favre_ref[row, k] = value
        for k in range(3):
            wide_ref[row, k] = hat[MOMENTUM + k]
        wide_ref[row, 3] = density
        return carry

    lax.fori_loop(0, GRID_ROWS, grid_row, 0)
    for k in range(6):
        sum_ref[k] = jnp.zeros((TILE, LANES), F32)

    def test_row(zz, carry):
        row = zz + 1

        def hat(k):
            total = (tile_ref[row - 1, k] + tile_ref[row + 1, k]) + 2.0 * tile_ref[row, k]
            return filter_x(total)

        slopes = []
        for k in range(8):
            value = favre_ref[row, k]
            along_x = shift_x(value, -1) - shift_x(value, 1)
            along_z = favre_ref[row + 1, k] - favre_ref[row - 1, k]
            slopes.append((along_x, level_slope(value, scale), along_z))
        values = [favre_ref[row, k] for k in range(8)]
        sums = contractions(
            hat, wide_ref[row, 3], [wide_ref[row, k] for k in range(3)],
            (values[:3], values[3], values[4:]), slopes,
        )
        for k in range(6):
            sum_ref[k] = sum_ref[k] + sums[k]
        return carry

    lax.fori_loop(0, ROWS, test_row, 0)

    on_left = lanes() < 64
    place = lanes() & (SPAN - 1)
    place = jnp.where(on_left, place, SPAN - 1 - place)
    for field in range(NF):
        tile = clamped = corner_own_ref[field]
        for c in range(HALO):
            copied = jnp.where(on_left, shift_x(tile, c - HALO), shift_x(tile, HALO - c))
            clamped = jnp.where(place == c, copied, clamped)
        clamped_ref[field] = clamped


def corner_kernel(
    clamped_ref, got_one_ref, got_other_ref, sum_ref,
    totals_ref, corner_ref, tile_ref, speed_ref
):
    lane = lanes()
    even = is_even()
    scale = slope_scale()
    even_column = is_first_of_pair("gx")
    column = lax.axis_index("gx")
    first, last = column == 0, column == lax.axis_size("gx") - 1
    place = lane & (SPAN - 1)
    on_left = lane < 64
    low, high = jnp.where(first, 0, HALO), jnp.where(last, SPAN, SPAN - HALO)
    halo = (on_left & (place < low)) | (jnp.logical_not(on_left) & (place >= high))
    fields = []
    for field in range(NF):
        pair, second = divmod(field, 2)
        one, other = tile_of(got_one_ref, pair), tile_of(got_other_ref, pair)
        from_left = jnp.where(even_column, other, one)
        from_right = jnp.where(even_column, one, other)
        if second:
            got = shift_x(jnp.where(on_left, from_right, from_left), 64)
        else:
            got = jnp.where(on_left, from_left, from_right)
        fields.append(jnp.where(halo, got, clamped_ref[field]))
        corner_ref[field] = fields[field]
    state = model_state(fields)

    def slopes_of(value):
        along_x = shift_x(value, -1) - shift_x(value, 1)
        along_z = shift_x(value, -SPAN) - shift_x(value, SPAN)
        return along_x, level_slope(value, scale), along_z

    def filtered(value):
        pair = value + shift_x(value, -SPAN)
        return filter_x(pair + shift_x(pair, SPAN))

    tiles = grid_terms(lambda k: state[k], [slopes_of(state[SPEED + k]) for k in range(SLOPED - 1)])
    for k in range(STRESS, TILES):
        tile_ref[k] = tiles[k]
    for k in range(3):
        speed_ref[k] = state[SPEED + k]
    wide = [filtered(state[k]) for k in range(SPEED)]
    density, speed, thermal, fraction = favre(wide)
    sums = contractions(
        lambda k: filtered(tiles[k]), density, wide[MOMENTUM : MOMENTUM + 3],
        (speed, thermal, fraction), [slopes_of(value) for value in speed + [thermal] + fraction],
    )
    main_totals, corner_totals = [sum_ref[k] for k in range(6)], []
    for value in sums:
        value = value + shift_x(value, -SPAN)
        corner_totals.append(value + shift_x(value, -2 * SPAN))
    edges = jnp.zeros((TILE, LANES), F32)
    for k in range(3):
        packed = []
        for main, side in zip(main_totals[2 * k : 2 * k + 2], corner_totals[2 * k : 2 * k + 2]):
            main = jnp.where(lane < 2, shift_x(side, -19), main)
            main = jnp.where(lane >= LANES - 2, shift_x(side, 126 - 83), main)
            packed.append((main + shift_s(main, 1), side + shift_s(side, 1), main, side))
        top_main = shift_s(packed[0][0], -1) * (1.0 / 512.0)
        top_side = shift_s(packed[0][1], -1) * (1.0 / 512.0)
        totals_ref[pl.ds(k * TILE, TILE), :] = jnp.where(even, top_main, packed[1][0] * (1.0 / 1024.0))
        side = jnp.where(even, top_side, packed[1][1] * (1.0 / 1024.0))
        edges = jnp.where(lane == 2 * k, shift_x(side, 2 * k - 18), edges)
        edges = jnp.where(lane == 2 * k + 1, shift_x(side, 2 * k + 1 - 85), edges)
    totals_ref[pl.ds(3 * TILE, TILE), :] = edges


def term_kernel(tile_ref, state_ref, corner_ref, corner_speed_ref, terms_ref):
    lane = lanes()
    bottom, top = level_edges()

    def terms(place, d):
        speed = [state_ref[place + 1, SPEED + k] for k in range(3)]
        return subgrid_terms(lambda k: tile_ref[place, k], speed, d)

    corner_speed = [corner_speed_ref[k] for k in range(3)]
    corner = [subgrid_terms(lambda k: corner_ref[k], corner_speed, d) for d in range(3)]
    corner[2] = [shift_x(value, -SPAN) - shift_x(value, SPAN) for value in corner[2]]

    def patched(value, side, zz):
        value = jnp.where(lane == 0, shift_x(side, -19 - SPAN * zz), value)
        return jnp.where(lane == LANES - 1, shift_x(side, 43 - SPAN * zz), value)

    for zz in range(ROWS):
        row = zz + 1
        along_x, along_y = terms(row, 0), terms(row, 1)
        before, after = terms(row - 1, 2), terms(row + 1, 2)
        for n in range(TERMS):
            right = shift_x(corner[0][n], 42 - SPAN * zz)
            left = shift_x(corner[0][n], -18 - SPAN * zz)
            terms_ref[zz, n, 0] = jnp.where(lane >= LANES - 2, right, shift_x(along_x[n], -1))
            terms_ref[zz, n, 1] = jnp.where(lane < 2, left, shift_x(along_x[n], 1))
            terms_ref[zz, n, 2] = patched(after[n] - before[n], corner[2][n], zz)
            along = patched(along_y[n], corner[1][n], zz)
            terms_ref[zz, n, 3] = jnp.where(top, along, shift_s(along, -2))
            terms_ref[zz, n, 4] = jnp.where(bottom, -along, shift_s(along, 2))


def final_kernel(*refs, parts):
    part_refs = refs[:parts]
    base_ref, terms_ref, out_ref, coefficient_ref, scratch = refs[parts:]
    lane = lanes()
    even = is_even()
    bottom, top = level_edges()
    totals = [
        (tile_of(part_refs[0], k) + tile_of(part_refs[1], k))
        + (tile_of(part_refs[2], k) + tile_of(part_refs[3], k))
        for k in range(4)
    ]
    ratios = []
    for total in totals:
        total = total * (1.0 / (TILE * lax.axis_size("gz")))
        numerator = jnp.where(even, total, shift_s(total, 1))
        denominator = jnp.where(even, shift_s(total, -1), total)
        ratios.append(numerator / (denominator + RATIO_EPSILON))
    column = lax.axis_index("gx")
    first, last = column == 0, column == lax.axis_size("gx") - 1
    here, ahead, behind, above, below = [], [], [], [], []
    for k in range(3):
        ratio = ratios[k]
        scratch[...] = ratio
        coefficient_ref[k] = scratch[pl.ds(0, 4, stride=2), :]
        before = jnp.where(first, ratio, shift_x(ratios[3], -2 * k))
        after = jnp.where(last, ratio, shift_x(ratios[3], 127 - (2 * k + 1)))
        ratio = 0.25 * ratio
        here.append(ratio)
        ahead.append(jnp.where(lane == LANES - 1, 0.25 * after, shift_x(ratio, -1)))
        behind.append(jnp.where(lane == 0, 0.25 * before, shift_x(ratio, 1)))
        above.append(2.0 * jnp.where(top, ratio, shift_s(ratio, -2)))
        below.append(2.0 * jnp.where(bottom, ratio, shift_s(ratio, 2)))

    def row(zz, carry):
        sums = [tile_of(base_ref, field * ROWS + zz) for field in range(NF)]
        for n in range(TERMS):
            k = TERM_MODEL[n]
            change = (
                (ahead[k] * terms_ref[zz, n, 0] - behind[k] * terms_ref[zz, n, 1])
                + here[k] * terms_ref[zz, n, 2]
                + (above[k] * terms_ref[zz, n, 3] - below[k] * terms_ref[zz, n, 4])
            )
            sums[TERM_FIELD[n]] = sums[TERM_FIELD[n]] + change
        for field in range(NF):
            out_ref[pl.ds(field * 32 + zz, TILE, stride=4), :] = sums[field]
        return carry

    lax.fori_loop(0, ROWS, row, 0)


def call(kernel, out_shapes, scratch=(), inputs=0, final=False):
    shape_of = jax.ShapeDtypeStruct if final else pltpu.VMEM
    run = pl.pallas_call(
        kernel,
        out_shape=[shape_of(shape, F32) for shape in out_shapes],
        in_specs=[VMEM] * inputs,
        out_specs=[VMEM] * len(out_shapes),
        scratch_shapes=[pltpu.VMEM(shape, F32) for shape in scratch],
        compiler_params=SMALL,
    )

    def placed(*args):
        return run(*[pltpu.with_memory_space_constraint(arg, pltpu.VMEM) for arg in args])

    return placed


def body(constituent_mass, flow_speeds, thermal_pair, blowing_indicator):
    count_x = lax.axis_size("gx")
    count_z = lax.axis_size("gz")

    def swap(axis, count, near):
        step = [1, -1] if near else [-1, 1]
        return lambda value: lax.ppermute(
            value, axis, [(i, (i + step[i % 2]) % count) for i in range(count)]
        )

    arrays = [
        value.reshape(-1, LANES) for value in (constituent_mass, flow_speeds, thermal_pair)
    ]
    packed = (PACK_ROWS, LANES)
    rows = (GROUPS * TILE, LANES)
    fields = (NF, TILE, LANES)
    own, left, right, far, near, blown = pl.pallas_call(
        pack_kernel,
        out_shape=[
            pltpu.VMEM(shape, F32)
            for shape in (
                rows, packed, packed, (MESSAGE_ROWS, LANES), (MESSAGE_ROWS, LANES),
                (4 * TILE, LANES),
            )
        ],
        in_specs=[pl.BlockSpec(memory_space=pltpu.HBM)] * 4,
        out_specs=[VMEM] * 6,
        scratch_shapes=[
            pltpu.VMEM((NF * 4 * TILE, LANES), F32),
            pltpu.VMEM(blowing_indicator.shape, jnp.int32),
            pltpu.SemaphoreType.DMA((4,)),
        ],
        compiler_params=SMALL,
    )(*[
        pltpu.with_memory_space_constraint(value, pltpu.HBM)
        for value in arrays + [blowing_indicator]
    ])
    far = swap("gz", count_z, False)(far)
    near = swap("gz", count_z, True)(near)
    face, part = call(stream_kernel, [rows, rows], inputs=2)(own, blown)
    far, near, face, part = lax.optimization_barrier((far, near, face, part))

    corner, one, other = call(
        corner_pack_kernel,
        [fields, (PAIRS * TILE, LANES), (PAIRS * TILE, LANES)],
        inputs=4,
    )(left, right, far, near)
    got_one = swap("gx", count_x, True)(one)
    got_other = swap("gx", count_x, False)(other)
    sums, clamped, tiles, state, raw = call(
        model_kernel,
        [
            (6, TILE, LANES),
            fields,
            (GRID_ROWS, TILES, TILE, LANES),
            (STATE_ROWS, STATE_COUNT, TILE, LANES),
            (SPAN_TILES, NF, TILE, LANES),
        ],
        scratch=[(GRID_ROWS, 4, TILE, LANES), (GRID_ROWS, 8, TILE, LANES)],
        inputs=4,
    )(own, far, near, corner)
    got_one, got_other, sums = lax.optimization_barrier((got_one, got_other, sums))
    totals, corner, corner_tiles, corner_speed = call(
        corner_kernel,
        [(4 * TILE, LANES), fields, (TILES, TILE, LANES), (3, TILE, LANES)],
        inputs=4,
    )(clamped, got_one, got_other, sums)

    (terms,) = call(term_kernel, [(ROWS, TERMS, 5, TILE, LANES)], inputs=4)(
        tiles, state, corner_tiles, corner_speed
    )
    (part,) = call(ends_kernel, [rows], inputs=3)(corner, face, part)
    (base,) = call(
        span_kernel,
        [rows],
        scratch=[
            (SPAN_TILES, NF, TILE, LANES), (SPAN_TILES, NF, TILE, LANES), (SPAN_TILES, TILE, LANES),
        ],
        inputs=2,
    )(raw, part)

    def crossed(value, mask):
        return lax.ppermute(value, "gz", [(i, i ^ mask) for i in range(count_z)])

    totals = totals + crossed(totals, 1)
    reach = 2
    while count_z > 4 * reach:
        a, b, c = (crossed(totals, k * reach) for k in (1, 2, 3))
        totals = (totals + a) + (b + c)
        reach *= 4
    parts = [totals] + [
        crossed(totals, k * reach) if k * reach < count_z else jnp.zeros_like(totals)
        for k in (1, 2, 3)
    ]

    def final(*refs):
        final_kernel(*refs, parts=4)

    tendency, coefficients = call(
        final,
        [(NF * 32, LANES), (3, 4, LANES)],
        scratch=[(TILE, LANES)],
        inputs=6,
        final=True,
    )(*parts, base, terms)
    return tendency.reshape(NF, 4, TILE, LANES), coefficients


def solution(mesh):
    placed = (
        P(None, None, "gz", "gx"),
        P(None, None, "gz", "gx"),
        P(None, None, "gz", "gx"),
        P("gz", "gx"),
    )
    return jax.shard_map(
        body,
        mesh=mesh,
        in_specs=placed,
        out_specs=(P(None, None, "gz", "gx"), P(None, None, "gx")),
        check_vma=False,
    )
```

```python
import jax
import jax.numpy as jnp
from jax import lax
from jax.experimental import pallas as pl
from jax.experimental.pallas import tpu as pltpu
from jax.sharding import PartitionSpec as P


NSP = 5
NF = 10
ROWS = 4
TILE = 8
LANES = 128
HALO = 3
SPAN = 8
LAST = LANES - 5
GROUPS = NF * ROWS
PAIRS = NF // 2
PACKS = 3
PACK_ROWS = PACKS * TILE
MAIN_ROWS = PAIRS * HALO * TILE
MESSAGE_ROWS = MAIN_ROWS + PACK_ROWS

HEAT_RATIO = 1.4
FILTER_SQUARE = 0.5 ** (2.0 / 3.0)
TEST_SQUARE = 2.0 ** (2.0 / 3.0)
FORMATION = (0.0, 0.0, 0.1, 0.5, 0.25)
BLOWING = 0.3
SMOOTH_FLOOR = 0.01
RATIO_EPSILON = 1e-06

VMEM = pl.BlockSpec(memory_space=pltpu.VMEM)
F32 = jnp.float32
SMALL = pltpu.CompilerParams(vmem_limit_bytes=8 << 20)


def lanes():
    return lax.broadcasted_iota(jnp.int32, (TILE, LANES), 1)


def sublanes():
    return lax.broadcasted_iota(jnp.int32, (TILE, LANES), 0)


def shift_x(tile, step):
    if isinstance(step, int):
        step = step % LANES
        if step == 0:
            return tile
    return pltpu.roll(tile, step, 1)


def shift_s(tile, step):
    return pltpu.roll(tile, step % TILE, 0)


def is_even():
    return (sublanes() & 1) == 0


def level_edges():
    level = sublanes() >> 1
    return level == 0, level == 3


def slot_of(index):
    start = index * TILE
    return pl.ds(start if isinstance(index, int) else pl.multiple_of(start, TILE), TILE)


def tile_of(ref, index):
    return ref[slot_of(index), :]


def is_first_of_pair(axis):
    return (lax.axis_index(axis) & 1) == 0


def halo_tile(far_ref, near_ref, below, index):
    first, second = (far_ref, near_ref) if below else (near_ref, far_ref)
    return jnp.where(is_first_of_pair("gz"), tile_of(first, index), tile_of(second, index))


def pack_kernel(
    mass_hbm, speed_hbm, heat_hbm, blow_hbm, own_ref, left_ref, right_ref, far_ref, near_ref,
    blow_rows, given_ref, blow_ref, arrived
):
    start, copies = 0, []
    for k, source in enumerate((mass_hbm, speed_hbm, heat_hbm)):
        target = given_ref.at[pl.ds(start, source.shape[0])]
        copies.append(pltpu.make_async_copy(source, target, arrived.at[k]))
        start += source.shape[0]
    copies.append(pltpu.make_async_copy(blow_hbm, blow_ref, arrived.at[3]))
    for copy in copies:
        copy.start()
    for copy in copies:
        copy.wait()
    lane = lanes()
    even = is_even()
    first_core = is_first_of_pair("gz")

    def post(index, up, down):
        far_ref[slot_of(index), :] = jnp.where(first_core, down, up)
        near_ref[slot_of(index), :] = jnp.where(first_core, up, down)

    tiles = {}
    left = right = jnp.zeros((TILE, LANES), F32)
    for field in range(NF):
        for zz in range(ROWS):
            tile = given_ref[pl.ds(field * 32 + zz, TILE, stride=4), :]
            tiles[field, zz] = tile
            own_ref[slot_of(field * ROWS + zz), :] = tile
            start = 32 * (field % 4) + SPAN * zz
            reached = lane >= start
            left = jnp.where(reached, shift_x(tile, start + HALO), left)
            right = jnp.where(reached, shift_x(tile, start - LAST), right)
        if field % 4 == 3 or field == NF - 1:
            k = field // 4
            left_ref[slot_of(k), :] = left
            right_ref[slot_of(k), :] = right
            post(
                MAIN_ROWS // TILE + k,
                jnp.where(even, shift_s(left, -1), right),
                jnp.where(even, left, shift_s(right, 1)),
            )
        if field % 2:
            for k in range(HALO):
                post(
                    field // 2 * HALO + k,
                    jnp.where(even, shift_s(tiles[field - 1, k + 1], -1), tiles[field, k + 1]),
                    jnp.where(even, tiles[field, k], shift_s(tiles[field - 1, k], 1)),
                )
    for level in range(4):
        blow_rows[pl.ds(level * TILE, TILE), :] = blow_ref[...].astype(F32)


def gather_rows(own_ref, far_ref, near_ref, raw_ref):
    even = is_even()
    for field in range(NF):
        pair, second = divmod(field, 2)
        own = [tile_of(own_ref, field * ROWS + zz) for zz in range(ROWS)]
        for zz in range(ROWS):
            raw_ref[zz + HALO, field] = own[zz]
        for k in range(HALO):
            low = halo_tile(far_ref, near_ref, True, pair * HALO + k)
            high = halo_tile(far_ref, near_ref, False, pair * HALO + k)
            if second:
                low, high = shift_s(low, -1), shift_s(high, 1)
            raw_ref[k, field] = jnp.where(even, low, shift_s(own[k + 1], 1))
            raw_ref[k + HALO + ROWS, field] = jnp.where(even, shift_s(own[k], -1), high)


def edge_packs(left_ref, right_ref, far_ref, near_ref, k):
    even = is_even()
    left, right = tile_of(left_ref, k), tile_of(right_ref, k)
    low, high = (halo_tile(far_ref, near_ref, below, MAIN_ROWS // TILE + k) for below in (True, False))
    return (
        (
            jnp.where(even, low, shift_s(left, 1)),
            left,
            jnp.where(even, shift_s(left, -1), shift_s(high, 1)),
        ),
        (
            jnp.where(even, shift_s(low, -1), shift_s(right, 1)),
            right,
            jnp.where(even, shift_s(right, -1), high),
        ),
    )


def corner_pack_kernel(left_ref, right_ref, far_ref, near_ref, corner_ref, one_ref, other_ref):
    lane = lanes()
    even_column = is_first_of_pair("gx")
    corners = []
    for k in range(PACKS):
        packs = edge_packs(left_ref, right_ref, far_ref, near_ref, k)
        for j in range(min(4, NF - 4 * k)):
            start = 32 * j
            tile = None
            for side in range(2):
                for block, (bound, move) in enumerate(((0, -16), (16, 16), (48, 48))):
                    moved = shift_x(packs[side][block], 64 * side + move - start)
                    tile = (
                        moved if tile is None
                        else jnp.where(lane >= 64 * side + bound, moved, tile)
                    )
            corner_ref[4 * k + j] = tile
            corners.append(tile)
    for pair in range(PAIRS):
        first, second = corners[2 * pair], corners[2 * pair + 1]
        to_left = jnp.where(lane >= 64, shift_x(first, 66), shift_x(second, 2))
        to_right = jnp.where(lane < 64, shift_x(first, -66), shift_x(second, -2))
        one_ref[slot_of(pair), :] = jnp.where(even_column, to_right, to_left)
        other_ref[slot_of(pair), :] = jnp.where(even_column, to_left, to_right)


def state_of(fields):
    mass, motion = fields[:NSP], fields[NSP : NSP + 3]
    thermal, vibration = fields[NSP + 3], fields[NSP + 4]
    density = (mass[0] + mass[1]) + (mass[2] + mass[3]) + mass[4]
    formed = FORMATION[2] * mass[2] + FORMATION[3] * mass[3] + FORMATION[4] * mass[4]
    motion_square = motion[0] * motion[0] + motion[1] * motion[1] + motion[2] * motion[2]
    energy = density * (2.5 * thermal + vibration + 0.5 * motion_square) + formed
    conserved = (
        list(mass) + [density * speed for speed in motion] + [energy, density * vibration]
    )
    return density, density * thermal, jnp.sqrt(HEAT_RATIO * thermal), conserved


def flux_of(conserved, pressure, speed, component):
    flux = [value * speed for value in conserved]
    flux[NSP + component] = flux[NSP + component] + pressure
    flux[NSP + 3] = flux[NSP + 3] + pressure * speed
    return flux


def correction(d0, d1, d2, d3):
    floor = 4.0 * SMOOTH_FLOOR * 12.0 / 13.0
    share = 3.0 / 13.0
    e0, e1, e2 = d1 - d0, d2 - d1, d3 - d2
    g0, g1, g2 = e0 + (d1 + d1), d1 + d2, e2 - (d2 + d2)
    b0 = (e0 * e0 + floor) + share * (g0 * g0)
    b1 = (e1 * e1 + floor) + share * (g1 * g1)
    b2 = (e2 * e2 + floor) + share * (g2 * g2)
    p0, p1, p2 = b1 * b2, b0 * b2, b0 * b1
    w0 = p0 * p0
    w1 = 6.0 * (p1 * p1)
    w2 = 3.0 * (p2 * p2)
    r0 = 5.0 * d1 - (d0 + d0)
    r1 = d1 + (d2 + d2)
    r2 = 4.0 * d2 - d3
    return (w0 * r0 + w1 * r1 + w2 * r2) / (w0 + w1 + w2)


def face_flux(here, slopes, jumps, signal):
    waves = [signal * jump for jump in jumps]
    plus = [slopes[k] + waves[k] for k in range(4)]
    minus = [waves[k] - slopes[k] for k in range(1, 5)]
    gain = correction(*plus)
    loss = correction(minus[3], minus[2], minus[1], minus[0])
    return here + 0.5 * (slopes[2] - waves[2]) + (gain + loss) * (1.0 / 12.0)


def faces_along_x(flux, conserved, signal):
    slope = shift_x(flux, -1) - flux
    jump = shift_x(conserved, -1) - conserved
    slopes = [shift_x(slope, -k) for k in range(-2, 3)]
    jumps = [shift_x(jump, -k) for k in range(-2, 3)]
    return face_flux(flux, slopes, jumps, signal)


def stream_kernel(own_ref, blow_rows, face_ref, part_ref):
    bottom, top = level_edges()

    def row(zz, carry):
        fields = [tile_of(own_ref, field * ROWS + zz) for field in range(NF)]
        density, pressure, sound, conserved = state_of(fields)
        speed = fields[NSP]
        flux = flux_of(conserved, pressure, speed, 0)
        signal = jnp.abs(speed) + sound
        signal = jnp.maximum(signal, shift_x(signal, -1))

        normal_speed = fields[NSP + 1]
        normal_flux = flux_of(conserved, pressure, normal_speed, 1)
        normal_signal = jnp.abs(normal_speed) + sound
        normal_signal = 0.5 * jnp.maximum(normal_signal, shift_s(normal_signal, -2))
        blown = BLOWING * blow_rows[pl.ds(zz, TILE, stride=4), :]
        lift = blown / density
        enthalpy = 3.5 * fields[NSP + 3] + fields[NSP + 4] + 0.5 * lift * lift
        wall = [lift * fields[s] for s in range(NSP)]
        formed = FORMATION[2] * wall[2] + FORMATION[3] * wall[3] + FORMATION[4] * wall[4]
        zero = jnp.zeros((TILE, LANES), F32)
        wall = wall + [
            zero, blown * lift + pressure, zero, blown * enthalpy + formed, blown * fields[NSP + 4]
        ]
        relaxation = 2.0 * density * (fields[NSP + 3] - fields[NSP + 4])
        for field in range(NF):
            value, normal = conserved[field], normal_flux[field]
            slot = slot_of(field * ROWS + zz)
            face_ref[slot, :] = faces_along_x(flux[field], value, signal)
            above = shift_s(value, -2)
            level_face = 0.5 * (normal + shift_s(normal, -2)) - normal_signal * (above - value)
            level_face = jnp.where(top, normal, level_face)
            change = 2.0 * (jnp.where(bottom, wall[field], shift_s(level_face, 2)) - level_face)
            part_ref[slot, :] = change + relaxation if field == NF - 1 else change
        return carry

    lax.fori_loop(0, ROWS, row, 0)


def ends_kernel(corner_ref, face_ref, part_ref, out_ref):
    lane = lanes()
    fields = [corner_ref[field] for field in range(NF)]
    density, pressure, sound, conserved = state_of(fields)
    flux = flux_of(conserved, pressure, fields[NSP], 0)
    signal = jnp.abs(fields[NSP]) + sound
    signal = jnp.maximum(signal, shift_x(signal, -1))
    for field in range(NF):
        end_face = faces_along_x(flux[field], conserved[field], signal)
        for zz in range(ROWS):
            left = shift_x(end_face, 109 - SPAN * zz)
            right = shift_x(end_face, 43 - SPAN * zz)
            slot = slot_of(field * ROWS + zz)
            face = jnp.where(
                lane < 2, left, jnp.where(lane >= LANES - 3, right, face_ref[slot, :])
            )
            before = shift_x(jnp.where(lane == LANES - 1, left, face), 1)
            out_ref[slot, :] = part_ref[slot, :] + (before - face)


SPAN_TILES = ROWS + 2 * HALO


def span_kernel(raw_ref, part_ref, out_ref, value_ref, flux_ref, signal_ref):
    for place in range(SPAN_TILES):
        fields = [raw_ref[place, field] for field in range(NF)]
        _, pressure, sound, conserved = state_of(fields)
        speed = fields[NSP + 2]
        flux = flux_of(conserved, pressure, speed, 2)
        signal_ref[place] = jnp.abs(speed) + sound
        for field in range(NF):
            value_ref[place, field] = conserved[field]
            flux_ref[place, field] = flux[field]

    def faces_of(place):
        signal = jnp.maximum(signal_ref[place], signal_ref[place + 1])
        faces = []
        for field in range(NF):
            flux = [flux_ref[place + k, field] for k in range(-2, 4)]
            value = [value_ref[place + k, field] for k in range(-2, 4)]
            slopes = [flux[k + 1] - flux[k] for k in range(5)]
            jumps = [value[k + 1] - value[k] for k in range(5)]
            faces.append(face_flux(flux[2], slopes, jumps, signal))
        return tuple(faces)

    def row(zz, before):
        faces = faces_of(zz + HALO)
        for field in range(NF):
            slot = slot_of(field * ROWS + zz)
            out_ref[slot, :] = part_ref[slot, :] + (before[field] - faces[field])
        return faces

    lax.fori_loop(0, ROWS, row, faces_of(HALO - 1))


MASS, MOMENTUM, HEAT = 0, 5, 8
SPEED, THERMAL, VIBRATION, FRACTION, DENSITY = 9, 12, 13, 14, 19
STATE_COUNT = 20
SLOPED = 10
STATE_ROWS = 8
GRID_ROWS = 6
PAIR_INDEX = ((0, 0), (1, 1), (0, 1), (0, 2), (1, 2), (2, 2))

PRODUCT, STRESS, HEAT_FLUX, HEAT_SLOPE, MASS_FLUX, MASS_SLOPE = 0, 6, 11, 14, 17, 29
LAST_STRESS = 41
FILTERED = 42
SIDE_SLOPE = FILTERED
TILES = FILTERED + 3

TERMS = 12
TERM_FIELD = (0, 1, 2, 3, 4, 5, 6, 7, 8, 8, 8, 9)
TERM_MODEL = (2, 2, 2, 2, 2, 0, 0, 0, 0, 1, 2, 1)


def model_state(fields):
    mass, motion = fields[:NSP], fields[NSP : NSP + 3]
    thermal, vibration = fields[NSP + 3], fields[NSP + 4]
    density = (mass[0] + mass[1]) + (mass[2] + mass[3]) + mass[4]
    inverse = 1.0 / density
    fraction = [m * inverse for m in mass]
    return (
        list(mass)
        + [density * speed for speed in motion]
        + [density * thermal]
        + list(motion)
        + [thermal, vibration]
        + fraction
        + [density]
    )


def level_slope(value, scale):
    bottom, top = level_edges()
    above = jnp.where(top, value, shift_s(value, -2))
    below = jnp.where(bottom, value, shift_s(value, 2))
    return scale * (above - below)


def strain(slopes):
    diagonal = [2.0 * slopes[k][k] for k in range(3)]
    third = (diagonal[0] + diagonal[1] + diagonal[2]) * (1.0 / 3.0)
    first, second = diagonal[0] - third, diagonal[1] - third
    mixed = [slopes[0][1] + slopes[1][0], slopes[0][2] + slopes[2][0], slopes[1][2] + slopes[2][1]]
    last = diagonal[2] - third
    square = (
        first * first + second * second + last * last
        + 2.0 * (mixed[0] * mixed[0] + mixed[1] * mixed[1] + mixed[2] * mixed[2])
    )
    magnitude = jnp.sqrt(0.125 * square + 1e-06)
    return [first, second] + mixed + [last], magnitude


def grid_terms(here, slopes):
    deviator, magnitude = strain(slopes[:3])
    eddy = FILTER_SQUARE * here(DENSITY) * magnitude
    speed = [here(SPEED + k) for k in range(3)]
    momentum = [here(MOMENTUM + k) for k in range(3)]
    thermal = here(THERMAL)
    stress = [eddy * part for part in deviator]
    tiles = [momentum[i] * speed[j] for i, j in PAIR_INDEX]
    tiles += stress[:5]
    tiles += [m * thermal for m in momentum]
    tiles += [eddy * slopes[3][d] for d in range(3)]
    tiles += [here(MASS + s) * speed[d] for s in range(4) for d in range(3)]
    tiles += [eddy * slopes[5 + s][d] for s in range(4) for d in range(3)]
    tiles.append(stress[5])
    return tiles + [eddy * slopes[4][d] for d in range(3)]


def subgrid_terms(tile, speed, d):
    places = (STRESS, STRESS + 1, STRESS + 2, STRESS + 3, STRESS + 4, LAST_STRESS)
    full = ((0, 2, 3), (2, 1, 4), (3, 4, 5))
    tau = [tile(places[full[i][d]]) for i in range(3)]
    species = [tile(MASS_SLOPE + 3 * s + d) for s in range(4)]
    species.append(-((species[0] + species[1]) + (species[2] + species[3])))
    work = speed[0] * tau[0] + speed[1] * tau[1] + speed[2] * tau[2]
    vibration = tile(SIDE_SLOPE + d)
    heat = 3.5 * tile(HEAT_SLOPE + d) + vibration
    formed = FORMATION[2] * species[2] + FORMATION[3] * species[3] + FORMATION[4] * species[4]
    return species + tau + [work, heat, formed, vibration]


def favre(hat):
    density = (hat[0] + hat[1]) + (hat[2] + hat[3]) + hat[4]
    inverse = 1.0 / density
    return density, [hat[5 + k] * inverse for k in range(3)], hat[8] * inverse, [
        hat[s] * inverse for s in range(4)
    ]


def contractions(hat, density, momentum, favre_here, slopes):
    speed, thermal, fraction = favre_here
    deviator, magnitude = strain(slopes[:3])
    eddy = TEST_SQUARE * density * magnitude
    stress = [hat(STRESS + n) for n in range(5)] + [hat(LAST_STRESS)]
    sums = []
    top = bottom = None

    def add(total, value):
        return value if total is None else total + value

    off_top = off_bottom = None
    for n, (i, j) in enumerate(PAIR_INDEX):
        resolved = hat(PRODUCT + n) - momentum[i] * speed[j]
        model = stress[n] - eddy * deviator[n]
        if i == j:
            top, bottom = add(top, resolved * model), add(bottom, model * model)
        else:
            off_top, off_bottom = add(off_top, resolved * model), add(off_bottom, model * model)
    sums += [top + (off_top + off_top), bottom + (off_bottom + off_bottom)]
    top = bottom = None
    for d in range(3):
        resolved = hat(HEAT_FLUX + d) - momentum[d] * thermal
        model = hat(HEAT_SLOPE + d) - eddy * slopes[3][d]
        top, bottom = add(top, resolved * model), add(bottom, model * model)
    sums += [top, bottom]
    top = bottom = None
    for d in range(3):
        last_resolved = last_model = None
        for s in range(4):
            resolved = hat(MASS_FLUX + 3 * s + d) - momentum[d] * fraction[s]
            model = hat(MASS_SLOPE + 3 * s + d) - eddy * slopes[4 + s][d]
            last_resolved, last_model = add(last_resolved, resolved), add(last_model, model)
            top, bottom = add(top, resolved * model), add(bottom, model * model)
        top, bottom = top + last_resolved * last_model, bottom + last_model * last_model
    return sums + [top, bottom]


def filter_x(tile):
    pair = tile + shift_x(tile, -1)
    return pair + shift_x(pair, 1)


def slope_scale():
    bottom, top = level_edges()
    return jnp.where(bottom | top, 4.0, 2.0)


def model_kernel(
    own_ref, far_ref, near_ref, corner_own_ref,
    sum_ref, clamped_ref, tile_ref, state_ref, raw_ref,
    wide_ref, favre_ref,
):
    scale = slope_scale()
    gather_rows(own_ref, far_ref, near_ref, raw_ref)
    for row in range(STATE_ROWS):
        states = model_state([raw_ref[row + 1, field] for field in range(NF)])
        for k in range(STATE_COUNT):
            state_ref[row, k] = states[k]

    def grid_row(row, carry):
        def here(k):
            return state_ref[row + 1, k]

        slopes = []
        for k in range(SLOPED - 1):
            value = here(SPEED + k)
            along_x = shift_x(value, -1) - shift_x(value, 1)
            along_z = state_ref[row + 2, SPEED + k] - state_ref[row, SPEED + k]
            slopes.append((along_x, level_slope(value, scale), along_z))
        for k, tile in enumerate(grid_terms(here, slopes)):
            tile_ref[row, k] = tile
        hat = []
        for k in range(SPEED):
            total = (state_ref[row, k] + state_ref[row + 2, k]) + 2.0 * here(k)
            hat.append(filter_x(total))
        density, speed, thermal, fraction = favre(hat)
        for k, value in enumerate(speed + [thermal] + fraction):
            favre_ref[row, k] = value
        for k in range(3):
            wide_ref[row, k] = hat[MOMENTUM + k]
        wide_ref[row, 3] = density
        return carry

    lax.fori_loop(0, GRID_ROWS, grid_row, 0)
    for k in range(6):
        sum_ref[k] = jnp.zeros((TILE, LANES), F32)

    def test_row(zz, carry):
        row = zz + 1

        def hat(k):
            total = (tile_ref[row - 1, k] + tile_ref[row + 1, k]) + 2.0 * tile_ref[row, k]
            return filter_x(total)

        slopes = []
        for k in range(8):
            value = favre_ref[row, k]
            along_x = shift_x(value, -1) - shift_x(value, 1)
            along_z = favre_ref[row + 1, k] - favre_ref[row - 1, k]
            slopes.append((along_x, level_slope(value, scale), along_z))
        values = [favre_ref[row, k] for k in range(8)]
        sums = contractions(
            hat, wide_ref[row, 3], [wide_ref[row, k] for k in range(3)],
            (values[:3], values[3], values[4:]), slopes,
        )
        for k in range(6):
            sum_ref[k] = sum_ref[k] + sums[k]
        return carry

    lax.fori_loop(0, ROWS, test_row, 0)

    on_left = lanes() < 64
    place = lanes() & (SPAN - 1)
    place = jnp.where(on_left, place, SPAN - 1 - place)
    for field in range(NF):
        tile = clamped = corner_own_ref[field]
        for c in range(HALO):
            copied = jnp.where(on_left, shift_x(tile, c - HALO), shift_x(tile, HALO - c))
            clamped = jnp.where(place == c, copied, clamped)
        clamped_ref[field] = clamped


def corner_kernel(
    clamped_ref, got_one_ref, got_other_ref, sum_ref,
    totals_ref, corner_ref, tile_ref, speed_ref
):
    lane = lanes()
    even = is_even()
    scale = slope_scale()
    even_column = is_first_of_pair("gx")
    column = lax.axis_index("gx")
    first, last = column == 0, column == lax.axis_size("gx") - 1
    place = lane & (SPAN - 1)
    on_left = lane < 64
    low, high = jnp.where(first, 0, HALO), jnp.where(last, SPAN, SPAN - HALO)
    halo = (on_left & (place < low)) | (jnp.logical_not(on_left) & (place >= high))
    fields = []
    for field in range(NF):
        pair, second = divmod(field, 2)
        one, other = tile_of(got_one_ref, pair), tile_of(got_other_ref, pair)
        from_left = jnp.where(even_column, other, one)
        from_right = jnp.where(even_column, one, other)
        if second:
            got = shift_x(jnp.where(on_left, from_right, from_left), 64)
        else:
            got = jnp.where(on_left, from_left, from_right)
        fields.append(jnp.where(halo, got, clamped_ref[field]))
        corner_ref[field] = fields[field]
    state = model_state(fields)

    def slopes_of(value):
        along_x = shift_x(value, -1) - shift_x(value, 1)
        along_z = shift_x(value, -SPAN) - shift_x(value, SPAN)
        return along_x, level_slope(value, scale), along_z

    def filtered(value):
        pair = value + shift_x(value, -SPAN)
        return filter_x(pair + shift_x(pair, SPAN))

    tiles = grid_terms(lambda k: state[k], [slopes_of(state[SPEED + k]) for k in range(SLOPED - 1)])
    for k in range(STRESS, TILES):
        tile_ref[k] = tiles[k]
    for k in range(3):
        speed_ref[k] = state[SPEED + k]
    wide = [filtered(state[k]) for k in range(SPEED)]
    density, speed, thermal, fraction = favre(wide)
    sums = contractions(
        lambda k: filtered(tiles[k]), density, wide[MOMENTUM : MOMENTUM + 3],
        (speed, thermal, fraction), [slopes_of(value) for value in speed + [thermal] + fraction],
    )
    main_totals, corner_totals = [sum_ref[k] for k in range(6)], []
    for value in sums:
        value = value + shift_x(value, -SPAN)
        corner_totals.append(value + shift_x(value, -2 * SPAN))
    edges = jnp.zeros((TILE, LANES), F32)
    for k in range(3):
        packed = []
        for main, side in zip(main_totals[2 * k : 2 * k + 2], corner_totals[2 * k : 2 * k + 2]):
            main = jnp.where(lane < 2, shift_x(side, -19), main)
            main = jnp.where(lane >= LANES - 2, shift_x(side, 126 - 83), main)
            packed.append((main + shift_s(main, 1), side + shift_s(side, 1), main, side))
        top_main = shift_s(packed[0][0], -1) * (1.0 / 512.0)
        top_side = shift_s(packed[0][1], -1) * (1.0 / 512.0)
        totals_ref[pl.ds(k * TILE, TILE), :] = jnp.where(even, top_main, packed[1][0] * (1.0 / 1024.0))
        side = jnp.where(even, top_side, packed[1][1] * (1.0 / 1024.0))
        edges = jnp.where(lane == 2 * k, shift_x(side, 2 * k - 18), edges)
        edges = jnp.where(lane == 2 * k + 1, shift_x(side, 2 * k + 1 - 85), edges)
    totals_ref[pl.ds(3 * TILE, TILE), :] = edges


def term_kernel(tile_ref, state_ref, corner_ref, corner_speed_ref, terms_ref):
    lane = lanes()
    bottom, top = level_edges()

    def terms(place, d):
        speed = [state_ref[place + 1, SPEED + k] for k in range(3)]
        return subgrid_terms(lambda k: tile_ref[place, k], speed, d)

    corner_speed = [corner_speed_ref[k] for k in range(3)]
    corner = [subgrid_terms(lambda k: corner_ref[k], corner_speed, d) for d in range(3)]
    corner[2] = [shift_x(value, -SPAN) - shift_x(value, SPAN) for value in corner[2]]

    def patched(value, side, zz):
        value = jnp.where(lane == 0, shift_x(side, -19 - SPAN * zz), value)
        return jnp.where(lane == LANES - 1, shift_x(side, 43 - SPAN * zz), value)

    for zz in range(ROWS):
        row = zz + 1
        along_x, along_y = terms(row, 0), terms(row, 1)
        before, after = terms(row - 1, 2), terms(row + 1, 2)
        for n in range(TERMS):
            right = shift_x(corner[0][n], 42 - SPAN * zz)
            left = shift_x(corner[0][n], -18 - SPAN * zz)
            terms_ref[zz, n, 0] = jnp.where(lane >= LANES - 2, right, shift_x(along_x[n], -1))
            terms_ref[zz, n, 1] = jnp.where(lane < 2, left, shift_x(along_x[n], 1))
            terms_ref[zz, n, 2] = patched(after[n] - before[n], corner[2][n], zz)
            along = patched(along_y[n], corner[1][n], zz)
            terms_ref[zz, n, 3] = jnp.where(top, along, shift_s(along, -2))
            terms_ref[zz, n, 4] = jnp.where(bottom, -along, shift_s(along, 2))


def final_kernel(*refs, parts):
    part_refs = refs[:parts]
    base_ref, terms_ref, out_ref, coefficient_ref, scratch = refs[parts:]
    lane = lanes()
    even = is_even()
    bottom, top = level_edges()
    totals = [
        (tile_of(part_refs[0], k) + tile_of(part_refs[1], k))
        + (tile_of(part_refs[2], k) + tile_of(part_refs[3], k))
        for k in range(4)
    ]
    ratios = []
    for total in totals:
        total = total * (1.0 / (TILE * lax.axis_size("gz")))
        numerator = jnp.where(even, total, shift_s(total, 1))
        denominator = jnp.where(even, shift_s(total, -1), total)
        ratios.append(numerator / (denominator + RATIO_EPSILON))
    column = lax.axis_index("gx")
    first, last = column == 0, column == lax.axis_size("gx") - 1
    here, ahead, behind, above, below = [], [], [], [], []
    for k in range(3):
        ratio = ratios[k]
        scratch[...] = ratio
        coefficient_ref[k] = scratch[pl.ds(0, 4, stride=2), :]
        before = jnp.where(first, ratio, shift_x(ratios[3], -2 * k))
        after = jnp.where(last, ratio, shift_x(ratios[3], 127 - (2 * k + 1)))
        ratio = 0.25 * ratio
        here.append(ratio)
        ahead.append(jnp.where(lane == LANES - 1, 0.25 * after, shift_x(ratio, -1)))
        behind.append(jnp.where(lane == 0, 0.25 * before, shift_x(ratio, 1)))
        above.append(2.0 * jnp.where(top, ratio, shift_s(ratio, -2)))
        below.append(2.0 * jnp.where(bottom, ratio, shift_s(ratio, 2)))

    def row(zz, carry):
        sums = [tile_of(base_ref, field * ROWS + zz) for field in range(NF)]
        for n in range(TERMS):
            k = TERM_MODEL[n]
            change = (
                (ahead[k] * terms_ref[zz, n, 0] - behind[k] * terms_ref[zz, n, 1])
                + here[k] * terms_ref[zz, n, 2]
                + (above[k] * terms_ref[zz, n, 3] - below[k] * terms_ref[zz, n, 4])
            )
            sums[TERM_FIELD[n]] = sums[TERM_FIELD[n]] + change
        for field in range(NF):
            out_ref[pl.ds(field * 32 + zz, TILE, stride=4), :] = sums[field]
        return carry

    lax.fori_loop(0, ROWS, row, 0)


def call(kernel, out_shapes, scratch=(), inputs=0, final=False):
    shape_of = jax.ShapeDtypeStruct if final else pltpu.VMEM
    run = pl.pallas_call(
        kernel,
        out_shape=[shape_of(shape, F32) for shape in out_shapes],
        in_specs=[VMEM] * inputs,
        out_specs=[VMEM] * len(out_shapes),
        scratch_shapes=[pltpu.VMEM(shape, F32) for shape in scratch],
        compiler_params=SMALL,
    )

    def placed(*args):
        return run(*[pltpu.with_memory_space_constraint(arg, pltpu.VMEM) for arg in args])

    return placed


def body(constituent_mass, flow_speeds, thermal_pair, blowing_indicator):
    count_x = lax.axis_size("gx")
    count_z = lax.axis_size("gz")

    def swap(axis, count, near):
        step = [1, -1] if near else [-1, 1]
        return lambda value: lax.ppermute(
            value, axis, [(i, (i + step[i % 2]) % count) for i in range(count)]
        )

    arrays = [
        value.reshape(-1, LANES) for value in (constituent_mass, flow_speeds, thermal_pair)
    ]
    packed = (PACK_ROWS, LANES)
    rows = (GROUPS * TILE, LANES)
    fields = (NF, TILE, LANES)
    own, left, right, far, near, blown = pl.pallas_call(
        pack_kernel,
        out_shape=[
            pltpu.VMEM(shape, F32)
            for shape in (
                rows, packed, packed, (MESSAGE_ROWS, LANES), (MESSAGE_ROWS, LANES),
                (4 * TILE, LANES),
            )
        ],
        in_specs=[pl.BlockSpec(memory_space=pltpu.HBM)] * 4,
        out_specs=[VMEM] * 6,
        scratch_shapes=[
            pltpu.VMEM((NF * 4 * TILE, LANES), F32),
            pltpu.VMEM(blowing_indicator.shape, jnp.int32),
            pltpu.SemaphoreType.DMA((4,)),
        ],
        compiler_params=SMALL,
    )(*[
        pltpu.with_memory_space_constraint(value, pltpu.HBM)
        for value in arrays + [blowing_indicator]
    ])
    far = swap("gz", count_z, False)(far)
    near = swap("gz", count_z, True)(near)
    face, part = call(stream_kernel, [rows, rows], inputs=2)(own, blown)
    far, near, face, part = lax.optimization_barrier((far, near, face, part))

    corner, one, other = call(
        corner_pack_kernel,
        [fields, (PAIRS * TILE, LANES), (PAIRS * TILE, LANES)],
        inputs=4,
    )(left, right, far, near)
    got_one = swap("gx", count_x, True)(one)
    got_other = swap("gx", count_x, False)(other)
    sums, clamped, tiles, state, raw = call(
        model_kernel,
        [
            (6, TILE, LANES),
            fields,
            (GRID_ROWS, TILES, TILE, LANES),
            (STATE_ROWS, STATE_COUNT, TILE, LANES),
            (SPAN_TILES, NF, TILE, LANES),
        ],
        scratch=[(GRID_ROWS, 4, TILE, LANES), (GRID_ROWS, 8, TILE, LANES)],
        inputs=4,
    )(own, far, near, corner)
    got_one, got_other, sums = lax.optimization_barrier((got_one, got_other, sums))
    totals, corner, corner_tiles, corner_speed = call(
        corner_kernel,
        [(4 * TILE, LANES), fields, (TILES, TILE, LANES), (3, TILE, LANES)],
        inputs=4,
    )(clamped, got_one, got_other, sums)

    (terms,) = call(term_kernel, [(ROWS, TERMS, 5, TILE, LANES)], inputs=4)(
        tiles, state, corner_tiles, corner_speed
    )
    (part,) = call(ends_kernel, [rows], inputs=3)(corner, face, part)
    (base,) = call(
        span_kernel,
        [rows],
        scratch=[
            (SPAN_TILES, NF, TILE, LANES), (SPAN_TILES, NF, TILE, LANES), (SPAN_TILES, TILE, LANES),
        ],
        inputs=2,
    )(raw, part)

    def crossed(value, mask):
        return lax.ppermute(value, "gz", [(i, i ^ mask) for i in range(count_z)])

    totals = totals + crossed(totals, 1)
    reach = 2
    while count_z > 4 * reach:
        a, b, c = (crossed(totals, k * reach) for k in (1, 2, 3))
        totals = (totals + a) + (b + c)
        reach *= 4
    parts = [totals] + [
        crossed(totals, k * reach) if k * reach < count_z else jnp.zeros_like(totals)
        for k in (2, 3, 1)
    ]

    def final(*refs):
        final_kernel(*refs, parts=4)

    tendency, coefficients = call(
        final,
        [(NF * 32, LANES), (3, 4, LANES)],
        scratch=[(TILE, LANES)],
        inputs=6,
        final=True,
    )(*parts, base, terms)
    return tendency.reshape(NF, 4, TILE, LANES), coefficients


def solution(mesh):
    placed = (
        P(None, None, "gz", "gx"),
        P(None, None, "gz", "gx"),
        P(None, None, "gz", "gx"),
        P("gz", "gx"),
    )
    return jax.shard_map(
        body,
        mesh=mesh,
        in_specs=placed,
        out_specs=(P(None, None, "gz", "gx"), P(None, None, "gx")),
        check_vma=False,
    )
```

```python
import jax
import jax.numpy as jnp
from jax import lax
from jax.experimental import pallas as pl
from jax.experimental.pallas import tpu as pltpu
from jax.sharding import PartitionSpec as P


NSP = 5
NF = 10
ROWS = 4
TILE = 8
LANES = 128
HALO = 3
SPAN = 8
LAST = LANES - 5
GROUPS = NF * ROWS
PAIRS = NF // 2
PACKS = 3
PACK_ROWS = PACKS * TILE
MAIN_ROWS = PAIRS * HALO * TILE

HEAT_RATIO = 1.4
FILTER_SQUARE = 0.5 ** (2.0 / 3.0)
TEST_SQUARE = 2.0 ** (2.0 / 3.0)
FORMATION = (0.0, 0.0, 0.1, 0.5, 0.25)
BLOWING = 0.3
SMOOTH_FLOOR = 0.01
RATIO_EPSILON = 1e-06

VMEM = pl.BlockSpec(memory_space=pltpu.VMEM)
F32 = jnp.float32
SMALL = pltpu.CompilerParams(vmem_limit_bytes=8 << 20)


def lanes():
    return lax.broadcasted_iota(jnp.int32, (TILE, LANES), 1)


def sublanes():
    return lax.broadcasted_iota(jnp.int32, (TILE, LANES), 0)


def shift_x(tile, step):
    if isinstance(step, int):
        step = step % LANES
        if step == 0:
            return tile
    return pltpu.roll(tile, step, 1)


def shift_s(tile, step):
    return pltpu.roll(tile, step % TILE, 0)


def is_even():
    return (sublanes() & 1) == 0


def level_edges():
    level = sublanes() >> 1
    return level == 0, level == 3


def slot_of(index):
    start = index * TILE
    return pl.ds(start if isinstance(index, int) else pl.multiple_of(start, TILE), TILE)


def tile_of(ref, index):
    return ref[slot_of(index), :]


def is_first_of_pair(axis):
    return (lax.axis_index(axis) & 1) == 0


def halo_tile(far_ref, near_ref, below, index):
    first, second = (far_ref, near_ref) if below else (near_ref, far_ref)
    return jnp.where(is_first_of_pair("gz"), tile_of(first, index), tile_of(second, index))


def pack_kernel(
    mass_hbm, speed_hbm, heat_hbm, blow_hbm, own_ref, far_ref, near_ref, blow_rows,
    given_ref, blow_ref, arrived
):
    start, copies = 0, []
    for k, source in enumerate((mass_hbm, speed_hbm, heat_hbm)):
        target = given_ref.at[pl.ds(start, source.shape[0])]
        copies.append(pltpu.make_async_copy(source, target, arrived.at[k]))
        start += source.shape[0]
    copies.append(pltpu.make_async_copy(blow_hbm, blow_ref, arrived.at[3]))
    for copy in copies:
        copy.start()
    for copy in copies:
        copy.wait()
    even = is_even()
    first_core = is_first_of_pair("gz")
    tiles = {}
    for field in range(NF):
        for zz in range(ROWS):
            tile = given_ref[pl.ds(field * 32 + zz, TILE, stride=4), :]
            tiles[field, zz] = tile
            own_ref[slot_of(field * ROWS + zz), :] = tile
        if field % 2:
            for k in range(HALO):
                up = jnp.where(even, shift_s(tiles[field - 1, k + 1], -1), tiles[field, k + 1])
                down = jnp.where(even, tiles[field, k], shift_s(tiles[field - 1, k], 1))
                slot = slot_of(field // 2 * HALO + k)
                far_ref[slot, :] = jnp.where(first_core, down, up)
                near_ref[slot, :] = jnp.where(first_core, up, down)
    for level in range(4):
        blow_rows[pl.ds(level * TILE, TILE), :] = blow_ref[...].astype(F32)


def gather_rows(own_ref, far_ref, near_ref, raw_ref):
    even = is_even()
    for field in range(NF):
        pair, second = divmod(field, 2)
        own = [tile_of(own_ref, field * ROWS + zz) for zz in range(ROWS)]
        for zz in range(ROWS):
            raw_ref[zz + HALO, field] = own[zz]
        for k in range(HALO):
            low = halo_tile(far_ref, near_ref, True, pair * HALO + k)
            high = halo_tile(far_ref, near_ref, False, pair * HALO + k)
            if second:
                low, high = shift_s(low, -1), shift_s(high, 1)
            raw_ref[k, field] = jnp.where(even, low, shift_s(own[k + 1], 1))
            raw_ref[k + HALO + ROWS, field] = jnp.where(even, shift_s(own[k], -1), high)


def own_corner_kernel(own_ref, corner_ref):
    lane = lanes()
    within = lane & 63
    for field in range(NF):
        tile = None
        for side in range(2):
            for zz in range(ROWS):
                start = 64 * side + SPAN * (zz + 2)
                moved = shift_x(
                    tile_of(own_ref, field * ROWS + zz), start - LAST if side else start + HALO
                )
                tile = moved if tile is None else jnp.where(lane >= start, moved, tile)
        low, high = shift_s(shift_x(tile, -32), 1), shift_s(shift_x(tile, 32), -1)
        corner_ref[field] = jnp.where(within < 16, low, jnp.where(within >= 48, high, tile))


def corner_pack_kernel(own_corner_ref, far_ref, near_ref, corner_ref, one_ref, other_ref):
    lane = lanes()
    even = is_even()
    even_column = is_first_of_pair("gx")
    within = lane & 63
    halo = (even & (within < 16)) | (jnp.logical_not(even) & (within >= 48))
    corners = []
    for pair in range(PAIRS):
        rows = [
            (SPAN * (zz + 2), halo_tile(far_ref, near_ref, zz < 0, pair * HALO + zz % 4 - (zz < 0)))
            for zz in (-2, -1, 4, 5)
        ]
        tile = None
        for side in range(2):
            for start, row in rows:
                start += 64 * side
                moved = shift_x(row, start - LAST if side else start + HALO)
                tile = moved if tile is None else jnp.where(lane >= start, moved, tile)
        swapped = jnp.where(within < 32, shift_s(tile, -1), shift_s(tile, 1))
        for n, got in enumerate((tile, swapped)):
            corners.append(jnp.where(halo, got, own_corner_ref[2 * pair + n]))
            corner_ref[2 * pair + n] = corners[-1]
    ahead = (lane & (SPAN - 1)) < HALO

    def packed(group, move):
        halves = [
            jnp.where(
                ahead, shift_x(group[n], 32 * n + move), shift_x(group[n + 1], 32 * n + HALO + move)
            )
            for n in range(0, len(group), 2)
        ]
        return halves[0] if len(halves) == 1 else jnp.where(lane < 64, *halves)

    for k in range(PACKS):
        group = corners[4 * k : 4 * k + 4]
        to_left, to_right = packed(group, -3), packed(group, -66)
        one_ref[slot_of(k), :] = jnp.where(even_column, to_right, to_left)
        other_ref[slot_of(k), :] = jnp.where(even_column, to_left, to_right)


def state_of(fields):
    mass, motion = fields[:NSP], fields[NSP : NSP + 3]
    thermal, vibration = fields[NSP + 3], fields[NSP + 4]
    density = (mass[0] + mass[1]) + (mass[2] + mass[3]) + mass[4]
    formed = FORMATION[2] * mass[2] + FORMATION[3] * mass[3] + FORMATION[4] * mass[4]
    motion_square = motion[0] * motion[0] + motion[1] * motion[1] + motion[2] * motion[2]
    energy = density * (2.5 * thermal + vibration + 0.5 * motion_square) + formed
    conserved = (
        list(mass) + [density * speed for speed in motion] + [energy, density * vibration]
    )
    return density, density * thermal, jnp.sqrt(HEAT_RATIO * thermal), conserved


def flux_of(conserved, pressure, speed, component):
    flux = [value * speed for value in conserved]
    flux[NSP + component] = flux[NSP + component] + pressure
    flux[NSP + 3] = flux[NSP + 3] + pressure * speed
    return flux


def correction(d0, d1, d2, d3):
    floor = 4.0 * SMOOTH_FLOOR * 12.0 / 13.0
    share = 3.0 / 13.0
    e0, e1, e2 = d1 - d0, d2 - d1, d3 - d2
    g0, g1, g2 = e0 + (d1 + d1), d1 + d2, e2 - (d2 + d2)
    b0 = (e0 * e0 + floor) + share * (g0 * g0)
    b1 = (e1 * e1 + floor) + share * (g1 * g1)
    b2 = (e2 * e2 + floor) + share * (g2 * g2)
    p0, p1, p2 = b1 * b2, b0 * b2, b0 * b1
    w0 = p0 * p0
    w1 = 6.0 * (p1 * p1)
    w2 = 3.0 * (p2 * p2)
    r0 = 5.0 * d1 - (d0 + d0)
    r1 = d1 + (d2 + d2)
    r2 = 4.0 * d2 - d3
    return (w0 * r0 + w1 * r1 + w2 * r2) / (w0 + w1 + w2)


def face_flux(here, slopes, jumps, signal):
    waves = [signal * jump for jump in jumps]
    plus = [slopes[k] + waves[k] for k in range(4)]
    minus = [waves[k] - slopes[k] for k in range(1, 5)]
    gain = correction(*plus)
    loss = correction(minus[3], minus[2], minus[1], minus[0])
    return here + 0.5 * (slopes[2] - waves[2]) + (gain + loss) * (1.0 / 12.0)


def faces_along_x(flux, conserved, signal):
    slope = shift_x(flux, -1) - flux
    jump = shift_x(conserved, -1) - conserved
    slopes = [shift_x(slope, -k) for k in range(-2, 3)]
    jumps = [shift_x(jump, -k) for k in range(-2, 3)]
    return face_flux(flux, slopes, jumps, signal)


def stream_kernel(own_ref, blow_rows, face_ref, part_ref):
    bottom, top = level_edges()

    def row(zz, carry):
        fields = [tile_of(own_ref, field * ROWS + zz) for field in range(NF)]
        density, pressure, sound, conserved = state_of(fields)
        speed = fields[NSP]
        flux = flux_of(conserved, pressure, speed, 0)
        signal = jnp.abs(speed) + sound
        signal = jnp.maximum(signal, shift_x(signal, -1))

        normal_speed = fields[NSP + 1]
        normal_flux = flux_of(conserved, pressure, normal_speed, 1)
        normal_signal = jnp.abs(normal_speed) + sound
        normal_signal = 0.5 * jnp.maximum(normal_signal, shift_s(normal_signal, -2))
        blown = BLOWING * blow_rows[pl.ds(zz, TILE, stride=4), :]
        lift = blown / density
        enthalpy = 3.5 * fields[NSP + 3] + fields[NSP + 4] + 0.5 * lift * lift
        wall = [lift * fields[s] for s in range(NSP)]
        formed = FORMATION[2] * wall[2] + FORMATION[3] * wall[3] + FORMATION[4] * wall[4]
        zero = jnp.zeros((TILE, LANES), F32)
        wall = wall + [
            zero, blown * lift + pressure, zero, blown * enthalpy + formed, blown * fields[NSP + 4]
        ]
        relaxation = 2.0 * density * (fields[NSP + 3] - fields[NSP + 4])
        for field in range(NF):
            value, normal = conserved[field], normal_flux[field]
            slot = slot_of(field * ROWS + zz)
            face_ref[slot, :] = faces_along_x(flux[field], value, signal)
            above = shift_s(value, -2)
            level_face = 0.5 * (normal + shift_s(normal, -2)) - normal_signal * (above - value)
            level_face = jnp.where(top, normal, level_face)
            change = 2.0 * (jnp.where(bottom, wall[field], shift_s(level_face, 2)) - level_face)
            part_ref[slot, :] = change + relaxation if field == NF - 1 else change
        return carry

    lax.fori_loop(0, ROWS, row, 0)


def ends_kernel(corner_ref, face_ref, part_ref, out_ref):
    lane = lanes()
    fields = [corner_ref[field] for field in range(NF)]
    density, pressure, sound, conserved = state_of(fields)
    flux = flux_of(conserved, pressure, fields[NSP], 0)
    signal = jnp.abs(fields[NSP]) + sound
    signal = jnp.maximum(signal, shift_x(signal, -1))
    for field in range(NF):
        end_face = faces_along_x(flux[field], conserved[field], signal)
        for zz in range(ROWS):
            left = shift_x(end_face, 109 - SPAN * zz)
            right = shift_x(end_face, 43 - SPAN * zz)
            slot = slot_of(field * ROWS + zz)
            face = jnp.where(
                lane < 2, left, jnp.where(lane >= LANES - 3, right, face_ref[slot, :])
            )
            before = shift_x(jnp.where(lane == LANES - 1, left, face), 1)
            out_ref[slot, :] = part_ref[slot, :] + (before - face)


SPAN_TILES = ROWS + 2 * HALO


def span_kernel(raw_ref, part_ref, out_ref, value_ref, flux_ref, signal_ref):
    for place in range(SPAN_TILES):
        fields = [raw_ref[place, field] for field in range(NF)]
        _, pressure, sound, conserved = state_of(fields)
        speed = fields[NSP + 2]
        flux = flux_of(conserved, pressure, speed, 2)
        signal_ref[place] = jnp.abs(speed) + sound
        for field in range(NF):
            value_ref[place, field] = conserved[field]
            flux_ref[place, field] = flux[field]

    def faces_of(place):
        signal = jnp.maximum(signal_ref[place], signal_ref[place + 1])
        faces = []
        for field in range(NF):
            flux = [flux_ref[place + k, field] for k in range(-2, 4)]
            value = [value_ref[place + k, field] for k in range(-2, 4)]
            slopes = [flux[k + 1] - flux[k] for k in range(5)]
            jumps = [value[k + 1] - value[k] for k in range(5)]
            faces.append(face_flux(flux[2], slopes, jumps, signal))
        return tuple(faces)

    def row(zz, before):
        faces = faces_of(zz + HALO)
        for field in range(NF):
            slot = slot_of(field * ROWS + zz)
            out_ref[slot, :] = part_ref[slot, :] + (before[field] - faces[field])
        return faces

    lax.fori_loop(0, ROWS, row, faces_of(HALO - 1))


MASS, MOMENTUM, HEAT = 0, 5, 8
SPEED, THERMAL, VIBRATION, FRACTION, DENSITY = 9, 12, 13, 14, 19
STATE_COUNT = 20
SLOPED = 10
STATE_ROWS = 8
GRID_ROWS = 6
PAIR_INDEX = ((0, 0), (1, 1), (0, 1), (0, 2), (1, 2), (2, 2))

PRODUCT, STRESS, HEAT_FLUX, HEAT_SLOPE, MASS_FLUX, MASS_SLOPE = 0, 6, 11, 14, 17, 29
LAST_STRESS = 41
FILTERED = 42
SIDE_SLOPE = FILTERED
TILES = FILTERED + 3

TERMS = 12
TERM_FIELD = (0, 1, 2, 3, 4, 5, 6, 7, 8, 8, 8, 9)
TERM_MODEL = (2, 2, 2, 2, 2, 0, 0, 0, 0, 1, 2, 1)


def model_state(fields):
    mass, motion = fields[:NSP], fields[NSP : NSP + 3]
    thermal, vibration = fields[NSP + 3], fields[NSP + 4]
    density = (mass[0] + mass[1]) + (mass[2] + mass[3]) + mass[4]
    inverse = 1.0 / density
    fraction = [m * inverse for m in mass]
    return (
        list(mass)
        + [density * speed for speed in motion]
        + [density * thermal]
        + list(motion)
        + [thermal, vibration]
        + fraction
        + [density]
    )


def level_slope(value, scale):
    bottom, top = level_edges()
    above = jnp.where(top, value, shift_s(value, -2))
    below = jnp.where(bottom, value, shift_s(value, 2))
    return scale * (above - below)


def strain(slopes):
    diagonal = [2.0 * slopes[k][k] for k in range(3)]
    third = (diagonal[0] + diagonal[1] + diagonal[2]) * (1.0 / 3.0)
    first, second = diagonal[0] - third, diagonal[1] - third
    mixed = [slopes[0][1] + slopes[1][0], slopes[0][2] + slopes[2][0], slopes[1][2] + slopes[2][1]]
    last = diagonal[2] - third
    square = (
        first * first + second * second + last * last
        + 2.0 * (mixed[0] * mixed[0] + mixed[1] * mixed[1] + mixed[2] * mixed[2])
    )
    magnitude = jnp.sqrt(0.125 * square + 1e-06)
    return [first, second] + mixed + [last], magnitude


def grid_terms(here, slopes):
    deviator, magnitude = strain(slopes[:3])
    eddy = FILTER_SQUARE * here(DENSITY) * magnitude
    speed = [here(SPEED + k) for k in range(3)]
    momentum = [here(MOMENTUM + k) for k in range(3)]
    thermal = here(THERMAL)
    stress = [eddy * part for part in deviator]
    tiles = [momentum[i] * speed[j] for i, j in PAIR_INDEX]
    tiles += stress[:5]
    tiles += [m * thermal for m in momentum]
    tiles += [eddy * slopes[3][d] for d in range(3)]
    tiles += [here(MASS + s) * speed[d] for s in range(4) for d in range(3)]
    tiles += [eddy * slopes[5 + s][d] for s in range(4) for d in range(3)]
    tiles.append(stress[5])
    return tiles + [eddy * slopes[4][d] for d in range(3)]


def subgrid_terms(tile, speed, d):
    places = (STRESS, STRESS + 1, STRESS + 2, STRESS + 3, STRESS + 4, LAST_STRESS)
    full = ((0, 2, 3), (2, 1, 4), (3, 4, 5))
    tau = [tile(places[full[i][d]]) for i in range(3)]
    species = [tile(MASS_SLOPE + 3 * s + d) for s in range(4)]
    species.append(-((species[0] + species[1]) + (species[2] + species[3])))
    work = speed[0] * tau[0] + speed[1] * tau[1] + speed[2] * tau[2]
    vibration = tile(SIDE_SLOPE + d)
    heat = 3.5 * tile(HEAT_SLOPE + d) + vibration
    formed = FORMATION[2] * species[2] + FORMATION[3] * species[3] + FORMATION[4] * species[4]
    return species + tau + [work, heat, formed, vibration]


def favre(hat):
    density = (hat[0] + hat[1]) + (hat[2] + hat[3]) + hat[4]
    inverse = 1.0 / density
    return density, [hat[5 + k] * inverse for k in range(3)], hat[8] * inverse, [
        hat[s] * inverse for s in range(4)
    ]


def contractions(hat, density, momentum, favre_here, slopes):
    speed, thermal, fraction = favre_here
    deviator, magnitude = strain(slopes[:3])
    eddy = TEST_SQUARE * density * magnitude
    stress = [hat(STRESS + n) for n in range(5)] + [hat(LAST_STRESS)]
    sums = []
    top = bottom = None

    def add(total, value):
        return value if total is None else total + value

    off_top = off_bottom = None
    for n, (i, j) in enumerate(PAIR_INDEX):
        resolved = hat(PRODUCT + n) - momentum[i] * speed[j]
        model = stress[n] - eddy * deviator[n]
        if i == j:
            top, bottom = add(top, resolved * model), add(bottom, model * model)
        else:
            off_top, off_bottom = add(off_top, resolved * model), add(off_bottom, model * model)
    sums += [top + (off_top + off_top), bottom + (off_bottom + off_bottom)]
    top = bottom = None
    for d in range(3):
        resolved = hat(HEAT_FLUX + d) - momentum[d] * thermal
        model = hat(HEAT_SLOPE + d) - eddy * slopes[3][d]
        top, bottom = add(top, resolved * model), add(bottom, model * model)
    sums += [top, bottom]
    top = bottom = None
    for d in range(3):
        last_resolved = last_model = None
        for s in range(4):
            resolved = hat(MASS_FLUX + 3 * s + d) - momentum[d] * fraction[s]
            model = hat(MASS_SLOPE + 3 * s + d) - eddy * slopes[4 + s][d]
            last_resolved, last_model = add(last_resolved, resolved), add(last_model, model)
            top, bottom = add(top, resolved * model), add(bottom, model * model)
        top, bottom = top + last_resolved * last_model, bottom + last_model * last_model
    return sums + [top, bottom]


def filter_x(tile):
    pair = tile + shift_x(tile, -1)
    return pair + shift_x(pair, 1)


def slope_scale():
    bottom, top = level_edges()
    return jnp.where(bottom | top, 4.0, 2.0)


def model_kernel(
    own_ref, far_ref, near_ref, corner_own_ref,
    sum_ref, clamped_ref, tile_ref, state_ref, raw_ref,
    wide_ref, favre_ref,
):
    scale = slope_scale()
    gather_rows(own_ref, far_ref, near_ref, raw_ref)
    for row in range(STATE_ROWS):
        states = model_state([raw_ref[row + 1, field] for field in range(NF)])
        for k in range(STATE_COUNT):
            state_ref[row, k] = states[k]

    def grid_row(row, carry):
        def here(k):
            return state_ref[row + 1, k]

        slopes = []
        for k in range(SLOPED - 1):
            value = here(SPEED + k)
            along_x = shift_x(value, -1) - shift_x(value, 1)
            along_z = state_ref[row + 2, SPEED + k] - state_ref[row, SPEED + k]
            slopes.append((along_x, level_slope(value, scale), along_z))
        for k, tile in enumerate(grid_terms(here, slopes)):
            tile_ref[row, k] = tile
        hat = []
        for k in range(SPEED):
            total = (state_ref[row, k] + state_ref[row + 2, k]) + 2.0 * here(k)
            hat.append(filter_x(total))
        density, speed, thermal, fraction = favre(hat)
        for k, value in enumerate(speed + [thermal] + fraction):
            favre_ref[row, k] = value
        for k in range(3):
            wide_ref[row, k] = hat[MOMENTUM + k]
        wide_ref[row, 3] = density
        return carry

    lax.fori_loop(0, GRID_ROWS, grid_row, 0)
    for k in range(6):
        sum_ref[k] = jnp.zeros((TILE, LANES), F32)

    def test_row(zz, carry):
        row = zz + 1

        def hat(k):
            total = (tile_ref[row - 1, k] + tile_ref[row + 1, k]) + 2.0 * tile_ref[row, k]
            return filter_x(total)

        slopes = []
        for k in range(8):
            value = favre_ref[row, k]
            along_x = shift_x(value, -1) - shift_x(value, 1)
            along_z = favre_ref[row + 1, k] - favre_ref[row - 1, k]
            slopes.append((along_x, level_slope(value, scale), along_z))
        values = [favre_ref[row, k] for k in range(8)]
        sums = contractions(
            hat, wide_ref[row, 3], [wide_ref[row, k] for k in range(3)],
            (values[:3], values[3], values[4:]), slopes,
        )
        for k in range(6):
            sum_ref[k] = sum_ref[k] + sums[k]
        return carry

    lax.fori_loop(0, ROWS, test_row, 0)

    on_left = lanes() < 64
    place = lanes() & (SPAN - 1)
    place = jnp.where(on_left, place, SPAN - 1 - place)
    for field in range(NF):
        tile = clamped = corner_own_ref[field]
        for c in range(HALO):
            copied = jnp.where(on_left, shift_x(tile, c - HALO), shift_x(tile, HALO - c))
            clamped = jnp.where(place == c, copied, clamped)
        clamped_ref[field] = clamped


def corner_kernel(
    clamped_ref, got_one_ref, got_other_ref, sum_ref,
    totals_ref, corner_ref, tile_ref, speed_ref
):
    lane = lanes()
    even = is_even()
    scale = slope_scale()
    even_column = is_first_of_pair("gx")
    column = lax.axis_index("gx")
    first, last = column == 0, column == lax.axis_size("gx") - 1
    place = lane & (SPAN - 1)
    on_left = lane < 64
    low, high = jnp.where(first, 0, HALO), jnp.where(last, SPAN, SPAN - HALO)
    halo = (on_left & (place < low)) | (jnp.logical_not(on_left) & (place >= high))
    fields = []
    for field in range(NF):
        k, j = divmod(field, 4)
        if j == 0:
            one, other = tile_of(got_one_ref, k), tile_of(got_other_ref, k)
            from_left = jnp.where(even_column, other, one)
            from_right = jnp.where(even_column, one, other)
        move = 64 * (j // 2) + HALO * (j % 2)
        got = jnp.where(on_left, shift_x(from_left, -move), shift_x(from_right, 69 - move))
        fields.append(jnp.where(halo, got, clamped_ref[field]))
        corner_ref[field] = fields[field]
    state = model_state(fields)

    def slopes_of(value):
        along_x = shift_x(value, -1) - shift_x(value, 1)
        along_z = shift_x(value, -SPAN) - shift_x(value, SPAN)
        return along_x, level_slope(value, scale), along_z

    def filtered(value):
        pair = value + shift_x(value, -SPAN)
        return filter_x(pair + shift_x(pair, SPAN))

    tiles = grid_terms(lambda k: state[k], [slopes_of(state[SPEED + k]) for k in range(SLOPED - 1)])
    for k in range(STRESS, TILES):
        tile_ref[k] = tiles[k]
    for k in range(3):
        speed_ref[k] = state[SPEED + k]
    wide = [filtered(state[k]) for k in range(SPEED)]
    density, speed, thermal, fraction = favre(wide)
    sums = contractions(
        lambda k: filtered(tiles[k]), density, wide[MOMENTUM : MOMENTUM + 3],
        (speed, thermal, fraction), [slopes_of(value) for value in speed + [thermal] + fraction],
    )
    main_totals, corner_totals = [sum_ref[k] for k in range(6)], []
    for value in sums:
        value = value + shift_x(value, -SPAN)
        corner_totals.append(value + shift_x(value, -2 * SPAN))
    edges = jnp.zeros((TILE, LANES), F32)
    for k in range(3):
        packed = []
        for main, side in zip(main_totals[2 * k : 2 * k + 2], corner_totals[2 * k : 2 * k + 2]):
            main = jnp.where(lane < 2, shift_x(side, -19), main)
            main = jnp.where(lane >= LANES - 2, shift_x(side, 126 - 83), main)
            packed.append((main + shift_s(main, 1), side + shift_s(side, 1), main, side))
        top_main = shift_s(packed[0][0], -1) * (1.0 / 512.0)
        top_side = shift_s(packed[0][1], -1) * (1.0 / 512.0)
        totals_ref[pl.ds(k * TILE, TILE), :] = jnp.where(even, top_main, packed[1][0] * (1.0 / 1024.0))
        side = jnp.where(even, top_side, packed[1][1] * (1.0 / 1024.0))
        edges = jnp.where(lane == 2 * k, shift_x(side, 2 * k - 18), edges)
        edges = jnp.where(lane == 2 * k + 1, shift_x(side, 2 * k + 1 - 85), edges)
    totals_ref[pl.ds(3 * TILE, TILE), :] = edges


def term_kernel(tile_ref, state_ref, corner_ref, corner_speed_ref, terms_ref):
    lane = lanes()
    bottom, top = level_edges()

    def terms(place, d):
        speed = [state_ref[place + 1, SPEED + k] for k in range(3)]
        return subgrid_terms(lambda k: tile_ref[place, k], speed, d)

    corner_speed = [corner_speed_ref[k] for k in range(3)]
    corner = [subgrid_terms(lambda k: corner_ref[k], corner_speed, d) for d in range(3)]
    corner[2] = [shift_x(value, -SPAN) - shift_x(value, SPAN) for value in corner[2]]

    def patched(value, side, zz):
        value = jnp.where(lane == 0, shift_x(side, -19 - SPAN * zz), value)
        return jnp.where(lane == LANES - 1, shift_x(side, 43 - SPAN * zz), value)

    for zz in range(ROWS):
        row = zz + 1
        along_x, along_y = terms(row, 0), terms(row, 1)
        before, after = terms(row - 1, 2), terms(row + 1, 2)
        for n in range(TERMS):
            right = shift_x(corner[0][n], 42 - SPAN * zz)
            left = shift_x(corner[0][n], -18 - SPAN * zz)
            terms_ref[zz, n, 0] = jnp.where(lane >= LANES - 2, right, shift_x(along_x[n], -1))
            terms_ref[zz, n, 1] = jnp.where(lane < 2, left, shift_x(along_x[n], 1))
            terms_ref[zz, n, 2] = patched(after[n] - before[n], corner[2][n], zz)
            along = patched(along_y[n], corner[1][n], zz)
            terms_ref[zz, n, 3] = jnp.where(top, along, shift_s(along, -2))
            terms_ref[zz, n, 4] = jnp.where(bottom, -along, shift_s(along, 2))


def final_kernel(*refs, parts):
    part_refs = refs[:parts]
    base_ref, terms_ref, out_ref, coefficient_ref, scratch = refs[parts:]
    lane = lanes()
    even = is_even()
    bottom, top = level_edges()
    totals = [
        (tile_of(part_refs[0], k) + tile_of(part_refs[1], k))
        + (tile_of(part_refs[2], k) + tile_of(part_refs[3], k))
        for k in range(4)
    ]
    ratios = []
    for total in totals:
        total = total * (1.0 / (TILE * lax.axis_size("gz")))
        numerator = jnp.where(even, total, shift_s(total, 1))
        denominator = jnp.where(even, shift_s(total, -1), total)
        ratios.append(numerator / (denominator + RATIO_EPSILON))
    column = lax.axis_index("gx")
    first, last = column == 0, column == lax.axis_size("gx") - 1
    here, ahead, behind, above, below = [], [], [], [], []
    for k in range(3):
        ratio = ratios[k]
        scratch[...] = ratio
        coefficient_ref[k] = scratch[pl.ds(0, 4, stride=2), :]
        before = jnp.where(first, ratio, shift_x(ratios[3], -2 * k))
        after = jnp.where(last, ratio, shift_x(ratios[3], 127 - (2 * k + 1)))
        ratio = 0.25 * ratio
        here.append(ratio)
        ahead.append(jnp.where(lane == LANES - 1, 0.25 * after, shift_x(ratio, -1)))
        behind.append(jnp.where(lane == 0, 0.25 * before, shift_x(ratio, 1)))
        above.append(2.0 * jnp.where(top, ratio, shift_s(ratio, -2)))
        below.append(2.0 * jnp.where(bottom, ratio, shift_s(ratio, 2)))

    def row(zz, carry):
        sums = [tile_of(base_ref, field * ROWS + zz) for field in range(NF)]
        for n in range(TERMS):
            k = TERM_MODEL[n]
            change = (
                (ahead[k] * terms_ref[zz, n, 0] - behind[k] * terms_ref[zz, n, 1])
                + here[k] * terms_ref[zz, n, 2]
                + (above[k] * terms_ref[zz, n, 3] - below[k] * terms_ref[zz, n, 4])
            )
            sums[TERM_FIELD[n]] = sums[TERM_FIELD[n]] + change
        for field in range(NF):
            out_ref[pl.ds(field * 32 + zz, TILE, stride=4), :] = sums[field]
        return carry

    lax.fori_loop(0, ROWS, row, 0)


def call(kernel, out_shapes, scratch=(), inputs=0):
    run = pl.pallas_call(
        kernel,
        out_shape=[pltpu.VMEM(shape, F32) for shape in out_shapes],
        in_specs=[VMEM] * inputs,
        out_specs=[VMEM] * len(out_shapes),
        scratch_shapes=[pltpu.VMEM(shape, F32) for shape in scratch],
        compiler_params=SMALL,
    )
    return lambda *args: run(*in_vmem(args))


def in_vmem(args):
    return [pltpu.with_memory_space_constraint(arg, pltpu.VMEM) for arg in args]


def body(constituent_mass, flow_speeds, thermal_pair, blowing_indicator):
    count_x = lax.axis_size("gx")
    count_z = lax.axis_size("gz")

    def swap(axis, count, near):
        step = [1, -1] if near else [-1, 1]
        return lambda value: lax.ppermute(
            value, axis, [(i, (i + step[i % 2]) % count) for i in range(count)]
        )

    arrays = [
        value.reshape(-1, LANES) for value in (constituent_mass, flow_speeds, thermal_pair)
    ]
    packed = (PACK_ROWS, LANES)
    rows = (GROUPS * TILE, LANES)
    fields = (NF, TILE, LANES)
    own, far, near, blown = pl.pallas_call(
        pack_kernel,
        out_shape=[
            pltpu.VMEM(shape, F32)
            for shape in (
                rows, (MAIN_ROWS, LANES), (MAIN_ROWS, LANES), (4 * TILE, LANES),
            )
        ],
        in_specs=[pl.BlockSpec(memory_space=pltpu.HBM)] * 4,
        out_specs=[VMEM] * 4,
        scratch_shapes=[
            pltpu.VMEM((NF * 4 * TILE, LANES), F32),
            pltpu.VMEM(blowing_indicator.shape, jnp.int32),
            pltpu.SemaphoreType.DMA((4,)),
        ],
        compiler_params=SMALL,
    )(*[
        pltpu.with_memory_space_constraint(value, pltpu.HBM)
        for value in arrays + [blowing_indicator]
    ])
    far = swap("gz", count_z, False)(far)
    near = swap("gz", count_z, True)(near)
    face, part = call(stream_kernel, [rows, rows], inputs=2)(own, blown)
    (corner,) = call(own_corner_kernel, [fields], inputs=1)(own)
    far, near, face, part, corner = lax.optimization_barrier((far, near, face, part, corner))

    corner, one, other = call(
        corner_pack_kernel,
        [fields, packed, packed],
        inputs=3,
    )(corner, far, near)
    got_one = swap("gx", count_x, True)(one)
    got_other = swap("gx", count_x, False)(other)
    sums, clamped, tiles, state, raw = call(
        model_kernel,
        [
            (6, TILE, LANES),
            fields,
            (GRID_ROWS, TILES, TILE, LANES),
            (STATE_ROWS, STATE_COUNT, TILE, LANES),
            (SPAN_TILES, NF, TILE, LANES),
        ],
        scratch=[(GRID_ROWS, 4, TILE, LANES), (GRID_ROWS, 8, TILE, LANES)],
        inputs=4,
    )(own, far, near, corner)
    got_one, got_other, sums = lax.optimization_barrier((got_one, got_other, sums))
    totals, corner, corner_tiles, corner_speed = call(
        corner_kernel,
        [(4 * TILE, LANES), fields, (TILES, TILE, LANES), (3, TILE, LANES)],
        inputs=4,
    )(clamped, got_one, got_other, sums)

    (terms,) = call(term_kernel, [(ROWS, TERMS, 5, TILE, LANES)], inputs=4)(
        tiles, state, corner_tiles, corner_speed
    )
    (part,) = call(ends_kernel, [rows], inputs=3)(corner, face, part)
    (base,) = call(
        span_kernel,
        [rows],
        scratch=[
            (SPAN_TILES, NF, TILE, LANES), (SPAN_TILES, NF, TILE, LANES), (SPAN_TILES, TILE, LANES),
        ],
        inputs=2,
    )(raw, part)

    def crossed(value, mask):
        return lax.ppermute(value, "gz", [(i, i ^ mask) for i in range(count_z)])

    totals = totals + crossed(totals, 1)
    reach = 2
    while count_z > 4 * reach:
        a, b, c = (crossed(totals, k * reach) for k in (1, 2, 3))
        totals = (totals + a) + (b + c)
        reach *= 4
    parts = [totals] + [
        crossed(totals, k * reach) if k * reach < count_z else jnp.zeros_like(totals)
        for k in (2, 3, 1)
    ]

    def final(*refs):
        final_kernel(*refs, parts=4)

    tendency, coefficients = pl.pallas_call(
        final,
        out_shape=[jax.ShapeDtypeStruct(shape, F32) for shape in ((NF * 32, LANES), (3, 4, LANES))],
        in_specs=[VMEM] * 6,
        out_specs=[VMEM] * 2,
        scratch_shapes=[pltpu.VMEM((TILE, LANES), F32)],
        compiler_params=SMALL,
    )(*in_vmem(parts + [base, terms]))
    return tendency.reshape(NF, 4, TILE, LANES), coefficients


def solution(mesh):
    placed = (
        P(None, None, "gz", "gx"),
        P(None, None, "gz", "gx"),
        P(None, None, "gz", "gx"),
        P("gz", "gx"),
    )
    return jax.shard_map(
        body,
        mesh=mesh,
        in_specs=placed,
        out_specs=(P(None, None, "gz", "gx"), P(None, None, "gx")),
        check_vma=False,
    )
```

```python
import jax
import jax.numpy as jnp
from jax import lax
from jax.experimental import pallas as pl
from jax.experimental.pallas import tpu as pltpu
from jax.sharding import PartitionSpec as P


NSP = 5
NF = 10
ROWS = 4
TILE = 8
LANES = 128
HALO = 3
SPAN = 8
LAST = LANES - 5
GROUPS = NF * ROWS
PAIRS = NF // 2
PACKS = 3
PACK_ROWS = PACKS * TILE
MAIN_ROWS = PAIRS * HALO * TILE

HEAT_RATIO = 1.4
FILTER_SQUARE = 0.5 ** (2.0 / 3.0)
TEST_SQUARE = 2.0 ** (2.0 / 3.0)
FORMATION = (0.0, 0.0, 0.1, 0.5, 0.25)
BLOWING = 0.3
SMOOTH_FLOOR = 0.01
RATIO_EPSILON = 1e-06

VMEM = pl.BlockSpec(memory_space=pltpu.VMEM)
F32 = jnp.float32
SMALL = pltpu.CompilerParams(vmem_limit_bytes=8 << 20)


def lanes():
    return lax.broadcasted_iota(jnp.int32, (TILE, LANES), 1)


def sublanes():
    return lax.broadcasted_iota(jnp.int32, (TILE, LANES), 0)


def shift_x(tile, step):
    if isinstance(step, int):
        step = step % LANES
        if step == 0:
            return tile
    return pltpu.roll(tile, step, 1)


def shift_s(tile, step):
    return pltpu.roll(tile, step % TILE, 0)


def is_even():
    return (sublanes() & 1) == 0


def level_edges():
    level = sublanes() >> 1
    return level == 0, level == 3


def slot_of(index):
    start = index * TILE
    return pl.ds(start if isinstance(index, int) else pl.multiple_of(start, TILE), TILE)


def tile_of(ref, index):
    return ref[slot_of(index), :]


def is_first_of_pair(axis):
    return (lax.axis_index(axis) & 1) == 0


def halo_tile(far_ref, near_ref, below, index):
    first, second = (far_ref, near_ref) if below else (near_ref, far_ref)
    return jnp.where(is_first_of_pair("gz"), tile_of(first, index), tile_of(second, index))


def pack_kernel(
    mass_hbm, speed_hbm, heat_hbm, blow_hbm, own_ref, far_ref, near_ref, blow_rows,
    given_ref, blow_ref, arrived
):
    start, copies = 0, []
    for k, source in enumerate((mass_hbm, speed_hbm, heat_hbm)):
        target = given_ref.at[pl.ds(start, source.shape[0])]
        copies.append(pltpu.make_async_copy(source, target, arrived.at[k]))
        start += source.shape[0]
    copies.append(pltpu.make_async_copy(blow_hbm, blow_ref, arrived.at[3]))
    for copy in copies:
        copy.start()
    for copy in copies:
        copy.wait()
    even = is_even()
    first_core = is_first_of_pair("gz")
    tiles = {}
    for field in range(NF):
        for zz in range(ROWS):
            tile = given_ref[pl.ds(field * 32 + zz, TILE, stride=4), :]
            tiles[field, zz] = tile
            own_ref[slot_of(field * ROWS + zz), :] = tile
        if field % 2:
            for k in range(HALO):
                up = jnp.where(even, shift_s(tiles[field - 1, k + 1], -1), tiles[field, k + 1])
                down = jnp.where(even, tiles[field, k], shift_s(tiles[field - 1, k], 1))
                slot = slot_of(field // 2 * HALO + k)
                far_ref[slot, :] = jnp.where(first_core, down, up)
                near_ref[slot, :] = jnp.where(first_core, up, down)
    for level in range(4):
        blow_rows[pl.ds(level * TILE, TILE), :] = blow_ref[...].astype(F32)


def gather_rows(own_ref, far_ref, near_ref, raw_ref):
    even = is_even()
    for field in range(NF):
        pair, second = divmod(field, 2)
        own = [tile_of(own_ref, field * ROWS + zz) for zz in range(ROWS)]
        for zz in range(ROWS):
            raw_ref[zz + HALO, field] = own[zz]
        for k in range(HALO):
            low = halo_tile(far_ref, near_ref, True, pair * HALO + k)
            high = halo_tile(far_ref, near_ref, False, pair * HALO + k)
            if second:
                low, high = shift_s(low, -1), shift_s(high, 1)
            raw_ref[k, field] = jnp.where(even, low, shift_s(own[k + 1], 1))
            raw_ref[k + HALO + ROWS, field] = jnp.where(even, shift_s(own[k], -1), high)


def own_corner_kernel(own_ref, corner_ref):
    lane = lanes()
    within = lane & 63
    for field in range(NF):
        tile = None
        for side in range(2):
            for zz in range(ROWS):
                start = 64 * side + SPAN * (zz + 2)
                moved = shift_x(
                    tile_of(own_ref, field * ROWS + zz), start - LAST if side else start + HALO
                )
                tile = moved if tile is None else jnp.where(lane >= start, moved, tile)
        low, high = shift_s(shift_x(tile, -32), 1), shift_s(shift_x(tile, 32), -1)
        corner_ref[field] = jnp.where(within < 16, low, jnp.where(within >= 48, high, tile))


def corner_pack_kernel(own_corner_ref, far_ref, near_ref, corner_ref, right_ref, left_ref):
    lane = lanes()
    even = is_even()
    within = lane & 63
    halo = (even & (within < 16)) | (jnp.logical_not(even) & (within >= 48))
    corners = []
    for pair in range(PAIRS):
        rows = [
            (SPAN * (zz + 2), halo_tile(far_ref, near_ref, zz < 0, pair * HALO + zz % 4 - (zz < 0)))
            for zz in (-2, -1, 4, 5)
        ]
        tile = None
        for side in range(2):
            for start, row in rows:
                start += 64 * side
                moved = shift_x(row, start - LAST if side else start + HALO)
                tile = moved if tile is None else jnp.where(lane >= start, moved, tile)
        swapped = jnp.where(within < 32, shift_s(tile, -1), shift_s(tile, 1))
        for n, got in enumerate((tile, swapped)):
            corners.append(jnp.where(halo, got, own_corner_ref[2 * pair + n]))
            corner_ref[2 * pair + n] = corners[-1]
    ahead = (lane & (SPAN - 1)) < HALO

    def packed(group, move):
        halves = [
            jnp.where(
                ahead, shift_x(group[n], 32 * n + move), shift_x(group[n + 1], 32 * n + HALO + move)
            )
            for n in range(0, len(group), 2)
        ]
        return halves[0] if len(halves) == 1 else jnp.where(lane < 64, *halves)

    for k in range(PACKS):
        group = corners[4 * k : 4 * k + 4]
        to_left, to_right = packed(group, -3), packed(group, -66)
        right_ref[slot_of(k), :] = to_right
        left_ref[slot_of(k), :] = to_left


def state_of(fields):
    mass, motion = fields[:NSP], fields[NSP : NSP + 3]
    thermal, vibration = fields[NSP + 3], fields[NSP + 4]
    density = (mass[0] + mass[1]) + (mass[2] + mass[3]) + mass[4]
    formed = FORMATION[2] * mass[2] + FORMATION[3] * mass[3] + FORMATION[4] * mass[4]
    motion_square = motion[0] * motion[0] + motion[1] * motion[1] + motion[2] * motion[2]
    energy = density * (2.5 * thermal + vibration + 0.5 * motion_square) + formed
    conserved = (
        list(mass) + [density * speed for speed in motion] + [energy, density * vibration]
    )
    return density, density * thermal, jnp.sqrt(HEAT_RATIO * thermal), conserved


def flux_of(conserved, pressure, speed, component):
    flux = [value * speed for value in conserved]
    flux[NSP + component] = flux[NSP + component] + pressure
    flux[NSP + 3] = flux[NSP + 3] + pressure * speed
    return flux


def correction(d0, d1, d2, d3):
    floor = 4.0 * SMOOTH_FLOOR * 12.0 / 13.0
    share = 3.0 / 13.0
    e0, e1, e2 = d1 - d0, d2 - d1, d3 - d2
    g0, g1, g2 = e0 + (d1 + d1), d1 + d2, e2 - (d2 + d2)
    b0 = (e0 * e0 + floor) + share * (g0 * g0)
    b1 = (e1 * e1 + floor) + share * (g1 * g1)
    b2 = (e2 * e2 + floor) + share * (g2 * g2)
    p0, p1, p2 = b1 * b2, b0 * b2, b0 * b1
    w0 = p0 * p0
    w1 = 6.0 * (p1 * p1)
    w2 = 3.0 * (p2 * p2)
    r0 = 5.0 * d1 - (d0 + d0)
    r1 = d1 + (d2 + d2)
    r2 = 4.0 * d2 - d3
    return (w0 * r0 + w1 * r1 + w2 * r2) / (w0 + w1 + w2)


def face_flux(here, slopes, jumps, signal):
    waves = [signal * jump for jump in jumps]
    plus = [slopes[k] + waves[k] for k in range(4)]
    minus = [waves[k] - slopes[k] for k in range(1, 5)]
    gain = correction(*plus)
    loss = correction(minus[3], minus[2], minus[1], minus[0])
    return here + 0.5 * (slopes[2] - waves[2]) + (gain + loss) * (1.0 / 12.0)


def faces_along_x(flux, conserved, signal):
    slope = shift_x(flux, -1) - flux
    jump = shift_x(conserved, -1) - conserved
    slopes = [shift_x(slope, -k) for k in range(-2, 3)]
    jumps = [shift_x(jump, -k) for k in range(-2, 3)]
    return face_flux(flux, slopes, jumps, signal)


def stream_kernel(own_ref, blow_rows, face_ref, part_ref):
    bottom, top = level_edges()

    def row(zz, carry):
        fields = [tile_of(own_ref, field * ROWS + zz) for field in range(NF)]
        density, pressure, sound, conserved = state_of(fields)
        speed = fields[NSP]
        flux = flux_of(conserved, pressure, speed, 0)
        signal = jnp.abs(speed) + sound
        signal = jnp.maximum(signal, shift_x(signal, -1))

        normal_speed = fields[NSP + 1]
        normal_flux = flux_of(conserved, pressure, normal_speed, 1)
        normal_signal = jnp.abs(normal_speed) + sound
        normal_signal = 0.5 * jnp.maximum(normal_signal, shift_s(normal_signal, -2))
        blown = BLOWING * blow_rows[pl.ds(zz, TILE, stride=4), :]
        lift = blown / density
        enthalpy = 3.5 * fields[NSP + 3] + fields[NSP + 4] + 0.5 * lift * lift
        wall = [lift * fields[s] for s in range(NSP)]
        formed = FORMATION[2] * wall[2] + FORMATION[3] * wall[3] + FORMATION[4] * wall[4]
        zero = jnp.zeros((TILE, LANES), F32)
        wall = wall + [
            zero, blown * lift + pressure, zero, blown * enthalpy + formed, blown * fields[NSP + 4]
        ]
        relaxation = 2.0 * density * (fields[NSP + 3] - fields[NSP + 4])
        for field in range(NF):
            value, normal = conserved[field], normal_flux[field]
            slot = slot_of(field * ROWS + zz)
            face_ref[slot, :] = faces_along_x(flux[field], value, signal)
            above = shift_s(value, -2)
            level_face = 0.5 * (normal + shift_s(normal, -2)) - normal_signal * (above - value)
            level_face = jnp.where(top, normal, level_face)
            change = 2.0 * (jnp.where(bottom, wall[field], shift_s(level_face, 2)) - level_face)
            part_ref[slot, :] = change + relaxation if field == NF - 1 else change
        return carry

    lax.fori_loop(0, ROWS, row, 0)


def ends_kernel(corner_ref, face_ref, part_ref, out_ref):
    lane = lanes()
    fields = [corner_ref[field] for field in range(NF)]
    density, pressure, sound, conserved = state_of(fields)
    flux = flux_of(conserved, pressure, fields[NSP], 0)
    signal = jnp.abs(fields[NSP]) + sound
    signal = jnp.maximum(signal, shift_x(signal, -1))
    for field in range(NF):
        end_face = faces_along_x(flux[field], conserved[field], signal)
        for zz in range(ROWS):
            left = shift_x(end_face, 109 - SPAN * zz)
            right = shift_x(end_face, 43 - SPAN * zz)
            slot = slot_of(field * ROWS + zz)
            face = jnp.where(
                lane < 2, left, jnp.where(lane >= LANES - 3, right, face_ref[slot, :])
            )
            before = shift_x(jnp.where(lane == LANES - 1, left, face), 1)
            out_ref[slot, :] = part_ref[slot, :] + (before - face)


SPAN_TILES = ROWS + 2 * HALO


def span_kernel(raw_ref, part_ref, out_ref, value_ref, flux_ref, signal_ref):
    for place in range(SPAN_TILES):
        fields = [raw_ref[place, field] for field in range(NF)]
        _, pressure, sound, conserved = state_of(fields)
        speed = fields[NSP + 2]
        flux = flux_of(conserved, pressure, speed, 2)
        signal_ref[place] = jnp.abs(speed) + sound
        for field in range(NF):
            value_ref[place, field] = conserved[field]
            flux_ref[place, field] = flux[field]

    def faces_of(place):
        signal = jnp.maximum(signal_ref[place], signal_ref[place + 1])
        faces = []
        for field in range(NF):
            flux = [flux_ref[place + k, field] for k in range(-2, 4)]
            value = [value_ref[place + k, field] for k in range(-2, 4)]
            slopes = [flux[k + 1] - flux[k] for k in range(5)]
            jumps = [value[k + 1] - value[k] for k in range(5)]
            faces.append(face_flux(flux[2], slopes, jumps, signal))
        return tuple(faces)

    def row(zz, before):
        faces = faces_of(zz + HALO)
        for field in range(NF):
            slot = slot_of(field * ROWS + zz)
            out_ref[slot, :] = part_ref[slot, :] + (before[field] - faces[field])
        return faces

    lax.fori_loop(0, ROWS, row, faces_of(HALO - 1))


MASS, MOMENTUM, HEAT = 0, 5, 8
SPEED, THERMAL, VIBRATION, FRACTION, DENSITY = 9, 12, 13, 14, 19
STATE_COUNT = 20
SLOPED = 10
STATE_ROWS = 8
GRID_ROWS = 6
PAIR_INDEX = ((0, 0), (1, 1), (0, 1), (0, 2), (1, 2), (2, 2))

PRODUCT, STRESS, HEAT_FLUX, HEAT_SLOPE, MASS_FLUX, MASS_SLOPE = 0, 6, 11, 14, 17, 29
LAST_STRESS = 41
FILTERED = 42
SIDE_SLOPE = FILTERED
TILES = FILTERED + 3

TERMS = 12
TERM_FIELD = (0, 1, 2, 3, 4, 5, 6, 7, 8, 8, 8, 9)
TERM_MODEL = (2, 2, 2, 2, 2, 0, 0, 0, 0, 1, 2, 1)


def model_state(fields):
    mass, motion = fields[:NSP], fields[NSP : NSP + 3]
    thermal, vibration = fields[NSP + 3], fields[NSP + 4]
    density = (mass[0] + mass[1]) + (mass[2] + mass[3]) + mass[4]
    inverse = 1.0 / density
    fraction = [m * inverse for m in mass]
    return (
        list(mass)
        + [density * speed for speed in motion]
        + [density * thermal]
        + list(motion)
        + [thermal, vibration]
        + fraction
        + [density]
    )


def level_slope(value, scale):
    bottom, top = level_edges()
    above = jnp.where(top, value, shift_s(value, -2))
    below = jnp.where(bottom, value, shift_s(value, 2))
    return scale * (above - below)


def strain(slopes):
    diagonal = [2.0 * slopes[k][k] for k in range(3)]
    third = (diagonal[0] + diagonal[1] + diagonal[2]) * (1.0 / 3.0)
    first, second = diagonal[0] - third, diagonal[1] - third
    mixed = [slopes[0][1] + slopes[1][0], slopes[0][2] + slopes[2][0], slopes[1][2] + slopes[2][1]]
    last = diagonal[2] - third
    square = (
        first * first + second * second + last * last
        + 2.0 * (mixed[0] * mixed[0] + mixed[1] * mixed[1] + mixed[2] * mixed[2])
    )
    magnitude = jnp.sqrt(0.125 * square + 1e-06)
    return [first, second] + mixed + [last], magnitude


def grid_terms(here, slopes):
    deviator, magnitude = strain(slopes[:3])
    eddy = FILTER_SQUARE * here(DENSITY) * magnitude
    speed = [here(SPEED + k) for k in range(3)]
    momentum = [here(MOMENTUM + k) for k in range(3)]
    thermal = here(THERMAL)
    stress = [eddy * part for part in deviator]
    tiles = [momentum[i] * speed[j] for i, j in PAIR_INDEX]
    tiles += stress[:5]
    tiles += [m * thermal for m in momentum]
    tiles += [eddy * slopes[3][d] for d in range(3)]
    tiles += [here(MASS + s) * speed[d] for s in range(4) for d in range(3)]
    tiles += [eddy * slopes[5 + s][d] for s in range(4) for d in range(3)]
    tiles.append(stress[5])
    return tiles + [eddy * slopes[4][d] for d in range(3)]


def subgrid_terms(tile, speed, d):
    places = (STRESS, STRESS + 1, STRESS + 2, STRESS + 3, STRESS + 4, LAST_STRESS)
    full = ((0, 2, 3), (2, 1, 4), (3, 4, 5))
    tau = [tile(places[full[i][d]]) for i in range(3)]
    species = [tile(MASS_SLOPE + 3 * s + d) for s in range(4)]
    species.append(-((species[0] + species[1]) + (species[2] + species[3])))
    work = speed[0] * tau[0] + speed[1] * tau[1] + speed[2] * tau[2]
    vibration = tile(SIDE_SLOPE + d)
    heat = 3.5 * tile(HEAT_SLOPE + d) + vibration
    formed = FORMATION[2] * species[2] + FORMATION[3] * species[3] + FORMATION[4] * species[4]
    return species + tau + [work, heat, formed, vibration]


def favre(hat):
    density = (hat[0] + hat[1]) + (hat[2] + hat[3]) + hat[4]
    inverse = 1.0 / density
    return density, [hat[5 + k] * inverse for k in range(3)], hat[8] * inverse, [
        hat[s] * inverse for s in range(4)
    ]


def contractions(hat, density, momentum, favre_here, slopes):
    speed, thermal, fraction = favre_here
    deviator, magnitude = strain(slopes[:3])
    eddy = TEST_SQUARE * density * magnitude
    stress = [hat(STRESS + n) for n in range(5)] + [hat(LAST_STRESS)]
    sums = []
    top = bottom = None

    def add(total, value):
        return value if total is None else total + value

    off_top = off_bottom = None
    for n, (i, j) in enumerate(PAIR_INDEX):
        resolved = hat(PRODUCT + n) - momentum[i] * speed[j]
        model = stress[n] - eddy * deviator[n]
        if i == j:
            top, bottom = add(top, resolved * model), add(bottom, model * model)
        else:
            off_top, off_bottom = add(off_top, resolved * model), add(off_bottom, model * model)
    sums += [top + (off_top + off_top), bottom + (off_bottom + off_bottom)]
    top = bottom = None
    for d in range(3):
        resolved = hat(HEAT_FLUX + d) - momentum[d] * thermal
        model = hat(HEAT_SLOPE + d) - eddy * slopes[3][d]
        top, bottom = add(top, resolved * model), add(bottom, model * model)
    sums += [top, bottom]
    top = bottom = None
    for d in range(3):
        last_resolved = last_model = None
        for s in range(4):
            resolved = hat(MASS_FLUX + 3 * s + d) - momentum[d] * fraction[s]
            model = hat(MASS_SLOPE + 3 * s + d) - eddy * slopes[4 + s][d]
            last_resolved, last_model = add(last_resolved, resolved), add(last_model, model)
            top, bottom = add(top, resolved * model), add(bottom, model * model)
        top, bottom = top + last_resolved * last_model, bottom + last_model * last_model
    return sums + [top, bottom]


def filter_x(tile):
    pair = tile + shift_x(tile, -1)
    return pair + shift_x(pair, 1)


def slope_scale():
    bottom, top = level_edges()
    return jnp.where(bottom | top, 4.0, 2.0)


def model_kernel(
    own_ref, far_ref, near_ref, corner_own_ref,
    sum_ref, clamped_ref, tile_ref, state_ref, raw_ref,
    wide_ref, favre_ref,
):
    scale = slope_scale()
    gather_rows(own_ref, far_ref, near_ref, raw_ref)
    for row in range(STATE_ROWS):
        states = model_state([raw_ref[row + 1, field] for field in range(NF)])
        for k in range(STATE_COUNT):
            state_ref[row, k] = states[k]

    def grid_row(row, carry):
        def here(k):
            return state_ref[row + 1, k]

        slopes = []
        for k in range(SLOPED - 1):
            value = here(SPEED + k)
            along_x = shift_x(value, -1) - shift_x(value, 1)
            along_z = state_ref[row + 2, SPEED + k] - state_ref[row, SPEED + k]
            slopes.append((along_x, level_slope(value, scale), along_z))
        for k, tile in enumerate(grid_terms(here, slopes)):
            tile_ref[row, k] = tile
        hat = []
        for k in range(SPEED):
            total = (state_ref[row, k] + state_ref[row + 2, k]) + 2.0 * here(k)
            hat.append(filter_x(total))
        density, speed, thermal, fraction = favre(hat)
        for k, value in enumerate(speed + [thermal] + fraction):
            favre_ref[row, k] = value
        for k in range(3):
            wide_ref[row, k] = hat[MOMENTUM + k]
        wide_ref[row, 3] = density
        return carry

    lax.fori_loop(0, GRID_ROWS, grid_row, 0)
    for k in range(6):
        sum_ref[k] = jnp.zeros((TILE, LANES), F32)

    def test_row(zz, carry):
        row = zz + 1

        def hat(k):
            total = (tile_ref[row - 1, k] + tile_ref[row + 1, k]) + 2.0 * tile_ref[row, k]
            return filter_x(total)

        slopes = []
        for k in range(8):
            value = favre_ref[row, k]
            along_x = shift_x(value, -1) - shift_x(value, 1)
            along_z = favre_ref[row + 1, k] - favre_ref[row - 1, k]
            slopes.append((along_x, level_slope(value, scale), along_z))
        values = [favre_ref[row, k] for k in range(8)]
        sums = contractions(
            hat, wide_ref[row, 3], [wide_ref[row, k] for k in range(3)],
            (values[:3], values[3], values[4:]), slopes,
        )
        for k in range(6):
            sum_ref[k] = sum_ref[k] + sums[k]
        return carry

    lax.fori_loop(0, ROWS, test_row, 0)

    on_left = lanes() < 64
    place = lanes() & (SPAN - 1)
    place = jnp.where(on_left, place, SPAN - 1 - place)
    for field in range(NF):
        tile = clamped = corner_own_ref[field]
        for c in range(HALO):
            copied = jnp.where(on_left, shift_x(tile, c - HALO), shift_x(tile, HALO - c))
            clamped = jnp.where(place == c, copied, clamped)
        clamped_ref[field] = clamped


def corner_kernel(
    clamped_ref, got_left_ref, got_right_ref, sum_ref,
    totals_ref, corner_ref, tile_ref, speed_ref
):
    lane = lanes()
    even = is_even()
    scale = slope_scale()
    column = lax.axis_index("gx")
    first, last = column == 0, column == lax.axis_size("gx") - 1
    place = lane & (SPAN - 1)
    on_left = lane < 64
    low, high = jnp.where(first, 0, HALO), jnp.where(last, SPAN, SPAN - HALO)
    halo = (on_left & (place < low)) | (jnp.logical_not(on_left) & (place >= high))
    fields = []
    for field in range(NF):
        k, j = divmod(field, 4)
        if j == 0:
            from_left, from_right = tile_of(got_left_ref, k), tile_of(got_right_ref, k)
        move = 64 * (j // 2) + HALO * (j % 2)
        got = jnp.where(on_left, shift_x(from_left, -move), shift_x(from_right, 69 - move))
        fields.append(jnp.where(halo, got, clamped_ref[field]))
        corner_ref[field] = fields[field]
    state = model_state(fields)

    def slopes_of(value):
        along_x = shift_x(value, -1) - shift_x(value, 1)
        along_z = shift_x(value, -SPAN) - shift_x(value, SPAN)
        return along_x, level_slope(value, scale), along_z

    def filtered(value):
        pair = value + shift_x(value, -SPAN)
        return filter_x(pair + shift_x(pair, SPAN))

    tiles = grid_terms(lambda k: state[k], [slopes_of(state[SPEED + k]) for k in range(SLOPED - 1)])
    for k in range(STRESS, TILES):
        tile_ref[k] = tiles[k]
    for k in range(3):
        speed_ref[k] = state[SPEED + k]
    wide = [filtered(state[k]) for k in range(SPEED)]
    density, speed, thermal, fraction = favre(wide)
    sums = contractions(
        lambda k: filtered(tiles[k]), density, wide[MOMENTUM : MOMENTUM + 3],
        (speed, thermal, fraction), [slopes_of(value) for value in speed + [thermal] + fraction],
    )
    main_totals, corner_totals = [sum_ref[k] for k in range(6)], []
    for value in sums:
        value = value + shift_x(value, -SPAN)
        corner_totals.append(value + shift_x(value, -2 * SPAN))
    edges = jnp.zeros((TILE, LANES), F32)
    for k in range(3):
        packed = []
        for main, side in zip(main_totals[2 * k : 2 * k + 2], corner_totals[2 * k : 2 * k + 2]):
            main = jnp.where(lane < 2, shift_x(side, -19), main)
            main = jnp.where(lane >= LANES - 2, shift_x(side, 126 - 83), main)
            packed.append((main + shift_s(main, 1), side + shift_s(side, 1), main, side))
        top_main = shift_s(packed[0][0], -1) * (1.0 / 512.0)
        top_side = shift_s(packed[0][1], -1) * (1.0 / 512.0)
        totals_ref[pl.ds(k * TILE, TILE), :] = jnp.where(even, top_main, packed[1][0] * (1.0 / 1024.0))
        side = jnp.where(even, top_side, packed[1][1] * (1.0 / 1024.0))
        edges = jnp.where(lane == 2 * k, shift_x(side, 2 * k - 18), edges)
        edges = jnp.where(lane == 2 * k + 1, shift_x(side, 2 * k + 1 - 85), edges)
    totals_ref[pl.ds(3 * TILE, TILE), :] = edges


def term_kernel(tile_ref, state_ref, corner_ref, corner_speed_ref, terms_ref):
    lane = lanes()
    bottom, top = level_edges()

    def terms(place, d):
        speed = [state_ref[place + 1, SPEED + k] for k in range(3)]
        return subgrid_terms(lambda k: tile_ref[place, k], speed, d)

    corner_speed = [corner_speed_ref[k] for k in range(3)]
    corner = [subgrid_terms(lambda k: corner_ref[k], corner_speed, d) for d in range(3)]
    corner[2] = [shift_x(value, -SPAN) - shift_x(value, SPAN) for value in corner[2]]

    def patched(value, side, zz):
        value = jnp.where(lane == 0, shift_x(side, -19 - SPAN * zz), value)
        return jnp.where(lane == LANES - 1, shift_x(side, 43 - SPAN * zz), value)

    for zz in range(ROWS):
        row = zz + 1
        along_x, along_y = terms(row, 0), terms(row, 1)
        before, after = terms(row - 1, 2), terms(row + 1, 2)
        for n in range(TERMS):
            right = shift_x(corner[0][n], 42 - SPAN * zz)
            left = shift_x(corner[0][n], -18 - SPAN * zz)
            terms_ref[zz, n, 0] = jnp.where(lane >= LANES - 2, right, shift_x(along_x[n], -1))
            terms_ref[zz, n, 1] = jnp.where(lane < 2, left, shift_x(along_x[n], 1))
            terms_ref[zz, n, 2] = patched(after[n] - before[n], corner[2][n], zz)
            along = patched(along_y[n], corner[1][n], zz)
            terms_ref[zz, n, 3] = jnp.where(top, along, shift_s(along, -2))
            terms_ref[zz, n, 4] = jnp.where(bottom, -along, shift_s(along, 2))


def final_kernel(*refs, parts):
    part_refs = refs[:parts]
    base_ref, terms_ref, out_ref, coefficient_ref, scratch = refs[parts:]
    lane = lanes()
    even = is_even()
    bottom, top = level_edges()
    totals = [
        (tile_of(part_refs[0], k) + tile_of(part_refs[1], k))
        + (tile_of(part_refs[2], k) + tile_of(part_refs[3], k))
        for k in range(4)
    ]
    ratios = []
    for total in totals:
        total = total * (1.0 / (TILE * lax.axis_size("gz")))
        numerator = jnp.where(even, total, shift_s(total, 1))
        denominator = jnp.where(even, shift_s(total, -1), total)
        ratios.append(numerator / (denominator + RATIO_EPSILON))
    column = lax.axis_index("gx")
    first, last = column == 0, column == lax.axis_size("gx") - 1
    here, ahead, behind, above, below = [], [], [], [], []
    for k in range(3):
        ratio = ratios[k]
        scratch[...] = ratio
        coefficient_ref[k] = scratch[pl.ds(0, 4, stride=2), :]
        before = jnp.where(first, ratio, shift_x(ratios[3], -2 * k))
        after = jnp.where(last, ratio, shift_x(ratios[3], 127 - (2 * k + 1)))
        ratio = 0.25 * ratio
        here.append(ratio)
        ahead.append(jnp.where(lane == LANES - 1, 0.25 * after, shift_x(ratio, -1)))
        behind.append(jnp.where(lane == 0, 0.25 * before, shift_x(ratio, 1)))
        above.append(2.0 * jnp.where(top, ratio, shift_s(ratio, -2)))
        below.append(2.0 * jnp.where(bottom, ratio, shift_s(ratio, 2)))

    def row(zz, carry):
        sums = [tile_of(base_ref, field * ROWS + zz) for field in range(NF)]
        for n in range(TERMS):
            k = TERM_MODEL[n]
            change = (
                (ahead[k] * terms_ref[zz, n, 0] - behind[k] * terms_ref[zz, n, 1])
                + here[k] * terms_ref[zz, n, 2]
                + (above[k] * terms_ref[zz, n, 3] - below[k] * terms_ref[zz, n, 4])
            )
            sums[TERM_FIELD[n]] = sums[TERM_FIELD[n]] + change
        for field in range(NF):
            out_ref[pl.ds(field * 32 + zz, TILE, stride=4), :] = sums[field]
        return carry

    lax.fori_loop(0, ROWS, row, 0)


def call(kernel, out_shapes, scratch=(), inputs=0):
    run = pl.pallas_call(
        kernel,
        out_shape=[pltpu.VMEM(shape, F32) for shape in out_shapes],
        in_specs=[VMEM] * inputs,
        out_specs=[VMEM] * len(out_shapes),
        scratch_shapes=[pltpu.VMEM(shape, F32) for shape in scratch],
        compiler_params=SMALL,
    )
    return lambda *args: run(*in_vmem(args))


def in_vmem(args):
    return [pltpu.with_memory_space_constraint(arg, pltpu.VMEM) for arg in args]


def body(constituent_mass, flow_speeds, thermal_pair, blowing_indicator):
    count_x = lax.axis_size("gx")
    count_z = lax.axis_size("gz")

    def swap(near):
        step = [1, -1] if near else [-1, 1]
        return lambda value: lax.ppermute(
            value, "gz", [(i, (i + step[i % 2]) % count_z) for i in range(count_z)]
        )

    def ring(step):
        return lambda value: lax.ppermute(
            value, "gx", [(i, (i + step) % count_x) for i in range(count_x)]
        )

    arrays = [
        value.reshape(-1, LANES) for value in (constituent_mass, flow_speeds, thermal_pair)
    ]
    packed = (PACK_ROWS, LANES)
    rows = (GROUPS * TILE, LANES)
    fields = (NF, TILE, LANES)
    own, far, near, blown = pl.pallas_call(
        pack_kernel,
        out_shape=[
            pltpu.VMEM(shape, F32)
            for shape in (
                rows, (MAIN_ROWS, LANES), (MAIN_ROWS, LANES), (4 * TILE, LANES),
            )
        ],
        in_specs=[pl.BlockSpec(memory_space=pltpu.HBM)] * 4,
        out_specs=[VMEM] * 4,
        scratch_shapes=[
            pltpu.VMEM((NF * 4 * TILE, LANES), F32),
            pltpu.VMEM(blowing_indicator.shape, jnp.int32),
            pltpu.SemaphoreType.DMA((4,)),
        ],
        compiler_params=SMALL,
    )(*[
        pltpu.with_memory_space_constraint(value, pltpu.HBM)
        for value in arrays + [blowing_indicator]
    ])
    far = swap(False)(far)
    near = swap(True)(near)
    face, part = call(stream_kernel, [rows, rows], inputs=2)(own, blown)
    (corner,) = call(own_corner_kernel, [fields], inputs=1)(own)
    far, near, face, part, corner = lax.optimization_barrier((far, near, face, part, corner))

    corner, to_right, to_left = call(
        corner_pack_kernel,
        [fields, packed, packed],
        inputs=3,
    )(corner, far, near)
    got_left = ring(1)(to_right)
    got_right = ring(-1)(to_left)
    sums, clamped, tiles, state, raw = call(
        model_kernel,
        [
            (6, TILE, LANES),
            fields,
            (GRID_ROWS, TILES, TILE, LANES),
            (STATE_ROWS, STATE_COUNT, TILE, LANES),
            (SPAN_TILES, NF, TILE, LANES),
        ],
        scratch=[(GRID_ROWS, 4, TILE, LANES), (GRID_ROWS, 8, TILE, LANES)],
        inputs=4,
    )(own, far, near, corner)
    got_left, got_right, sums = lax.optimization_barrier((got_left, got_right, sums))
    totals, corner, corner_tiles, corner_speed = call(
        corner_kernel,
        [(4 * TILE, LANES), fields, (TILES, TILE, LANES), (3, TILE, LANES)],
        inputs=4,
    )(clamped, got_left, got_right, sums)

    (terms,) = call(term_kernel, [(ROWS, TERMS, 5, TILE, LANES)], inputs=4)(
        tiles, state, corner_tiles, corner_speed
    )
    (part,) = call(ends_kernel, [rows], inputs=3)(corner, face, part)
    (base,) = call(
        span_kernel,
        [rows],
        scratch=[
            (SPAN_TILES, NF, TILE, LANES), (SPAN_TILES, NF, TILE, LANES), (SPAN_TILES, TILE, LANES),
        ],
        inputs=2,
    )(raw, part)

    def crossed(value, mask):
        return lax.ppermute(value, "gz", [(i, i ^ mask) for i in range(count_z)])

    totals = totals + crossed(totals, 1)
    reach = 2
    while count_z > 4 * reach:
        a, b, c = (crossed(totals, k * reach) for k in (1, 2, 3))
        totals = (totals + a) + (b + c)
        reach *= 4
    parts = [totals] + [
        crossed(totals, k * reach) if k * reach < count_z else jnp.zeros_like(totals)
        for k in (2, 3, 1)
    ]

    def final(*refs):
        final_kernel(*refs, parts=4)

    tendency, coefficients = pl.pallas_call(
        final,
        out_shape=[jax.ShapeDtypeStruct(shape, F32) for shape in ((NF * 32, LANES), (3, 4, LANES))],
        in_specs=[VMEM] * 6,
        out_specs=[VMEM] * 2,
        scratch_shapes=[pltpu.VMEM((TILE, LANES), F32)],
        compiler_params=SMALL,
    )(*in_vmem(parts + [base, terms]))
    return tendency.reshape(NF, 4, TILE, LANES), coefficients


def solution(mesh):
    placed = (
        P(None, None, "gz", "gx"),
        P(None, None, "gz", "gx"),
        P(None, None, "gz", "gx"),
        P("gz", "gx"),
    )
    return jax.shard_map(
        body,
        mesh=mesh,
        in_specs=placed,
        out_specs=(P(None, None, "gz", "gx"), P(None, None, "gx")),
        check_vma=False,
    )
```

```python
import jax
import jax.numpy as jnp
from jax import lax
from jax.experimental import pallas as pl
from jax.experimental.pallas import tpu as pltpu
from jax.sharding import PartitionSpec as P


NSP = 5
NF = 10
ROWS = 4
TILE = 8
LANES = 128
HALO = 3
SPAN = 8
LAST = LANES - 5
GROUPS = NF * ROWS
PAIRS = NF // 2
PACKS = 3
PACK_ROWS = PACKS * TILE
MAIN_ROWS = PAIRS * HALO * TILE

HEAT_RATIO = 1.4
FILTER_SQUARE = 0.5 ** (2.0 / 3.0)
TEST_SQUARE = 2.0 ** (2.0 / 3.0)
FORMATION = (0.0, 0.0, 0.1, 0.5, 0.25)
BLOWING = 0.3
SMOOTH_FLOOR = 0.01
RATIO_EPSILON = 1e-06

VMEM = pl.BlockSpec(memory_space=pltpu.VMEM)
F32 = jnp.float32
SMALL = pltpu.CompilerParams(vmem_limit_bytes=8 << 20)


def lanes():
    return lax.broadcasted_iota(jnp.int32, (TILE, LANES), 1)


def sublanes():
    return lax.broadcasted_iota(jnp.int32, (TILE, LANES), 0)


def shift_x(tile, step):
    if isinstance(step, int):
        step = step % LANES
        if step == 0:
            return tile
    return pltpu.roll(tile, step, 1)


def shift_s(tile, step):
    return pltpu.roll(tile, step % TILE, 0)


def is_even():
    return (sublanes() & 1) == 0


def level_edges():
    level = sublanes() >> 1
    return level == 0, level == 3


def slot_of(index):
    start = index * TILE
    return pl.ds(start if isinstance(index, int) else pl.multiple_of(start, TILE), TILE)


def tile_of(ref, index):
    return ref[slot_of(index), :]


def is_first_of_pair(axis):
    return (lax.axis_index(axis) & 1) == 0


def halo_tile(far_ref, near_ref, below, index):
    first, second = (far_ref, near_ref) if below else (near_ref, far_ref)
    return jnp.where(is_first_of_pair("gz"), tile_of(first, index), tile_of(second, index))


def pack_kernel(
    mass_hbm, speed_hbm, heat_hbm, blow_hbm, own_ref, far_ref, near_ref, blow_rows,
    given_ref, blow_ref, arrived
):
    start, copies = 0, []
    for k, source in enumerate((mass_hbm, speed_hbm, heat_hbm)):
        target = given_ref.at[pl.ds(start, source.shape[0])]
        copies.append(pltpu.make_async_copy(source, target, arrived.at[k]))
        start += source.shape[0]
    copies.append(pltpu.make_async_copy(blow_hbm, blow_ref, arrived.at[3]))
    for copy in copies:
        copy.start()
    for copy in copies:
        copy.wait()
    even = is_even()
    first_core = is_first_of_pair("gz")
    tiles = {}
    for field in range(NF):
        for zz in range(ROWS):
            tile = given_ref[pl.ds(field * 32 + zz, TILE, stride=4), :]
            tiles[field, zz] = tile
            own_ref[slot_of(field * ROWS + zz), :] = tile
        if field % 2:
            for k in range(HALO):
                up = jnp.where(even, shift_s(tiles[field - 1, k + 1], -1), tiles[field, k + 1])
                down = jnp.where(even, tiles[field, k], shift_s(tiles[field - 1, k], 1))
                slot = slot_of(field // 2 * HALO + k)
                far_ref[slot, :] = jnp.where(first_core, down, up)
                near_ref[slot, :] = jnp.where(first_core, up, down)
    for level in range(4):
        blow_rows[pl.ds(level * TILE, TILE), :] = blow_ref[...].astype(F32)


def gather_rows(own_ref, far_ref, near_ref, raw_ref):
    even = is_even()
    for field in range(NF):
        pair, second = divmod(field, 2)
        own = [tile_of(own_ref, field * ROWS + zz) for zz in range(ROWS)]
        for zz in range(ROWS):
            raw_ref[zz + HALO, field] = own[zz]
        for k in range(HALO):
            low = halo_tile(far_ref, near_ref, True, pair * HALO + k)
            high = halo_tile(far_ref, near_ref, False, pair * HALO + k)
            if second:
                low, high = shift_s(low, -1), shift_s(high, 1)
            raw_ref[k, field] = jnp.where(even, low, shift_s(own[k + 1], 1))
            raw_ref[k + HALO + ROWS, field] = jnp.where(even, shift_s(own[k], -1), high)


def own_corner_kernel(own_ref, corner_ref, filter_ref):
    shape = (LANES, LANES)
    source, target = (lax.broadcasted_iota(jnp.int32, shape, d) for d in range(2))

    def weight(a, b):
        apart = jnp.abs(a - b)
        return jnp.where(apart == 0, 2.0, jnp.where(apart == 1, 1.0, 0.0))

    along_x = weight(source & (SPAN - 1), target & (SPAN - 1))
    filter_ref[...] = along_x * weight(source >> 3, target >> 3)
    lane = lanes()
    within = lane & 63
    for field in range(NF):
        tile = None
        for side in range(2):
            for zz in range(ROWS):
                start = 64 * side + SPAN * (zz + 2)
                moved = shift_x(
                    tile_of(own_ref, field * ROWS + zz), start - LAST if side else start + HALO
                )
                tile = moved if tile is None else jnp.where(lane >= start, moved, tile)
        low, high = shift_s(shift_x(tile, -32), 1), shift_s(shift_x(tile, 32), -1)
        corner_ref[field] = jnp.where(within < 16, low, jnp.where(within >= 48, high, tile))


def corner_pack_kernel(own_corner_ref, far_ref, near_ref, corner_ref, right_ref, left_ref):
    lane = lanes()
    even = is_even()
    within = lane & 63
    halo = (even & (within < 16)) | (jnp.logical_not(even) & (within >= 48))
    corners = []
    for pair in range(PAIRS):
        rows = [
            (SPAN * (zz + 2), halo_tile(far_ref, near_ref, zz < 0, pair * HALO + zz % 4 - (zz < 0)))
            for zz in (-2, -1, 4, 5)
        ]
        tile = None
        for side in range(2):
            for start, row in rows:
                start += 64 * side
                moved = shift_x(row, start - LAST if side else start + HALO)
                tile = moved if tile is None else jnp.where(lane >= start, moved, tile)
        swapped = jnp.where(within < 32, shift_s(tile, -1), shift_s(tile, 1))
        for n, got in enumerate((tile, swapped)):
            corners.append(jnp.where(halo, got, own_corner_ref[2 * pair + n]))
            corner_ref[2 * pair + n] = corners[-1]
    ahead = (lane & (SPAN - 1)) < HALO

    def packed(group, move):
        halves = [
            jnp.where(
                ahead, shift_x(group[n], 32 * n + move), shift_x(group[n + 1], 32 * n + HALO + move)
            )
            for n in range(0, len(group), 2)
        ]
        return halves[0] if len(halves) == 1 else jnp.where(lane < 64, *halves)

    for k in range(PACKS):
        group = corners[4 * k : 4 * k + 4]
        to_left, to_right = packed(group, -3), packed(group, -66)
        right_ref[slot_of(k), :] = to_right
        left_ref[slot_of(k), :] = to_left


def state_of(fields):
    mass, motion = fields[:NSP], fields[NSP : NSP + 3]
    thermal, vibration = fields[NSP + 3], fields[NSP + 4]
    density = (mass[0] + mass[1]) + (mass[2] + mass[3]) + mass[4]
    formed = FORMATION[2] * mass[2] + FORMATION[3] * mass[3] + FORMATION[4] * mass[4]
    motion_square = motion[0] * motion[0] + motion[1] * motion[1] + motion[2] * motion[2]
    energy = density * (2.5 * thermal + vibration + 0.5 * motion_square) + formed
    conserved = (
        list(mass) + [density * speed for speed in motion] + [energy, density * vibration]
    )
    return density, density * thermal, jnp.sqrt(HEAT_RATIO * thermal), conserved


def flux_of(conserved, pressure, speed, component):
    flux = [value * speed for value in conserved]
    flux[NSP + component] = flux[NSP + component] + pressure
    flux[NSP + 3] = flux[NSP + 3] + pressure * speed
    return flux


def correction(d0, d1, d2, d3):
    floor = 4.0 * SMOOTH_FLOOR * 12.0 / 13.0
    share = 3.0 / 13.0
    e0, e1, e2 = d1 - d0, d2 - d1, d3 - d2
    g0, g1, g2 = e0 + (d1 + d1), d1 + d2, e2 - (d2 + d2)
    b0 = (e0 * e0 + floor) + share * (g0 * g0)
    b1 = (e1 * e1 + floor) + share * (g1 * g1)
    b2 = (e2 * e2 + floor) + share * (g2 * g2)
    p0, p1, p2 = b1 * b2, b0 * b2, b0 * b1
    w0 = p0 * p0
    w1 = 6.0 * (p1 * p1)
    w2 = 3.0 * (p2 * p2)
    r0 = 5.0 * d1 - (d0 + d0)
    r1 = d1 + (d2 + d2)
    r2 = 4.0 * d2 - d3
    return (w0 * r0 + w1 * r1 + w2 * r2) / (w0 + w1 + w2)


def face_flux(here, slopes, jumps, signal):
    waves = [signal * jump for jump in jumps]
    plus = [slopes[k] + waves[k] for k in range(4)]
    minus = [waves[k] - slopes[k] for k in range(1, 5)]
    gain = correction(*plus)
    loss = correction(minus[3], minus[2], minus[1], minus[0])
    return here + 0.5 * (slopes[2] - waves[2]) + (gain + loss) * (1.0 / 12.0)


def faces_along_x(flux, conserved, signal):
    slope = shift_x(flux, -1) - flux
    jump = shift_x(conserved, -1) - conserved
    slopes = [shift_x(slope, -k) for k in range(-2, 3)]
    jumps = [shift_x(jump, -k) for k in range(-2, 3)]
    return face_flux(flux, slopes, jumps, signal)


def stream_kernel(own_ref, blow_rows, face_ref, part_ref):
    bottom, top = level_edges()

    def row(zz, carry):
        fields = [tile_of(own_ref, field * ROWS + zz) for field in range(NF)]
        density, pressure, sound, conserved = state_of(fields)
        speed = fields[NSP]
        flux = flux_of(conserved, pressure, speed, 0)
        signal = jnp.abs(speed) + sound
        signal = jnp.maximum(signal, shift_x(signal, -1))

        normal_speed = fields[NSP + 1]
        normal_flux = flux_of(conserved, pressure, normal_speed, 1)
        normal_signal = jnp.abs(normal_speed) + sound
        normal_signal = 0.5 * jnp.maximum(normal_signal, shift_s(normal_signal, -2))
        blown = BLOWING * blow_rows[pl.ds(zz, TILE, stride=4), :]
        lift = blown / density
        enthalpy = 3.5 * fields[NSP + 3] + fields[NSP + 4] + 0.5 * lift * lift
        wall = [lift * fields[s] for s in range(NSP)]
        formed = FORMATION[2] * wall[2] + FORMATION[3] * wall[3] + FORMATION[4] * wall[4]
        zero = jnp.zeros((TILE, LANES), F32)
        wall = wall + [
            zero, blown * lift + pressure, zero, blown * enthalpy + formed, blown * fields[NSP + 4]
        ]
        relaxation = 2.0 * density * (fields[NSP + 3] - fields[NSP + 4])
        for field in range(NF):
            value, normal = conserved[field], normal_flux[field]
            slot = slot_of(field * ROWS + zz)
            face_ref[slot, :] = faces_along_x(flux[field], value, signal)
            above = shift_s(value, -2)
            level_face = 0.5 * (normal + shift_s(normal, -2)) - normal_signal * (above - value)
            level_face = jnp.where(top, normal, level_face)
            change = 2.0 * (jnp.where(bottom, wall[field], shift_s(level_face, 2)) - level_face)
            part_ref[slot, :] = change + relaxation if field == NF - 1 else change
        return carry

    lax.fori_loop(0, ROWS, row, 0)


def ends_kernel(corner_ref, face_ref, part_ref, out_ref):
    lane = lanes()
    fields = [corner_ref[field] for field in range(NF)]
    density, pressure, sound, conserved = state_of(fields)
    flux = flux_of(conserved, pressure, fields[NSP], 0)
    signal = jnp.abs(fields[NSP]) + sound
    signal = jnp.maximum(signal, shift_x(signal, -1))
    for field in range(NF):
        end_face = faces_along_x(flux[field], conserved[field], signal)
        for zz in range(ROWS):
            left = shift_x(end_face, 109 - SPAN * zz)
            right = shift_x(end_face, 43 - SPAN * zz)
            slot = slot_of(field * ROWS + zz)
            face = jnp.where(
                lane < 2, left, jnp.where(lane >= LANES - 3, right, face_ref[slot, :])
            )
            before = shift_x(jnp.where(lane == LANES - 1, left, face), 1)
            out_ref[slot, :] = part_ref[slot, :] + (before - face)


SPAN_TILES = ROWS + 2 * HALO


def span_kernel(raw_ref, part_ref, out_ref, value_ref, flux_ref, signal_ref):
    for place in range(SPAN_TILES):
        fields = [raw_ref[place, field] for field in range(NF)]
        _, pressure, sound, conserved = state_of(fields)
        speed = fields[NSP + 2]
        flux = flux_of(conserved, pressure, speed, 2)
        signal_ref[place] = jnp.abs(speed) + sound
        for field in range(NF):
            value_ref[place, field] = conserved[field]
            flux_ref[place, field] = flux[field]

    def faces_of(place):
        signal = jnp.maximum(signal_ref[place], signal_ref[place + 1])
        faces = []
        for field in range(NF):
            flux = [flux_ref[place + k, field] for k in range(-2, 4)]
            value = [value_ref[place + k, field] for k in range(-2, 4)]
            slopes = [flux[k + 1] - flux[k] for k in range(5)]
            jumps = [value[k + 1] - value[k] for k in range(5)]
            faces.append(face_flux(flux[2], slopes, jumps, signal))
        return tuple(faces)

    def row(zz, before):
        faces = faces_of(zz + HALO)
        for field in range(NF):
            slot = slot_of(field * ROWS + zz)
            out_ref[slot, :] = part_ref[slot, :] + (before[field] - faces[field])
        return faces

    lax.fori_loop(0, ROWS, row, faces_of(HALO - 1))


MASS, MOMENTUM, HEAT = 0, 5, 8
SPEED, THERMAL, VIBRATION, FRACTION, DENSITY = 9, 12, 13, 14, 19
STATE_COUNT = 20
SLOPED = 10
STATE_ROWS = 8
GRID_ROWS = 6
PAIR_INDEX = ((0, 0), (1, 1), (0, 1), (0, 2), (1, 2), (2, 2))

PRODUCT, STRESS, HEAT_FLUX, HEAT_SLOPE, MASS_FLUX, MASS_SLOPE = 0, 6, 11, 14, 17, 29
LAST_STRESS = 41
FILTERED = 42
SIDE_SLOPE = FILTERED
TILES = FILTERED + 3

TERMS = 12
TERM_FIELD = (0, 1, 2, 3, 4, 5, 6, 7, 8, 8, 8, 9)
TERM_MODEL = (2, 2, 2, 2, 2, 0, 0, 0, 0, 1, 2, 1)


def model_state(fields):
    mass, motion = fields[:NSP], fields[NSP : NSP + 3]
    thermal, vibration = fields[NSP + 3], fields[NSP + 4]
    density = (mass[0] + mass[1]) + (mass[2] + mass[3]) + mass[4]
    inverse = 1.0 / density
    fraction = [m * inverse for m in mass]
    return (
        list(mass)
        + [density * speed for speed in motion]
        + [density * thermal]
        + list(motion)
        + [thermal, vibration]
        + fraction
        + [density]
    )


def level_slope(value, scale):
    bottom, top = level_edges()
    above = jnp.where(top, value, shift_s(value, -2))
    below = jnp.where(bottom, value, shift_s(value, 2))
    return scale * (above - below)


def strain(slopes):
    diagonal = [2.0 * slopes[k][k] for k in range(3)]
    third = (diagonal[0] + diagonal[1] + diagonal[2]) * (1.0 / 3.0)
    first, second = diagonal[0] - third, diagonal[1] - third
    mixed = [slopes[0][1] + slopes[1][0], slopes[0][2] + slopes[2][0], slopes[1][2] + slopes[2][1]]
    last = diagonal[2] - third
    square = (
        first * first + second * second + last * last
        + 2.0 * (mixed[0] * mixed[0] + mixed[1] * mixed[1] + mixed[2] * mixed[2])
    )
    magnitude = jnp.sqrt(0.125 * square + 1e-06)
    return [first, second] + mixed + [last], magnitude


def grid_terms(here, slopes):
    deviator, magnitude = strain(slopes[:3])
    eddy = FILTER_SQUARE * here(DENSITY) * magnitude
    speed = [here(SPEED + k) for k in range(3)]
    momentum = [here(MOMENTUM + k) for k in range(3)]
    thermal = here(THERMAL)
    stress = [eddy * part for part in deviator]
    tiles = [momentum[i] * speed[j] for i, j in PAIR_INDEX]
    tiles += stress[:5]
    tiles += [m * thermal for m in momentum]
    tiles += [eddy * slopes[3][d] for d in range(3)]
    tiles += [here(MASS + s) * speed[d] for s in range(4) for d in range(3)]
    tiles += [eddy * slopes[5 + s][d] for s in range(4) for d in range(3)]
    tiles.append(stress[5])
    return tiles + [eddy * slopes[4][d] for d in range(3)]


def subgrid_terms(tile, speed, d):
    places = (STRESS, STRESS + 1, STRESS + 2, STRESS + 3, STRESS + 4, LAST_STRESS)
    full = ((0, 2, 3), (2, 1, 4), (3, 4, 5))
    tau = [tile(places[full[i][d]]) for i in range(3)]
    species = [tile(MASS_SLOPE + 3 * s + d) for s in range(4)]
    species.append(-((species[0] + species[1]) + (species[2] + species[3])))
    work = speed[0] * tau[0] + speed[1] * tau[1] + speed[2] * tau[2]
    vibration = tile(SIDE_SLOPE + d)
    heat = 3.5 * tile(HEAT_SLOPE + d) + vibration
    formed = FORMATION[2] * species[2] + FORMATION[3] * species[3] + FORMATION[4] * species[4]
    return species + tau + [work, heat, formed, vibration]


def favre(hat):
    density = (hat[0] + hat[1]) + (hat[2] + hat[3]) + hat[4]
    inverse = 1.0 / density
    return density, [hat[5 + k] * inverse for k in range(3)], hat[8] * inverse, [
        hat[s] * inverse for s in range(4)
    ]


def contractions(hat, density, momentum, favre_here, slopes):
    speed, thermal, fraction = favre_here
    deviator, magnitude = strain(slopes[:3])
    eddy = TEST_SQUARE * density * magnitude
    stress = [hat(STRESS + n) for n in range(5)] + [hat(LAST_STRESS)]
    sums = []
    top = bottom = None

    def add(total, value):
        return value if total is None else total + value

    off_top = off_bottom = None
    for n, (i, j) in enumerate(PAIR_INDEX):
        resolved = hat(PRODUCT + n) - momentum[i] * speed[j]
        model = stress[n] - eddy * deviator[n]
        if i == j:
            top, bottom = add(top, resolved * model), add(bottom, model * model)
        else:
            off_top, off_bottom = add(off_top, resolved * model), add(off_bottom, model * model)
    sums += [top + (off_top + off_top), bottom + (off_bottom + off_bottom)]
    top = bottom = None
    for d in range(3):
        resolved = hat(HEAT_FLUX + d) - momentum[d] * thermal
        model = hat(HEAT_SLOPE + d) - eddy * slopes[3][d]
        top, bottom = add(top, resolved * model), add(bottom, model * model)
    sums += [top, bottom]
    top = bottom = None
    for d in range(3):
        last_resolved = last_model = None
        for s in range(4):
            resolved = hat(MASS_FLUX + 3 * s + d) - momentum[d] * fraction[s]
            model = hat(MASS_SLOPE + 3 * s + d) - eddy * slopes[4 + s][d]
            last_resolved, last_model = add(last_resolved, resolved), add(last_model, model)
            top, bottom = add(top, resolved * model), add(bottom, model * model)
        top, bottom = top + last_resolved * last_model, bottom + last_model * last_model
    return sums + [top, bottom]


def filter_x(tile):
    pair = tile + shift_x(tile, -1)
    return pair + shift_x(pair, 1)


def slope_scale():
    bottom, top = level_edges()
    return jnp.where(bottom | top, 4.0, 2.0)


def joined(top, bottom):
    return jnp.where(
        is_even(),
        (top + shift_s(top, -1)) * (1.0 / 512.0),
        (bottom + shift_s(bottom, 1)) * (1.0 / 1024.0),
    )


def model_kernel(
    own_ref, far_ref, near_ref, corner_own_ref,
    main_ref, clamped_ref, tile_ref, state_ref, raw_ref,
    wide_ref, favre_ref, sum_ref,
):
    scale = slope_scale()
    gather_rows(own_ref, far_ref, near_ref, raw_ref)
    for row in range(STATE_ROWS):
        states = model_state([raw_ref[row + 1, field] for field in range(NF)])
        for k in range(STATE_COUNT):
            state_ref[row, k] = states[k]

    def grid_row(row, carry):
        def here(k):
            return state_ref[row + 1, k]

        slopes = []
        for k in range(SLOPED - 1):
            value = here(SPEED + k)
            along_x = shift_x(value, -1) - shift_x(value, 1)
            along_z = state_ref[row + 2, SPEED + k] - state_ref[row, SPEED + k]
            slopes.append((along_x, level_slope(value, scale), along_z))
        for k, tile in enumerate(grid_terms(here, slopes)):
            tile_ref[row, k] = tile
        hat = []
        for k in range(SPEED):
            total = (state_ref[row, k] + state_ref[row + 2, k]) + 2.0 * here(k)
            hat.append(filter_x(total))
        density, speed, thermal, fraction = favre(hat)
        for k, value in enumerate(speed + [thermal] + fraction):
            favre_ref[row, k] = value
        for k in range(3):
            wide_ref[row, k] = hat[MOMENTUM + k]
        wide_ref[row, 3] = density
        return carry

    lax.fori_loop(0, GRID_ROWS, grid_row, 0)
    for k in range(6):
        sum_ref[k] = jnp.zeros((TILE, LANES), F32)

    def test_row(zz, carry):
        row = zz + 1

        def hat(k):
            total = (tile_ref[row - 1, k] + tile_ref[row + 1, k]) + 2.0 * tile_ref[row, k]
            return filter_x(total)

        slopes = []
        for k in range(8):
            value = favre_ref[row, k]
            along_x = shift_x(value, -1) - shift_x(value, 1)
            along_z = favre_ref[row + 1, k] - favre_ref[row - 1, k]
            slopes.append((along_x, level_slope(value, scale), along_z))
        values = [favre_ref[row, k] for k in range(8)]
        sums = contractions(
            hat, wide_ref[row, 3], [wide_ref[row, k] for k in range(3)],
            (values[:3], values[3], values[4:]), slopes,
        )
        for k in range(6):
            sum_ref[k] = sum_ref[k] + sums[k]
        return carry

    lax.fori_loop(0, ROWS, test_row, 0)
    for k in range(3):
        main_ref[k] = joined(sum_ref[2 * k], sum_ref[2 * k + 1])

    on_left = lanes() < 64
    place = lanes() & (SPAN - 1)
    place = jnp.where(on_left, place, SPAN - 1 - place)
    for field in range(NF):
        tile = clamped = corner_own_ref[field]
        for c in range(HALO):
            copied = jnp.where(on_left, shift_x(tile, c - HALO), shift_x(tile, HALO - c))
            clamped = jnp.where(place == c, copied, clamped)
        clamped_ref[field] = clamped


def corner_kernel(
    clamped_ref, got_left_ref, got_right_ref, main_ref, filter_ref,
    totals_ref, corner_ref, tile_ref, speed_ref
):
    lane = lanes()
    scale = slope_scale()
    column = lax.axis_index("gx")
    first, last = column == 0, column == lax.axis_size("gx") - 1
    place = lane & (SPAN - 1)
    on_left = lane < 64
    low, high = jnp.where(first, 0, HALO), jnp.where(last, SPAN, SPAN - HALO)
    halo = (on_left & (place < low)) | (jnp.logical_not(on_left) & (place >= high))
    fields = []
    for field in range(NF):
        k, j = divmod(field, 4)
        if j == 0:
            from_left, from_right = tile_of(got_left_ref, k), tile_of(got_right_ref, k)
        move = 64 * (j // 2) + HALO * (j % 2)
        got = jnp.where(on_left, shift_x(from_left, -move), shift_x(from_right, 69 - move))
        fields.append(jnp.where(halo, got, clamped_ref[field]))
        corner_ref[field] = fields[field]
    state = model_state(fields)

    def slopes_of(value):
        along_x = shift_x(value, -1) - shift_x(value, 1)
        along_z = shift_x(value, -SPAN) - shift_x(value, SPAN)
        return along_x, level_slope(value, scale), along_z

    weights = filter_ref[...].astype(jnp.bfloat16)

    def filtered(values):
        rest, parts = jnp.concatenate(values, axis=0), []
        for _ in range(3):
            parts.append(rest.astype(jnp.bfloat16))
            rest = rest - parts[-1].astype(F32)
        size = rest.shape[0]
        result = jnp.dot(jnp.concatenate(parts, axis=0), weights, preferred_element_type=F32)
        result = (result[:size] + result[size : 2 * size]) + result[2 * size :]
        return [result[TILE * k : TILE * (k + 1)] for k in range(len(values))]

    tiles = grid_terms(lambda k: state[k], [slopes_of(state[SPEED + k]) for k in range(SLOPED - 1)])
    for k in range(STRESS, TILES):
        tile_ref[k] = tiles[k]
    for k in range(3):
        speed_ref[k] = state[SPEED + k]
    wide = filtered(state[:SPEED] + tiles[:FILTERED] + [state[0]])
    hat = wide[SPEED:]
    density, speed, thermal, fraction = favre(wide[:SPEED])
    sums = contractions(
        lambda k: hat[k], density, wide[MOMENTUM : MOMENTUM + 3],
        (speed, thermal, fraction), [slopes_of(value) for value in speed + [thermal] + fraction],
    )
    edges = jnp.zeros((TILE, LANES), F32)
    for k in range(3):
        side = joined(sums[2 * k], sums[2 * k + 1])
        side = side + shift_x(side, -SPAN)
        side = side + shift_x(side, -2 * SPAN)
        main = jnp.where(lane < 2, shift_x(side, -19), main_ref[k])
        totals_ref[slot_of(k), :] = jnp.where(lane >= LANES - 2, shift_x(side, 126 - 83), main)
        edges = jnp.where(lane == 2 * k, shift_x(side, 2 * k - 18), edges)
        edges = jnp.where(lane == 2 * k + 1, shift_x(side, 2 * k + 1 - 85), edges)
    totals_ref[pl.ds(3 * TILE, TILE), :] = edges


def term_kernel(tile_ref, state_ref, corner_ref, corner_speed_ref, terms_ref):
    lane = lanes()
    bottom, top = level_edges()

    def terms(place, d):
        speed = [state_ref[place + 1, SPEED + k] for k in range(3)]
        return subgrid_terms(lambda k: tile_ref[place, k], speed, d)

    corner_speed = [corner_speed_ref[k] for k in range(3)]
    corner = [subgrid_terms(lambda k: corner_ref[k], corner_speed, d) for d in range(3)]
    corner[2] = [shift_x(value, -SPAN) - shift_x(value, SPAN) for value in corner[2]]

    def patched(value, side, zz):
        value = jnp.where(lane == 0, shift_x(side, -19 - SPAN * zz), value)
        return jnp.where(lane == LANES - 1, shift_x(side, 43 - SPAN * zz), value)

    for zz in range(ROWS):
        row = zz + 1
        along_x, along_y = terms(row, 0), terms(row, 1)
        before, after = terms(row - 1, 2), terms(row + 1, 2)
        for n in range(TERMS):
            right = shift_x(corner[0][n], 42 - SPAN * zz)
            left = shift_x(corner[0][n], -18 - SPAN * zz)
            terms_ref[zz, n, 0] = jnp.where(lane >= LANES - 2, right, shift_x(along_x[n], -1))
            terms_ref[zz, n, 1] = jnp.where(lane < 2, left, shift_x(along_x[n], 1))
            terms_ref[zz, n, 2] = patched(after[n] - before[n], corner[2][n], zz)
            along = patched(along_y[n], corner[1][n], zz)
            terms_ref[zz, n, 3] = jnp.where(top, along, shift_s(along, -2))
            terms_ref[zz, n, 4] = jnp.where(bottom, -along, shift_s(along, 2))


def final_kernel(*refs, parts):
    part_refs = refs[:parts]
    base_ref, terms_ref, out_ref, coefficient_ref, scratch = refs[parts:]
    lane = lanes()
    even = is_even()
    bottom, top = level_edges()
    totals = [
        (tile_of(part_refs[0], k) + tile_of(part_refs[1], k))
        + (tile_of(part_refs[2], k) + tile_of(part_refs[3], k))
        for k in range(4)
    ]
    ratios = []
    for total in totals:
        total = total * (1.0 / (TILE * lax.axis_size("gz")))
        numerator = jnp.where(even, total, shift_s(total, 1))
        denominator = jnp.where(even, shift_s(total, -1), total)
        ratios.append(numerator / (denominator + RATIO_EPSILON))
    column = lax.axis_index("gx")
    first, last = column == 0, column == lax.axis_size("gx") - 1
    here, ahead, behind, above, below = [], [], [], [], []
    for k in range(3):
        ratio = ratios[k]
        scratch[...] = ratio
        coefficient_ref[k] = scratch[pl.ds(0, 4, stride=2), :]
        before = jnp.where(first, ratio, shift_x(ratios[3], -2 * k))
        after = jnp.where(last, ratio, shift_x(ratios[3], 127 - (2 * k + 1)))
        ratio = 0.25 * ratio
        here.append(ratio)
        ahead.append(jnp.where(lane == LANES - 1, 0.25 * after, shift_x(ratio, -1)))
        behind.append(jnp.where(lane == 0, 0.25 * before, shift_x(ratio, 1)))
        above.append(2.0 * jnp.where(top, ratio, shift_s(ratio, -2)))
        below.append(2.0 * jnp.where(bottom, ratio, shift_s(ratio, 2)))

    def row(zz, carry):
        sums = [tile_of(base_ref, field * ROWS + zz) for field in range(NF)]
        for n in range(TERMS):
            k = TERM_MODEL[n]
            change = (
                (ahead[k] * terms_ref[zz, n, 0] - behind[k] * terms_ref[zz, n, 1])
                + here[k] * terms_ref[zz, n, 2]
                + (above[k] * terms_ref[zz, n, 3] - below[k] * terms_ref[zz, n, 4])
            )
            sums[TERM_FIELD[n]] = sums[TERM_FIELD[n]] + change
        for field in range(NF):
            out_ref[pl.ds(field * 32 + zz, TILE, stride=4), :] = sums[field]
        return carry

    lax.fori_loop(0, ROWS, row, 0)


def call(kernel, out_shapes, scratch=(), inputs=0):
    run = pl.pallas_call(
        kernel,
        out_shape=[pltpu.VMEM(shape, F32) for shape in out_shapes],
        in_specs=[VMEM] * inputs,
        out_specs=[VMEM] * len(out_shapes),
        scratch_shapes=[pltpu.VMEM(shape, F32) for shape in scratch],
        compiler_params=SMALL,
    )
    return lambda *args: run(*in_vmem(args))


def in_vmem(args):
    return [pltpu.with_memory_space_constraint(arg, pltpu.VMEM) for arg in args]


def body(constituent_mass, flow_speeds, thermal_pair, blowing_indicator):
    count_x = lax.axis_size("gx")
    count_z = lax.axis_size("gz")

    def swap(near):
        step = [1, -1] if near else [-1, 1]
        return lambda value: lax.ppermute(
            value, "gz", [(i, (i + step[i % 2]) % count_z) for i in range(count_z)]
        )

    def ring(step):
        return lambda value: lax.ppermute(
            value, "gx", [(i, (i + step) % count_x) for i in range(count_x)]
        )

    arrays = [
        value.reshape(-1, LANES) for value in (constituent_mass, flow_speeds, thermal_pair)
    ]
    packed = (PACK_ROWS, LANES)
    rows = (GROUPS * TILE, LANES)
    fields = (NF, TILE, LANES)
    own, far, near, blown = pl.pallas_call(
        pack_kernel,
        out_shape=[
            pltpu.VMEM(shape, F32)
            for shape in (
                rows, (MAIN_ROWS, LANES), (MAIN_ROWS, LANES), (4 * TILE, LANES),
            )
        ],
        in_specs=[pl.BlockSpec(memory_space=pltpu.HBM)] * 4,
        out_specs=[VMEM] * 4,
        scratch_shapes=[
            pltpu.VMEM((NF * 4 * TILE, LANES), F32),
            pltpu.VMEM(blowing_indicator.shape, jnp.int32),
            pltpu.SemaphoreType.DMA((4,)),
        ],
        compiler_params=SMALL,
    )(*[
        pltpu.with_memory_space_constraint(value, pltpu.HBM)
        for value in arrays + [blowing_indicator]
    ])
    far = swap(False)(far)
    near = swap(True)(near)
    face, part = call(stream_kernel, [rows, rows], inputs=2)(own, blown)
    corner, weights = call(own_corner_kernel, [fields, (LANES, LANES)], inputs=1)(own)
    far, near, face, part, corner = lax.optimization_barrier((far, near, face, part, corner))

    corner, to_right, to_left = call(
        corner_pack_kernel,
        [fields, packed, packed],
        inputs=3,
    )(corner, far, near)
    got_left = ring(1)(to_right)
    got_right = ring(-1)(to_left)
    sums, clamped, tiles, state, raw = call(
        model_kernel,
        [
            (3, TILE, LANES),
            fields,
            (GRID_ROWS, TILES, TILE, LANES),
            (STATE_ROWS, STATE_COUNT, TILE, LANES),
            (SPAN_TILES, NF, TILE, LANES),
        ],
        scratch=[(GRID_ROWS, 4, TILE, LANES), (GRID_ROWS, 8, TILE, LANES), (6, TILE, LANES)],
        inputs=4,
    )(own, far, near, corner)
    got_left, got_right, sums = lax.optimization_barrier((got_left, got_right, sums))
    totals, corner, corner_tiles, corner_speed = call(
        corner_kernel,
        [(4 * TILE, LANES), fields, (TILES, TILE, LANES), (3, TILE, LANES)],
        inputs=5,
    )(clamped, got_left, got_right, sums, weights)

    (terms,) = call(term_kernel, [(ROWS, TERMS, 5, TILE, LANES)], inputs=4)(
        tiles, state, corner_tiles, corner_speed
    )
    (part,) = call(ends_kernel, [rows], inputs=3)(corner, face, part)
    (base,) = call(
        span_kernel,
        [rows],
        scratch=[
            (SPAN_TILES, NF, TILE, LANES), (SPAN_TILES, NF, TILE, LANES), (SPAN_TILES, TILE, LANES),
        ],
        inputs=2,
    )(raw, part)

    def crossed(value, mask):
        return lax.ppermute(value, "gz", [(i, i ^ mask) for i in range(count_z)])

    totals = totals + crossed(totals, 1)
    reach = 2
    while count_z > 4 * reach:
        a, b, c = (crossed(totals, k * reach) for k in (1, 2, 3))
        totals = (totals + a) + (b + c)
        reach *= 4
    parts = [totals] + [
        crossed(totals, k * reach) if k * reach < count_z else jnp.zeros_like(totals)
        for k in (2, 3, 1)
    ]

    def final(*refs):
        final_kernel(*refs, parts=4)

    tendency, coefficients = pl.pallas_call(
        final,
        out_shape=[jax.ShapeDtypeStruct(shape, F32) for shape in ((NF * 32, LANES), (3, 4, LANES))],
        in_specs=[VMEM] * 6,
        out_specs=[VMEM] * 2,
        scratch_shapes=[pltpu.VMEM((TILE, LANES), F32)],
        compiler_params=SMALL,
    )(*in_vmem(parts + [base, terms]))
    return tendency.reshape(NF, 4, TILE, LANES), coefficients


def solution(mesh):
    placed = (
        P(None, None, "gz", "gx"),
        P(None, None, "gz", "gx"),
        P(None, None, "gz", "gx"),
        P("gz", "gx"),
    )
    return jax.shard_map(
        body,
        mesh=mesh,
        in_specs=placed,
        out_specs=(P(None, None, "gz", "gx"), P(None, None, "gx")),
        check_vma=False,
    )
```

```python
import jax
import jax.numpy as jnp
from jax import lax
from jax.experimental import pallas as pl
from jax.experimental.pallas import tpu as pltpu
from jax.sharding import PartitionSpec as P


NSP = 5
NF = 10
ROWS = 4
TILE = 8
LANES = 128
HALO = 3
SPAN = 8
LAST = LANES - 5
GROUPS = NF * ROWS
PAIRS = NF // 2
PACKS = 3
PACK_ROWS = PACKS * TILE
MAIN_ROWS = PAIRS * HALO * TILE

HEAT_RATIO = 1.4
FILTER_SQUARE = 0.5 ** (2.0 / 3.0)
TEST_SQUARE = 2.0 ** (2.0 / 3.0)
FORMATION = (0.0, 0.0, 0.1, 0.5, 0.25)
BLOWING = 0.3
SMOOTH_FLOOR = 0.01
RATIO_EPSILON = 1e-06

VMEM = pl.BlockSpec(memory_space=pltpu.VMEM)
F32 = jnp.float32
SMALL = pltpu.CompilerParams(vmem_limit_bytes=8 << 20)


def lanes():
    return lax.broadcasted_iota(jnp.int32, (TILE, LANES), 1)


def sublanes():
    return lax.broadcasted_iota(jnp.int32, (TILE, LANES), 0)


def shift_x(tile, step):
    if isinstance(step, int):
        step = step % LANES
        if step == 0:
            return tile
    return pltpu.roll(tile, step, 1)


def shift_s(tile, step):
    return pltpu.roll(tile, step % TILE, 0)


def is_even():
    return (sublanes() & 1) == 0


def level_edges():
    level = sublanes() >> 1
    return level == 0, level == 3


def slot_of(index):
    start = index * TILE
    return pl.ds(start if isinstance(index, int) else pl.multiple_of(start, TILE), TILE)


def tile_of(ref, index):
    return ref[slot_of(index), :]


def is_first_of_pair(axis):
    return (lax.axis_index(axis) & 1) == 0


def halo_tile(far_ref, near_ref, below, index):
    first, second = (far_ref, near_ref) if below else (near_ref, far_ref)
    return jnp.where(is_first_of_pair("gz"), tile_of(first, index), tile_of(second, index))


def pack_kernel(
    mass_hbm, speed_hbm, heat_hbm, blow_hbm, own_ref, far_ref, near_ref, blow_rows,
    given_ref, blow_ref, arrived
):
    start, copies = 0, []
    for k, source in enumerate((mass_hbm, speed_hbm, heat_hbm)):
        target = given_ref.at[pl.ds(start, source.shape[0])]
        copies.append(pltpu.make_async_copy(source, target, arrived.at[k]))
        start += source.shape[0]
    copies.append(pltpu.make_async_copy(blow_hbm, blow_ref, arrived.at[3]))
    for copy in copies:
        copy.start()
    first_fields = (0, NSP, NSP + 3)
    even = is_even()
    first_core = is_first_of_pair("gz")
    tiles = {}
    for field in range(NF):
        if field in first_fields:
            copies[first_fields.index(field)].wait()
        for zz in range(ROWS):
            tile = given_ref[pl.ds(field * 32 + zz, TILE, stride=4), :]
            tiles[field, zz] = tile
            own_ref[slot_of(field * ROWS + zz), :] = tile
        if field % 2:
            for k in range(HALO):
                up = jnp.where(even, shift_s(tiles[field - 1, k + 1], -1), tiles[field, k + 1])
                down = jnp.where(even, tiles[field, k], shift_s(tiles[field - 1, k], 1))
                slot = slot_of(field // 2 * HALO + k)
                far_ref[slot, :] = jnp.where(first_core, down, up)
                near_ref[slot, :] = jnp.where(first_core, up, down)
    copies[3].wait()
    for level in range(4):
        blow_rows[pl.ds(level * TILE, TILE), :] = blow_ref[...].astype(F32)


def gather_rows(own_ref, far_ref, near_ref, raw_ref):
    even = is_even()
    for field in range(NF):
        pair, second = divmod(field, 2)
        own = [tile_of(own_ref, field * ROWS + zz) for zz in range(ROWS)]
        for zz in range(ROWS):
            raw_ref[zz + HALO, field] = own[zz]
        for k in range(HALO):
            low = halo_tile(far_ref, near_ref, True, pair * HALO + k)
            high = halo_tile(far_ref, near_ref, False, pair * HALO + k)
            if second:
                low, high = shift_s(low, -1), shift_s(high, 1)
            raw_ref[k, field] = jnp.where(even, low, shift_s(own[k + 1], 1))
            raw_ref[k + HALO + ROWS, field] = jnp.where(even, shift_s(own[k], -1), high)


def own_corner_kernel(own_ref, corner_ref, filter_ref):
    shape = (LANES, LANES)
    source, target = (lax.broadcasted_iota(jnp.int32, shape, d) for d in range(2))

    def weight(a, b):
        apart = jnp.abs(a - b)
        return jnp.where(apart == 0, 2.0, jnp.where(apart == 1, 1.0, 0.0))

    along_x = weight(source & (SPAN - 1), target & (SPAN - 1))
    filter_ref[...] = along_x * weight(source >> 3, target >> 3)
    lane = lanes()
    within = lane & 63
    for field in range(NF):
        tile = None
        for side in range(2):
            for zz in range(ROWS):
                start = 64 * side + SPAN * (zz + 2)
                moved = shift_x(
                    tile_of(own_ref, field * ROWS + zz), start - LAST if side else start + HALO
                )
                tile = moved if tile is None else jnp.where(lane >= start, moved, tile)
        low, high = shift_s(shift_x(tile, -32), 1), shift_s(shift_x(tile, 32), -1)
        corner_ref[field] = jnp.where(within < 16, low, jnp.where(within >= 48, high, tile))


def corner_pack_kernel(own_corner_ref, far_ref, near_ref, corner_ref, right_ref, left_ref):
    lane = lanes()
    even = is_even()
    within = lane & 63
    halo = (even & (within < 16)) | (jnp.logical_not(even) & (within >= 48))
    corners = []
    for pair in range(PAIRS):
        rows = [
            (SPAN * (zz + 2), halo_tile(far_ref, near_ref, zz < 0, pair * HALO + zz % 4 - (zz < 0)))
            for zz in (-2, -1, 4, 5)
        ]
        tile = None
        for side in range(2):
            for start, row in rows:
                start += 64 * side
                moved = shift_x(row, start - LAST if side else start + HALO)
                tile = moved if tile is None else jnp.where(lane >= start, moved, tile)
        swapped = jnp.where(within < 32, shift_s(tile, -1), shift_s(tile, 1))
        for n, got in enumerate((tile, swapped)):
            corners.append(jnp.where(halo, got, own_corner_ref[2 * pair + n]))
            corner_ref[2 * pair + n] = corners[-1]
    ahead = (lane & (SPAN - 1)) < HALO

    def packed(group, move):
        halves = [
            jnp.where(
                ahead, shift_x(group[n], 32 * n + move), shift_x(group[n + 1], 32 * n + HALO + move)
            )
            for n in range(0, len(group), 2)
        ]
        return halves[0] if len(halves) == 1 else jnp.where(lane < 64, *halves)

    for k in range(PACKS):
        group = corners[4 * k : 4 * k + 4]
        to_left, to_right = packed(group, -3), packed(group, -66)
        right_ref[slot_of(k), :] = to_right
        left_ref[slot_of(k), :] = to_left


def state_of(fields):
    mass, motion = fields[:NSP], fields[NSP : NSP + 3]
    thermal, vibration = fields[NSP + 3], fields[NSP + 4]
    density = (mass[0] + mass[1]) + (mass[2] + mass[3]) + mass[4]
    formed = FORMATION[2] * mass[2] + FORMATION[3] * mass[3] + FORMATION[4] * mass[4]
    motion_square = motion[0] * motion[0] + motion[1] * motion[1] + motion[2] * motion[2]
    energy = density * (2.5 * thermal + vibration + 0.5 * motion_square) + formed
    conserved = (
        list(mass) + [density * speed for speed in motion] + [energy, density * vibration]
    )
    return density, density * thermal, jnp.sqrt(HEAT_RATIO * thermal), conserved


def flux_of(conserved, pressure, speed, component):
    flux = [value * speed for value in conserved]
    flux[NSP + component] = flux[NSP + component] + pressure
    flux[NSP + 3] = flux[NSP + 3] + pressure * speed
    return flux


def correction(d0, d1, d2, d3):
    floor = 4.0 * SMOOTH_FLOOR * 12.0 / 13.0
    share = 3.0 / 13.0
    e0, e1, e2 = d1 - d0, d2 - d1, d3 - d2
    g0, g1, g2 = e0 + (d1 + d1), d1 + d2, e2 - (d2 + d2)
    b0 = (e0 * e0 + floor) + share * (g0 * g0)
    b1 = (e1 * e1 + floor) + share * (g1 * g1)
    b2 = (e2 * e2 + floor) + share * (g2 * g2)
    p0, p1, p2 = b1 * b2, b0 * b2, b0 * b1
    w0 = p0 * p0
    w1 = 6.0 * (p1 * p1)
    w2 = 3.0 * (p2 * p2)
    r0 = 5.0 * d1 - (d0 + d0)
    r1 = d1 + (d2 + d2)
    r2 = 4.0 * d2 - d3
    return (w0 * r0 + w1 * r1 + w2 * r2) / (w0 + w1 + w2)


def face_flux(here, slopes, jumps, signal):
    waves = [signal * jump for jump in jumps]
    plus = [slopes[k] + waves[k] for k in range(4)]
    minus = [waves[k] - slopes[k] for k in range(1, 5)]
    gain = correction(*plus)
    loss = correction(minus[3], minus[2], minus[1], minus[0])
    return here + 0.5 * (slopes[2] - waves[2]) + (gain + loss) * (1.0 / 12.0)


def faces_along_x(flux, conserved, signal):
    slope = shift_x(flux, -1) - flux
    jump = shift_x(conserved, -1) - conserved
    slopes = [shift_x(slope, -k) for k in range(-2, 3)]
    jumps = [shift_x(jump, -k) for k in range(-2, 3)]
    return face_flux(flux, slopes, jumps, signal)


def stream_kernel(own_ref, blow_rows, face_ref, part_ref):
    bottom, top = level_edges()

    def row(zz, carry):
        fields = [tile_of(own_ref, field * ROWS + zz) for field in range(NF)]
        density, pressure, sound, conserved = state_of(fields)
        speed = fields[NSP]
        flux = flux_of(conserved, pressure, speed, 0)
        signal = jnp.abs(speed) + sound
        signal = jnp.maximum(signal, shift_x(signal, -1))

        normal_speed = fields[NSP + 1]
        normal_flux = flux_of(conserved, pressure, normal_speed, 1)
        normal_signal = jnp.abs(normal_speed) + sound
        normal_signal = 0.5 * jnp.maximum(normal_signal, shift_s(normal_signal, -2))
        blown = BLOWING * blow_rows[pl.ds(zz, TILE, stride=4), :]
        lift = blown / density
        enthalpy = 3.5 * fields[NSP + 3] + fields[NSP + 4] + 0.5 * lift * lift
        wall = [lift * fields[s] for s in range(NSP)]
        formed = FORMATION[2] * wall[2] + FORMATION[3] * wall[3] + FORMATION[4] * wall[4]
        zero = jnp.zeros((TILE, LANES), F32)
        wall = wall + [
            zero, blown * lift + pressure, zero, blown * enthalpy + formed, blown * fields[NSP + 4]
        ]
        relaxation = 2.0 * density * (fields[NSP + 3] - fields[NSP + 4])
        for field in range(NF):
            value, normal = conserved[field], normal_flux[field]
            slot = slot_of(field * ROWS + zz)
            face_ref[slot, :] = faces_along_x(flux[field], value, signal)
            above = shift_s(value, -2)
            level_face = 0.5 * (normal + shift_s(normal, -2)) - normal_signal * (above - value)
            level_face = jnp.where(top, normal, level_face)
            change = 2.0 * (jnp.where(bottom, wall[field], shift_s(level_face, 2)) - level_face)
            part_ref[slot, :] = change + relaxation if field == NF - 1 else change
        return carry

    lax.fori_loop(0, ROWS, row, 0)


def ends_kernel(corner_ref, face_ref, part_ref, out_ref):
    lane = lanes()
    fields = [corner_ref[field] for field in range(NF)]
    density, pressure, sound, conserved = state_of(fields)
    flux = flux_of(conserved, pressure, fields[NSP], 0)
    signal = jnp.abs(fields[NSP]) + sound
    signal = jnp.maximum(signal, shift_x(signal, -1))
    for field in range(NF):
        end_face = faces_along_x(flux[field], conserved[field], signal)
        for zz in range(ROWS):
            left = shift_x(end_face, 109 - SPAN * zz)
            right = shift_x(end_face, 43 - SPAN * zz)
            slot = slot_of(field * ROWS + zz)
            face = jnp.where(
                lane < 2, left, jnp.where(lane >= LANES - 3, right, face_ref[slot, :])
            )
            before = shift_x(jnp.where(lane == LANES - 1, left, face), 1)
            out_ref[slot, :] = part_ref[slot, :] + (before - face)


SPAN_TILES = ROWS + 2 * HALO


def span_kernel(raw_ref, part_ref, out_ref, value_ref, flux_ref, signal_ref):
    for place in range(SPAN_TILES):
        fields = [raw_ref[place, field] for field in range(NF)]
        _, pressure, sound, conserved = state_of(fields)
        speed = fields[NSP + 2]
        flux = flux_of(conserved, pressure, speed, 2)
        signal_ref[place] = jnp.abs(speed) + sound
        for field in range(NF):
            value_ref[place, field] = conserved[field]
            flux_ref[place, field] = flux[field]

    def faces_of(place):
        signal = jnp.maximum(signal_ref[place], signal_ref[place + 1])
        faces = []
        for field in range(NF):
            flux = [flux_ref[place + k, field] for k in range(-2, 4)]
            value = [value_ref[place + k, field] for k in range(-2, 4)]
            slopes = [flux[k + 1] - flux[k] for k in range(5)]
            jumps = [value[k + 1] - value[k] for k in range(5)]
            faces.append(face_flux(flux[2], slopes, jumps, signal))
        return tuple(faces)

    def row(zz, before):
        faces = faces_of(zz + HALO)
        for field in range(NF):
            slot = slot_of(field * ROWS + zz)
            out_ref[slot, :] = part_ref[slot, :] + (before[field] - faces[field])
        return faces

    lax.fori_loop(0, ROWS, row, faces_of(HALO - 1))


MASS, MOMENTUM, HEAT = 0, 5, 8
SPEED, THERMAL, VIBRATION, FRACTION, DENSITY = 9, 12, 13, 14, 19
STATE_COUNT = 20
SLOPED = 10
STATE_ROWS = 8
GRID_ROWS = 6
PAIR_INDEX = ((0, 0), (1, 1), (0, 1), (0, 2), (1, 2), (2, 2))

PRODUCT, STRESS, HEAT_FLUX, HEAT_SLOPE, MASS_FLUX, MASS_SLOPE = 0, 6, 11, 14, 17, 29
LAST_STRESS = 41
FILTERED = 42
SIDE_SLOPE = FILTERED
TILES = FILTERED + 3

TERMS = 12
TERM_FIELD = (0, 1, 2, 3, 4, 5, 6, 7, 8, 8, 8, 9)
TERM_MODEL = (2, 2, 2, 2, 2, 0, 0, 0, 0, 1, 2, 1)


def model_state(fields):
    mass, motion = fields[:NSP], fields[NSP : NSP + 3]
    thermal, vibration = fields[NSP + 3], fields[NSP + 4]
    density = (mass[0] + mass[1]) + (mass[2] + mass[3]) + mass[4]
    inverse = 1.0 / density
    fraction = [m * inverse for m in mass]
    return (
        list(mass)
        + [density * speed for speed in motion]
        + [density * thermal]
        + list(motion)
        + [thermal, vibration]
        + fraction
        + [density]
    )


def level_slope(value, scale):
    bottom, top = level_edges()
    above = jnp.where(top, value, shift_s(value, -2))
    below = jnp.where(bottom, value, shift_s(value, 2))
    return scale * (above - below)


def strain(slopes):
    diagonal = [2.0 * slopes[k][k] for k in range(3)]
    third = (diagonal[0] + diagonal[1] + diagonal[2]) * (1.0 / 3.0)
    first, second = diagonal[0] - third, diagonal[1] - third
    mixed = [slopes[0][1] + slopes[1][0], slopes[0][2] + slopes[2][0], slopes[1][2] + slopes[2][1]]
    last = diagonal[2] - third
    square = (
        first * first + second * second + last * last
        + 2.0 * (mixed[0] * mixed[0] + mixed[1] * mixed[1] + mixed[2] * mixed[2])
    )
    magnitude = jnp.sqrt(0.125 * square + 1e-06)
    return [first, second] + mixed + [last], magnitude


def grid_terms(here, slopes):
    deviator, magnitude = strain(slopes[:3])
    eddy = FILTER_SQUARE * here(DENSITY) * magnitude
    speed = [here(SPEED + k) for k in range(3)]
    momentum = [here(MOMENTUM + k) for k in range(3)]
    thermal = here(THERMAL)
    stress = [eddy * part for part in deviator]
    tiles = [momentum[i] * speed[j] for i, j in PAIR_INDEX]
    tiles += stress[:5]
    tiles += [m * thermal for m in momentum]
    tiles += [eddy * slopes[3][d] for d in range(3)]
    tiles += [here(MASS + s) * speed[d] for s in range(4) for d in range(3)]
    tiles += [eddy * slopes[5 + s][d] for s in range(4) for d in range(3)]
    tiles.append(stress[5])
    return tiles + [eddy * slopes[4][d] for d in range(3)]


def subgrid_terms(tile, speed, d):
    places = (STRESS, STRESS + 1, STRESS + 2, STRESS + 3, STRESS + 4, LAST_STRESS)
    full = ((0, 2, 3), (2, 1, 4), (3, 4, 5))
    tau = [tile(places[full[i][d]]) for i in range(3)]
    species = [tile(MASS_SLOPE + 3 * s + d) for s in range(4)]
    species.append(-((species[0] + species[1]) + (species[2] + species[3])))
    work = speed[0] * tau[0] + speed[1] * tau[1] + speed[2] * tau[2]
    vibration = tile(SIDE_SLOPE + d)
    heat = 3.5 * tile(HEAT_SLOPE + d) + vibration
    formed = FORMATION[2] * species[2] + FORMATION[3] * species[3] + FORMATION[4] * species[4]
    return species + tau + [work, heat, formed, vibration]


def favre(hat):
    density = (hat[0] + hat[1]) + (hat[2] + hat[3]) + hat[4]
    inverse = 1.0 / density
    return density, [hat[5 + k] * inverse for k in range(3)], hat[8] * inverse, [
        hat[s] * inverse for s in range(4)
    ]


def contractions(hat, density, momentum, favre_here, slopes):
    speed, thermal, fraction = favre_here
    deviator, magnitude = strain(slopes[:3])
    eddy = TEST_SQUARE * density * magnitude
    stress = [hat(STRESS + n) for n in range(5)] + [hat(LAST_STRESS)]
    sums = []
    top = bottom = None

    def add(total, value):
        return value if total is None else total + value

    off_top = off_bottom = None
    for n, (i, j) in enumerate(PAIR_INDEX):
        resolved = hat(PRODUCT + n) - momentum[i] * speed[j]
        model = stress[n] - eddy * deviator[n]
        if i == j:
            top, bottom = add(top, resolved * model), add(bottom, model * model)
        else:
            off_top, off_bottom = add(off_top, resolved * model), add(off_bottom, model * model)
    sums += [top + (off_top + off_top), bottom + (off_bottom + off_bottom)]
    top = bottom = None
    for d in range(3):
        resolved = hat(HEAT_FLUX + d) - momentum[d] * thermal
        model = hat(HEAT_SLOPE + d) - eddy * slopes[3][d]
        top, bottom = add(top, resolved * model), add(bottom, model * model)
    sums += [top, bottom]
    top = bottom = None
    for d in range(3):
        last_resolved = last_model = None
        for s in range(4):
            resolved = hat(MASS_FLUX + 3 * s + d) - momentum[d] * fraction[s]
            model = hat(MASS_SLOPE + 3 * s + d) - eddy * slopes[4 + s][d]
            last_resolved, last_model = add(last_resolved, resolved), add(last_model, model)
            top, bottom = add(top, resolved * model), add(bottom, model * model)
        top, bottom = top + last_resolved * last_model, bottom + last_model * last_model
    return sums + [top, bottom]


def filter_x(tile):
    pair = tile + shift_x(tile, -1)
    return pair + shift_x(pair, 1)


def slope_scale():
    bottom, top = level_edges()
    return jnp.where(bottom | top, 4.0, 2.0)


def joined(top, bottom):
    return jnp.where(
        is_even(),
        (top + shift_s(top, -1)) * (1.0 / 512.0),
        (bottom + shift_s(bottom, 1)) * (1.0 / 1024.0),
    )


def model_kernel(
    own_ref, far_ref, near_ref, corner_own_ref,
    main_ref, clamped_ref, tile_ref, state_ref, raw_ref,
    wide_ref, favre_ref, sum_ref,
):
    scale = slope_scale()
    gather_rows(own_ref, far_ref, near_ref, raw_ref)
    for row in range(STATE_ROWS):
        states = model_state([raw_ref[row + 1, field] for field in range(NF)])
        for k in range(STATE_COUNT):
            state_ref[row, k] = states[k]

    def grid_row(row, carry):
        def here(k):
            return state_ref[row + 1, k]

        slopes = []
        for k in range(SLOPED - 1):
            value = here(SPEED + k)
            along_x = shift_x(value, -1) - shift_x(value, 1)
            along_z = state_ref[row + 2, SPEED + k] - state_ref[row, SPEED + k]
            slopes.append((along_x, level_slope(value, scale), along_z))
        for k, tile in enumerate(grid_terms(here, slopes)):
            tile_ref[row, k] = tile
        hat = []
        for k in range(SPEED):
            total = (state_ref[row, k] + state_ref[row + 2, k]) + 2.0 * here(k)
            hat.append(filter_x(total))
        density, speed, thermal, fraction = favre(hat)
        for k, value in enumerate(speed + [thermal] + fraction):
            favre_ref[row, k] = value
        for k in range(3):
            wide_ref[row, k] = hat[MOMENTUM + k]
        wide_ref[row, 3] = density
        return carry

    lax.fori_loop(0, GRID_ROWS, grid_row, 0)
    for k in range(6):
        sum_ref[k] = jnp.zeros((TILE, LANES), F32)

    def test_row(zz, carry):
        row = zz + 1

        def hat(k):
            total = (tile_ref[row - 1, k] + tile_ref[row + 1, k]) + 2.0 * tile_ref[row, k]
            return filter_x(total)

        slopes = []
        for k in range(8):
            value = favre_ref[row, k]
            along_x = shift_x(value, -1) - shift_x(value, 1)
            along_z = favre_ref[row + 1, k] - favre_ref[row - 1, k]
            slopes.append((along_x, level_slope(value, scale), along_z))
        values = [favre_ref[row, k] for k in range(8)]
        sums = contractions(
            hat, wide_ref[row, 3], [wide_ref[row, k] for k in range(3)],
            (values[:3], values[3], values[4:]), slopes,
        )
        for k in range(6):
            sum_ref[k] = sum_ref[k] + sums[k]
        return carry

    lax.fori_loop(0, ROWS, test_row, 0)
    for k in range(3):
        main_ref[k] = joined(sum_ref[2 * k], sum_ref[2 * k + 1])

    on_left = lanes() < 64
    place = lanes() & (SPAN - 1)
    place = jnp.where(on_left, place, SPAN - 1 - place)
    for field in range(NF):
        tile = clamped = corner_own_ref[field]
        for c in range(HALO):
            copied = jnp.where(on_left, shift_x(tile, c - HALO), shift_x(tile, HALO - c))
            clamped = jnp.where(place == c, copied, clamped)
        clamped_ref[field] = clamped


def corner_kernel(
    clamped_ref, got_left_ref, got_right_ref, main_ref, filter_ref,
    totals_ref, corner_ref, tile_ref, speed_ref
):
    lane = lanes()
    scale = slope_scale()
    column = lax.axis_index("gx")
    first, last = column == 0, column == lax.axis_size("gx") - 1
    place = lane & (SPAN - 1)
    on_left = lane < 64
    low, high = jnp.where(first, 0, HALO), jnp.where(last, SPAN, SPAN - HALO)
    halo = (on_left & (place < low)) | (jnp.logical_not(on_left) & (place >= high))
    fields = []
    for field in range(NF):
        k, j = divmod(field, 4)
        if j == 0:
            from_left, from_right = tile_of(got_left_ref, k), tile_of(got_right_ref, k)
        move = 64 * (j // 2) + HALO * (j % 2)
        got = jnp.where(on_left, shift_x(from_left, -move), shift_x(from_right, 69 - move))
        fields.append(jnp.where(halo, got, clamped_ref[field]))
        corner_ref[field] = fields[field]
    state = model_state(fields)

    def slopes_of(value):
        along_x = shift_x(value, -1) - shift_x(value, 1)
        along_z = shift_x(value, -SPAN) - shift_x(value, SPAN)
        return along_x, level_slope(value, scale), along_z

    weights = filter_ref[...].astype(jnp.bfloat16)

    def filtered(values):
        rest, parts = jnp.concatenate(values, axis=0), []
        for _ in range(3):
            parts.append(rest.astype(jnp.bfloat16))
            rest = rest - parts[-1].astype(F32)
        size = rest.shape[0]
        result = jnp.dot(jnp.concatenate(parts, axis=0), weights, preferred_element_type=F32)
        result = (result[:size] + result[size : 2 * size]) + result[2 * size :]
        return [result[TILE * k : TILE * (k + 1)] for k in range(len(values))]

    tiles = grid_terms(lambda k: state[k], [slopes_of(state[SPEED + k]) for k in range(SLOPED - 1)])
    for k in range(STRESS, TILES):
        tile_ref[k] = tiles[k]
    for k in range(3):
        speed_ref[k] = state[SPEED + k]
    wide = filtered(state[:SPEED] + tiles[:FILTERED] + [state[0]])
    hat = wide[SPEED:]
    density, speed, thermal, fraction = favre(wide[:SPEED])
    sums = contractions(
        lambda k: hat[k], density, wide[MOMENTUM : MOMENTUM + 3],
        (speed, thermal, fraction), [slopes_of(value) for value in speed + [thermal] + fraction],
    )
    edges = jnp.zeros((TILE, LANES), F32)
    for k in range(3):
        side = joined(sums[2 * k], sums[2 * k + 1])
        side = side + shift_x(side, -SPAN)
        side = side + shift_x(side, -2 * SPAN)
        main = jnp.where(lane < 2, shift_x(side, -19), main_ref[k])
        totals_ref[slot_of(k), :] = jnp.where(lane >= LANES - 2, shift_x(side, 126 - 83), main)
        edges = jnp.where(lane == 2 * k, shift_x(side, 2 * k - 18), edges)
        edges = jnp.where(lane == 2 * k + 1, shift_x(side, 2 * k + 1 - 85), edges)
    totals_ref[pl.ds(3 * TILE, TILE), :] = edges


def term_kernel(tile_ref, state_ref, corner_ref, corner_speed_ref, terms_ref):
    lane = lanes()
    bottom, top = level_edges()

    def terms(place, d):
        speed = [state_ref[place + 1, SPEED + k] for k in range(3)]
        return subgrid_terms(lambda k: tile_ref[place, k], speed, d)

    corner_speed = [corner_speed_ref[k] for k in range(3)]
    corner = [subgrid_terms(lambda k: corner_ref[k], corner_speed, d) for d in range(3)]
    corner[2] = [shift_x(value, -SPAN) - shift_x(value, SPAN) for value in corner[2]]

    def patched(value, side, zz):
        value = jnp.where(lane == 0, shift_x(side, -19 - SPAN * zz), value)
        return jnp.where(lane == LANES - 1, shift_x(side, 43 - SPAN * zz), value)

    for zz in range(ROWS):
        row = zz + 1
        along_x, along_y = terms(row, 0), terms(row, 1)
        before, after = terms(row - 1, 2), terms(row + 1, 2)
        for n in range(TERMS):
            right = shift_x(corner[0][n], 42 - SPAN * zz)
            left = shift_x(corner[0][n], -18 - SPAN * zz)
            terms_ref[zz, n, 0] = jnp.where(lane >= LANES - 2, right, shift_x(along_x[n], -1))
            terms_ref[zz, n, 1] = jnp.where(lane < 2, left, shift_x(along_x[n], 1))
            terms_ref[zz, n, 2] = patched(after[n] - before[n], corner[2][n], zz)
            along = patched(along_y[n], corner[1][n], zz)
            terms_ref[zz, n, 3] = jnp.where(top, along, shift_s(along, -2))
            terms_ref[zz, n, 4] = jnp.where(bottom, -along, shift_s(along, 2))


def final_kernel(*refs, parts):
    part_refs = refs[:parts]
    base_ref, terms_ref, out_ref, coefficient_ref, scratch = refs[parts:]
    lane = lanes()
    even = is_even()
    bottom, top = level_edges()
    totals = [
        (tile_of(part_refs[0], k) + tile_of(part_refs[1], k))
        + (tile_of(part_refs[2], k) + tile_of(part_refs[3], k))
        for k in range(4)
    ]
    ratios = []
    for total in totals:
        total = total * (1.0 / (TILE * lax.axis_size("gz")))
        numerator = jnp.where(even, total, shift_s(total, 1))
        denominator = jnp.where(even, shift_s(total, -1), total)
        ratios.append(numerator / (denominator + RATIO_EPSILON))
    column = lax.axis_index("gx")
    first, last = column == 0, column == lax.axis_size("gx") - 1
    here, ahead, behind, above, below = [], [], [], [], []
    for k in range(3):
        ratio = ratios[k]
        scratch[...] = ratio
        coefficient_ref[k] = scratch[pl.ds(0, 4, stride=2), :]
        before = jnp.where(first, ratio, shift_x(ratios[3], -2 * k))
        after = jnp.where(last, ratio, shift_x(ratios[3], 127 - (2 * k + 1)))
        ratio = 0.25 * ratio
        here.append(ratio)
        ahead.append(jnp.where(lane == LANES - 1, 0.25 * after, shift_x(ratio, -1)))
        behind.append(jnp.where(lane == 0, 0.25 * before, shift_x(ratio, 1)))
        above.append(2.0 * jnp.where(top, ratio, shift_s(ratio, -2)))
        below.append(2.0 * jnp.where(bottom, ratio, shift_s(ratio, 2)))

    def row(zz, carry):
        sums = [tile_of(base_ref, field * ROWS + zz) for field in range(NF)]
        for n in range(TERMS):
            k = TERM_MODEL[n]
            change = (
                (ahead[k] * terms_ref[zz, n, 0] - behind[k] * terms_ref[zz, n, 1])
                + here[k] * terms_ref[zz, n, 2]
                + (above[k] * terms_ref[zz, n, 3] - below[k] * terms_ref[zz, n, 4])
            )
            sums[TERM_FIELD[n]] = sums[TERM_FIELD[n]] + change
        for field in range(NF):
            out_ref[pl.ds(field * 32 + zz, TILE, stride=4), :] = sums[field]
        return carry

    lax.fori_loop(0, ROWS, row, 0)


def call(kernel, out_shapes, scratch=(), inputs=0):
    run = pl.pallas_call(
        kernel,
        out_shape=[pltpu.VMEM(shape, F32) for shape in out_shapes],
        in_specs=[VMEM] * inputs,
        out_specs=[VMEM] * len(out_shapes),
        scratch_shapes=[pltpu.VMEM(shape, F32) for shape in scratch],
        compiler_params=SMALL,
    )
    return lambda *args: run(*in_vmem(args))


def in_vmem(args):
    return [pltpu.with_memory_space_constraint(arg, pltpu.VMEM) for arg in args]


def body(constituent_mass, flow_speeds, thermal_pair, blowing_indicator):
    count_x = lax.axis_size("gx")
    count_z = lax.axis_size("gz")

    def swap(near):
        step = [1, -1] if near else [-1, 1]
        return lambda value: lax.ppermute(
            value, "gz", [(i, (i + step[i % 2]) % count_z) for i in range(count_z)]
        )

    def ring(step):
        return lambda value: lax.ppermute(
            value, "gx", [(i, (i + step) % count_x) for i in range(count_x)]
        )

    arrays = [
        value.reshape(-1, LANES) for value in (constituent_mass, flow_speeds, thermal_pair)
    ]
    packed = (PACK_ROWS, LANES)
    rows = (GROUPS * TILE, LANES)
    fields = (NF, TILE, LANES)
    own, far, near, blown = pl.pallas_call(
        pack_kernel,
        out_shape=[
            pltpu.VMEM(shape, F32)
            for shape in (
                rows, (MAIN_ROWS, LANES), (MAIN_ROWS, LANES), (4 * TILE, LANES),
            )
        ],
        in_specs=[pl.BlockSpec(memory_space=pltpu.HBM)] * 4,
        out_specs=[VMEM] * 4,
        scratch_shapes=[
            pltpu.VMEM((NF * 4 * TILE, LANES), F32),
            pltpu.VMEM(blowing_indicator.shape, jnp.int32),
            pltpu.SemaphoreType.DMA((4,)),
        ],
        compiler_params=SMALL,
    )(*[
        pltpu.with_memory_space_constraint(value, pltpu.HBM)
        for value in arrays + [blowing_indicator]
    ])
    far = swap(False)(far)
    near = swap(True)(near)
    face, part = call(stream_kernel, [rows, rows], inputs=2)(own, blown)
    corner, weights = call(own_corner_kernel, [fields, (LANES, LANES)], inputs=1)(own)
    far, near, face, part, corner = lax.optimization_barrier((far, near, face, part, corner))

    corner, to_right, to_left = call(
        corner_pack_kernel,
        [fields, packed, packed],
        inputs=3,
    )(corner, far, near)
    got_left = ring(1)(to_right)
    got_right = ring(-1)(to_left)
    sums, clamped, tiles, state, raw = call(
        model_kernel,
        [
            (3, TILE, LANES),
            fields,
            (GRID_ROWS, TILES, TILE, LANES),
            (STATE_ROWS, STATE_COUNT, TILE, LANES),
            (SPAN_TILES, NF, TILE, LANES),
        ],
        scratch=[(GRID_ROWS, 4, TILE, LANES), (GRID_ROWS, 8, TILE, LANES), (6, TILE, LANES)],
        inputs=4,
    )(own, far, near, corner)
    got_left, got_right, sums = lax.optimization_barrier((got_left, got_right, sums))
    totals, corner, corner_tiles, corner_speed = call(
        corner_kernel,
        [(4 * TILE, LANES), fields, (TILES, TILE, LANES), (3, TILE, LANES)],
        inputs=5,
    )(clamped, got_left, got_right, sums, weights)

    (terms,) = call(term_kernel, [(ROWS, TERMS, 5, TILE, LANES)], inputs=4)(
        tiles, state, corner_tiles, corner_speed
    )
    (part,) = call(ends_kernel, [rows], inputs=3)(corner, face, part)
    (base,) = call(
        span_kernel,
        [rows],
        scratch=[
            (SPAN_TILES, NF, TILE, LANES), (SPAN_TILES, NF, TILE, LANES), (SPAN_TILES, TILE, LANES),
        ],
        inputs=2,
    )(raw, part)

    def crossed(value, mask):
        return lax.ppermute(value, "gz", [(i, i ^ mask) for i in range(count_z)])

    totals = totals + crossed(totals, 1)
    reach = 2
    while count_z > 4 * reach:
        a, b, c = (crossed(totals, k * reach) for k in (1, 2, 3))
        totals = (totals + a) + (b + c)
        reach *= 4
    parts = [totals] + [
        crossed(totals, k * reach) if k * reach < count_z else jnp.zeros_like(totals)
        for k in (2, 3, 1)
    ]

    def final(*refs):
        final_kernel(*refs, parts=4)

    tendency, coefficients = pl.pallas_call(
        final,
        out_shape=[jax.ShapeDtypeStruct(shape, F32) for shape in ((NF * 32, LANES), (3, 4, LANES))],
        in_specs=[VMEM] * 6,
        out_specs=[VMEM] * 2,
        scratch_shapes=[pltpu.VMEM((TILE, LANES), F32)],
        compiler_params=SMALL,
    )(*in_vmem(parts + [base, terms]))
    return tendency.reshape(NF, 4, TILE, LANES), coefficients


def solution(mesh):
    placed = (
        P(None, None, "gz", "gx"),
        P(None, None, "gz", "gx"),
        P(None, None, "gz", "gx"),
        P("gz", "gx"),
    )
    return jax.shard_map(
        body,
        mesh=mesh,
        in_specs=placed,
        out_specs=(P(None, None, "gz", "gx"), P(None, None, "gx")),
        check_vma=False,
    )
```
